256 devices in a mesh: elev: 16 (over z, core), valley: 8 (over x_lo, y), down: 2 (over x_hi).
Axes of the slice: x: 4 (x_hi: 2, x_lo: 2; x = x_hi * 2 + x_lo), y: 4, z: 8, core: 2. Of those that a mesh axis runs over, the one named last changes fastest.
Arguments:
- resid: bfloat16 [16, 32, 4, 128, 256], P('elev', 'valley', 'down'), may hold values from -6 to 6
- direction: bfloat16 [16, 32, 4, 128, 256], P('elev', 'valley', 'down'), may hold values from -6 to 6
- diag_blocks: bfloat16 [16, 32, 4, 256, 256], P('elev', 'valley', 'down'), may hold values from -0.375 to 0.375
- lower_blocks: bfloat16 [16, 32, 4, 256, 256], P('elev', 'valley', 'down')
- upper_blocks: bfloat16 [16, 32, 4, 256, 256], P('elev', 'valley', 'down')
- inv_pivots: bfloat16 [16, 32, 4, 256, 256], P('elev', 'valley', 'down')
- down_coupling: bfloat16 [16, 32, 4, 256, 256], P('elev', 'valley', 'down'), may hold values from -0.375 to 0.375
- valley_coupling: bfloat16 [16, 32, 4, 256, 256], P('elev', 'valley', 'down'), may hold values from -0.375 to 0.375
- coupled_column: int32 [16, 32, 4], P('elev', 'valley', 'down'), may hold values from 0 to 31
Outputs:
- preconditioned: bfloat16 [16, 32, 4, 128, 256], P('elev', 'valley', 'down')
- image: float32 [16, 32, 4, 128, 256], P('elev', 'valley', 'down')
The draws below stay inside these ranges and needn't reach their ends.
All inputs are finite; a program needn't handle non-finite values.
Results may differ from the reference program's by a relative error of at most 0.015.
Values may be sent and summed in bfloat16 or wider, within the bound.
A program may use at most 64 MiB of HBM per device.

```python
import math
import jax
import jax.numpy as jnp

BS = 256
NR = 128
NLAY = 16
VBLK = 32
DBLK = 4


def decay_blocks(key):
    pick_key, slow_key, fast_key, noise_key = jax.random.split(key, 4)
    shape = (NLAY, VBLK, DBLK, BS)
    share = 0.5
    picked = jax.random.uniform(pick_key, shape, jnp.float32)
    slow = jax.random.uniform(slow_key, shape, jnp.float32, 0.86, 0.93)
    fast = jax.random.uniform(fast_key, shape, jnp.float32, 0.15, 0.6)
    rates = jnp.where(picked < share, slow, fast)
    noise = jax.random.normal(noise_key, shape + (BS,), jnp.float32) * (0.2 / math.sqrt(BS))
    return (-(rates[..., None] * jnp.eye(BS, dtype=jnp.float32) + noise)).astype(jnp.bfloat16)


def draw_lower_blocks(key, part):
    return decay_blocks(jax.random.fold_in(key, 11))


def draw_upper_blocks(key, part):
    return decay_blocks(jax.random.fold_in(key, 12))


def draw_inv_pivots(key, part):
    noise_key = jax.random.fold_in(key, 13)
    noise = jax.random.normal(noise_key, (NLAY, VBLK, DBLK, BS, BS), jnp.float32) * (0.2 / math.sqrt(BS))
    return (noise + jnp.eye(BS, dtype=jnp.float32)).astype(jnp.bfloat16)


def plant(array, key, smallest, high):
    longest = array.shape.index(max(array.shape))
    spots = []
    for shift in (0, 1):
        where = [jax.random.randint(jax.random.fold_in(key, axis), (), 0, length) for axis, length in enumerate(array.shape)]
        where[longest] = (where[longest] + shift) % array.shape[longest]
        spots.append(tuple(where))
    return array.at[spots[0]].set(smallest).at[spots[1]].set(high)


def shard_levels(stream_key, shape, cuts, low, high):
    def one(dim, shards_of):
        heights = jax.random.uniform(jax.random.fold_in(jax.random.fold_in(stream_key, 6), dim), (shards_of,), jnp.float32, low / len(cuts), high / len(cuts))
        return jnp.repeat(jnp.exp(heights), shape[dim] // shards_of).reshape((-1,) + (1,) * (len(shape) - dim - 1))

    level = one(*cuts[0])
    for cut in cuts[1:]:
        level = level * one(*cut)
    return level


def gaussian(rng, dims, width, most, pieces=(), held_as=jnp.bfloat16):
    values = width * jax.random.normal(rng, dims, jnp.float32)
    if pieces:
        values = values * shard_levels(rng, dims, pieces, -0.22, 0.18)
    return jnp.clip(values, -most, most).astype(held_as)


def setup_inputs(seed: int = 0) -> dict:
    streams_of = jax.random.split(jax.random.key(seed), 10)
    return {
        "resid": gaussian(streams_of[0], (NLAY, VBLK, DBLK, NR, BS), 1.0, 6.0, ((0, 16), (1, 8), (2, 2))),
        "direction": gaussian(streams_of[1], (NLAY, VBLK, DBLK, NR, BS), 1.0, 6.0, ((0, 16), (1, 8), (2, 2))),
        "diag_blocks": gaussian(streams_of[2], (NLAY, VBLK, DBLK, BS, BS), BS ** -0.5, 0.375, ((0, 16), (1, 8), (2, 2))),
        "lower_blocks": draw_lower_blocks(jax.random.fold_in(streams_of[9], 71), 0),
        "upper_blocks": draw_upper_blocks(jax.random.fold_in(streams_of[9], 71), 0),
        "inv_pivots": draw_inv_pivots(jax.random.fold_in(streams_of[9], 71), 0),
        "down_coupling": gaussian(streams_of[6], (NLAY, VBLK, DBLK, BS, BS), BS ** -0.5, 0.375, ((0, 16), (1, 8), (2, 2))),
        "valley_coupling": gaussian(streams_of[7], (NLAY, VBLK, DBLK, BS, BS), BS ** -0.5, 0.375, ((0, 16), (1, 8), (2, 2))),
        "coupled_column": plant(jax.random.randint(streams_of[8], (NLAY, VBLK, DBLK), 0, VBLK), jax.random.fold_in(streams_of[8], 1), 0, VBLK - 1).astype(jnp.int32),
    }


def product(vectors, blocks):
    return jnp.einsum('...rs,...st->...rt', vectors.astype(jnp.float32), blocks.astype(jnp.float32))


def reference(resid, direction, diag_blocks, lower_blocks, upper_blocks, inv_pivots, down_coupling, valley_coupling, coupled_column):
    layer_count = resid.shape[0]
    empty_front = jnp.zeros(resid.shape[1:], jnp.bfloat16)
    front = empty_front
    fronts = []
    for height in range(layer_count):
        inner = (resid[height].astype(jnp.float32) - product(front, lower_blocks[height])).astype(jnp.bfloat16)
        front = product(inner, inv_pivots[height]).astype(jnp.bfloat16)
        fronts.append(front)
    solved = [None] * layer_count
    above = empty_front
    for height in range(layer_count - 1, -1, -1):
        carried = product(above, upper_blocks[height]).astype(jnp.bfloat16)
        above = (fronts[height].astype(jnp.float32) - product(carried, inv_pivots[height])).astype(jnp.bfloat16)
        solved[height] = above
    preconditioned = jnp.stack(solved)
    down_index = jnp.arange(resid.shape[2], dtype=jnp.int32)[None, :]
    images = []
    for height in range(layer_count):
        current = direction[height]
        below_dir = direction[height - 1] if height > 0 else empty_front
        above_dir = direction[height + 1] if height + 1 < layer_count else empty_front
        upstream = jnp.concatenate([empty_front[:, :1], current[:, :-1]], axis=1)
        partner = current[coupled_column[height], down_index]
        total = product(current, diag_blocks[height])
        total = total + product(below_dir, lower_blocks[height])
        total = total + product(above_dir, upper_blocks[height])
        total = total + product(upstream, down_coupling[height])
        total = total + product(partner, valley_coupling[height])
        images.append(total)
    return preconditioned, jnp.stack(images)
```

```python
import functools

import jax
import jax.numpy as jnp
from jax import lax
from jax.experimental import pallas as pl
from jax.experimental.pallas import tpu as pltpu
from jax.sharding import PartitionSpec as P

MESH = pl.DeviceIdType.MESH
ROW_SPLIT = 2


def with_halo(block, sides, width):
    for axis, dim in sides:
        count = lax.axis_size(axis)
        forward = [(i, i + 1) for i in range(count - 1)]
        backward = [(target, source) for source, target in forward]
        low = lax.ppermute(
            lax.slice_in_dim(block, block.shape[dim] - width, None, axis=dim), axis, forward
        )
        high = lax.ppermute(lax.slice_in_dim(block, 0, width, axis=dim), axis, backward)
        block = jnp.concatenate([low, block, high], axis=dim)
    return block


def from_behind(value, axis, by):
    length = lax.axis_size(axis)
    pairs = [(i, i + by) for i in range(length) if 0 <= i + by < length]
    return lax.ppermute(value, axis, pairs)


def apply_blocks(vectors, blocks):
    return jnp.einsum("bqrs,bqst->bqrt", vectors, blocks, preferred_element_type=jnp.float32)


def sweep_kernel(
    resid_ref,
    lower_ref,
    upper_ref,
    pivot_ref,
    out_ref,
    fronts,
    fwd_buf,
    bwd_buf,
    fsend,
    frecv,
    bsend,
    brecv,
    *,
    n,
    per_block,
):
    f32 = jnp.float32
    bf16 = jnp.bfloat16
    h = lax.axis_index("elev")
    v = lax.axis_index("valley")
    d = lax.axis_index("down")
    chunks = resid_ref.shape[0]
    has_below = h > 0
    has_above = h < n - 1

    barrier = pltpu.get_barrier_semaphore()

    @pl.when(has_below)
    def _():
        pl.semaphore_signal(barrier, 1, device_id=(h - 1, v, d), device_id_type=MESH)

    @pl.when(has_above)
    def _():
        pl.semaphore_signal(barrier, 1, device_id=(h + 1, v, d), device_id_type=MESH)

    pl.semaphore_wait(barrier, has_below.astype(jnp.int32) + has_above.astype(jnp.int32))

    def fwd_copy(g):
        return pltpu.make_async_remote_copy(
            src_ref=fronts.at[g],
            dst_ref=fwd_buf.at[g],
            send_sem=fsend.at[g],
            recv_sem=frecv.at[g],
            device_id=(h + 1, v, d),
            device_id_type=MESH,
        )

    def bwd_copy(g):
        return pltpu.make_async_remote_copy(
            src_ref=out_ref.at[g],
            dst_ref=bwd_buf.at[g],
            send_sem=bsend.at[g],
            recv_sem=brecv.at[g],
            device_id=(h - 1, v, d),
            device_id_type=MESH,
        )

    def fwd_body(g, carry):
        blk = g // per_block

        @pl.when(has_below)
        def _():
            fwd_copy(g).wait_recv()
            inner = resid_ref[g].astype(f32) - jnp.dot(
                fwd_buf[g], lower_ref[blk], preferred_element_type=f32
            )
            fronts[g] = jnp.dot(
                inner.astype(bf16), pivot_ref[blk], preferred_element_type=f32
            ).astype(bf16)

        @pl.when(jnp.logical_not(has_below))
        def _():
            fronts[g] = jnp.dot(resid_ref[g], pivot_ref[blk], preferred_element_type=f32).astype(
                bf16
            )

        @pl.when(has_above)
        def _():
            fwd_copy(g).start()

        return carry

    lax.fori_loop(0, chunks, fwd_body, 0)

    def bwd_body(g, carry):
        blk = g // per_block

        @pl.when(has_above)
        def _():
            bwd_copy(g).wait_recv()
            carried = jnp.dot(bwd_buf[g], upper_ref[blk], preferred_element_type=f32).astype(bf16)
            out_ref[g] = (
                fronts[g].astype(f32) - jnp.dot(carried, pivot_ref[blk], preferred_element_type=f32)
            ).astype(bf16)

        @pl.when(jnp.logical_not(has_above))
        def _():
            out_ref[g] = fronts[g]

        @pl.when(has_below)
        def _():
            bwd_copy(g).start()

        return carry

    lax.fori_loop(0, chunks, bwd_body, 0)

    def drain(g, carry):
        @pl.when(has_above)
        def _():
            fwd_copy(g).wait_send()

        @pl.when(has_below)
        def _():
            bwd_copy(g).wait_send()

        return carry

    lax.fori_loop(0, chunks, drain, 0)


def sweep(resid_l, lower_l, upper_l, pivot_l):
    n = lax.axis_size("elev")
    chunks, rows, width = resid_l.shape
    per_block = chunks // lower_l.shape[0]
    vmem = pl.BlockSpec(memory_space=pltpu.VMEM)
    flops = 4 * chunks * rows * width * width
    weight_bytes = 3 * lower_l.size * lower_l.dtype.itemsize
    return pl.pallas_call(
        functools.partial(sweep_kernel, n=n, per_block=per_block),
        out_shape=jax.ShapeDtypeStruct(resid_l.shape, resid_l.dtype),
        in_specs=[vmem] * 4,
        out_specs=vmem,
        scratch_shapes=[
            pltpu.VMEM(resid_l.shape, resid_l.dtype),
            pltpu.VMEM(resid_l.shape, resid_l.dtype),
            pltpu.VMEM(resid_l.shape, resid_l.dtype),
            pltpu.SemaphoreType.DMA((chunks,)),
            pltpu.SemaphoreType.DMA((chunks,)),
            pltpu.SemaphoreType.DMA((chunks,)),
            pltpu.SemaphoreType.DMA((chunks,)),
        ],
        compiler_params=pltpu.CompilerParams(collective_id=0, has_side_effects=True),
        cost_estimate=pl.CostEstimate(
            flops=flops, bytes_accessed=weight_bytes + 2 * resid_l.size * 2, transcendentals=0
        ),
    )(resid_l, lower_l, upper_l, pivot_l)


def local(
    resid,
    direction,
    diag_blocks,
    lower_blocks,
    upper_blocks,
    inv_pivots,
    down_coupling,
    valley_coupling,
    coupled_column,
):
    lower_local = lower_blocks[0]
    upper_local = upper_blocks[0]
    pivot_local = inv_pivots[0]
    va, dc, nr, bs = resid.shape[1:]
    blocks = va * dc
    chunk_shape = (blocks * ROW_SPLIT, nr // ROW_SPLIT, bs)
    solved = sweep(
        resid[0].reshape(chunk_shape),
        lower_local.reshape(blocks, bs, bs),
        upper_local.reshape(blocks, bs, bs),
        pivot_local.reshape(blocks, bs, bs),
    ).reshape(resid.shape)

    current = direction[0]
    padded = with_halo(direction, (("elev", 0),), 1)
    below_dir = padded[0]
    above_dir = padded[2]
    rim_blocks = from_behind(current[:, -1:], "down", 1)
    upstream = jnp.concatenate([rim_blocks, current[:, :-1]], axis=1)
    partner_index = coupled_column[0]
    piece = lax.all_gather(current, "valley", axis=0, tiled=True)
    count = piece.shape[0]
    columns = jnp.arange(count, dtype=jnp.int32)
    picker = (partner_index[:, :, None] == columns[None, None, :]).astype(jnp.bfloat16)
    partner_sum = jnp.einsum("pqc,cqrs->pqrs", picker, piece, preferred_element_type=jnp.float32)
    partner = partner_sum.astype(jnp.bfloat16)
    total = apply_blocks(current, diag_blocks[0])
    total = total + apply_blocks(below_dir, lower_local)
    total = total + apply_blocks(above_dir, upper_local)
    total = total + apply_blocks(upstream, down_coupling[0])
    total = total + apply_blocks(partner, valley_coupling[0])
    return (solved, total[None])


def solution(mesh):
    spec = P("elev", "valley", "down", None, None)
    in_specs = (spec,) * 8 + (P("elev", "valley", "down"),)
    out_specs = (spec, spec)
    return jax.shard_map(local, mesh=mesh, in_specs=in_specs, out_specs=out_specs, check_vma=False)
```

```python
import functools

import jax
import jax.numpy as jnp
from jax import lax
from jax.experimental import pallas as pl
from jax.experimental.pallas import tpu as pltpu
from jax.sharding import PartitionSpec as P

MESH = pl.DeviceIdType.MESH
ROW_SPLIT = 2


def apply_blocks(vectors, blocks):
    return jnp.einsum("bqrs,bqst->bqrt", vectors, blocks, preferred_element_type=jnp.float32)


def sweep_kernel(
    resid_ref,
    dir_ref,
    diag_ref,
    lower_ref,
    upper_ref,
    pivot_ref,
    downc_ref,
    out_ref,
    img_ref,
    fronts,
    fwd_buf,
    bwd_buf,
    below_buf,
    above_buf,
    rim_buf,
    fsend,
    frecv,
    bsend,
    brecv,
    hsend,
    hrecv,
    rsend,
    rrecv,
    *,
    n,
    nd,
    dc,
    per_block,
):
    f32 = jnp.float32
    bf16 = jnp.bfloat16
    h = lax.axis_index("elev")
    v = lax.axis_index("valley")
    d = lax.axis_index("down")
    chunks = resid_ref.shape[0]
    blocks = dir_ref.shape[0]
    rims = rim_buf.shape[0]
    has_below = h > 0
    has_above = h < n - 1
    has_up = d > 0
    has_dn = d < nd - 1

    barrier = pltpu.get_barrier_semaphore()
    peers = [
        (has_below, (h - 1, v, d)),
        (has_above, (h + 1, v, d)),
        (has_up, (h, v, d - 1)),
        (has_dn, (h, v, d + 1)),
    ]
    count = 0
    for cond, peer in peers:
        count = count + cond.astype(jnp.int32)

        @pl.when(cond)
        def _():
            pl.semaphore_signal(barrier, 1, device_id=peer, device_id_type=MESH)

    pl.semaphore_wait(barrier, count)

    def fwd_copy(g):
        return pltpu.make_async_remote_copy(
            src_ref=fronts.at[g],
            dst_ref=fwd_buf.at[g],
            send_sem=fsend.at[g],
            recv_sem=frecv.at[g],
            device_id=(h + 1, v, d),
            device_id_type=MESH,
        )

    def bwd_copy(g, src):
        return pltpu.make_async_remote_copy(
            src_ref=src.at[g],
            dst_ref=bwd_buf.at[g],
            send_sem=bsend.at[g],
            recv_sem=brecv.at[g],
            device_id=(h - 1, v, d),
            device_id_type=MESH,
        )

    def halo_down():
        return pltpu.make_async_remote_copy(
            src_ref=dir_ref,
            dst_ref=above_buf,
            send_sem=hsend.at[0],
            recv_sem=hrecv.at[0],
            device_id=(h - 1, v, d),
            device_id_type=MESH,
        )

    def halo_up():
        return pltpu.make_async_remote_copy(
            src_ref=dir_ref,
            dst_ref=below_buf,
            send_sem=hsend.at[1],
            recv_sem=hrecv.at[1],
            device_id=(h + 1, v, d),
            device_id_type=MESH,
        )

    def rim_copy(a):
        return pltpu.make_async_remote_copy(
            src_ref=dir_ref.at[a * dc + dc - 1],
            dst_ref=rim_buf.at[a],
            send_sem=rsend.at[a],
            recv_sem=rrecv.at[a],
            device_id=(h, v, d + 1),
            device_id_type=MESH,
        )

    @pl.when(has_below)
    def _():
        halo_down().start()

    @pl.when(has_dn)
    def _():
        for a in range(rims):
            rim_copy(a).start()

    @pl.when(jnp.logical_not(has_below))
    def _():
        below_buf[...] = jnp.zeros(below_buf.shape, bf16)

    @pl.when(jnp.logical_not(has_above))
    def _():
        above_buf[...] = jnp.zeros(above_buf.shape, bf16)

    @pl.when(jnp.logical_not(has_up))
    def _():
        rim_buf[...] = jnp.zeros(rim_buf.shape, bf16)

    def fwd_body(g, carry):
        blk = g // per_block

        @pl.when(has_below)
        def _():
            fwd_copy(g).wait_recv()
            inner = resid_ref[g].astype(f32) - jnp.dot(
                fwd_buf[g], lower_ref[blk], preferred_element_type=f32
            )
            fronts[g] = jnp.dot(
                inner.astype(bf16), pivot_ref[blk], preferred_element_type=f32
            ).astype(bf16)

        @pl.when(jnp.logical_not(has_below))
        def _():
            fronts[g] = jnp.dot(resid_ref[g], pivot_ref[blk], preferred_element_type=f32).astype(
                bf16
            )

        @pl.when(has_above)
        def _():
            fwd_copy(g).start()

        @pl.when(jnp.logical_not(has_above))
        def _():
            out_ref[g] = fronts[g]

        @pl.when(jnp.logical_and(jnp.logical_not(has_above), has_below))
        def _():
            bwd_copy(g, fronts).start()

        return carry

    lax.fori_loop(0, chunks, fwd_body, 0)

    @pl.when(has_above)
    def _():
        halo_up().start()

    def image_body(b, carry):
        a = b // dc
        c = b % dc
        acc = jnp.dot(dir_ref[b], diag_ref[b], preferred_element_type=f32)
        acc = acc + jnp.dot(below_buf[b], lower_ref[b], preferred_element_type=f32)
        acc = acc + jnp.dot(above_buf[b], upper_ref[b], preferred_element_type=f32)
        upstream = jnp.where(c == 0, rim_buf[a], dir_ref[jnp.maximum(b - 1, 0)])
        img_ref[b] = acc + jnp.dot(upstream, downc_ref[b], preferred_element_type=f32)
        return carry

    def image():
        @pl.when(has_below)
        def _():
            halo_up().wait_recv()

        @pl.when(has_above)
        def _():
            halo_down().wait_recv()

        @pl.when(has_up)
        def _():
            for a in range(rims):
                rim_copy(a).wait_recv()

        lax.fori_loop(0, blocks, image_body, 0)

    early = h < n // 2

    @pl.when(early)
    def _():
        image()

    def bwd_body(g, carry):
        blk = g // per_block

        @pl.when(has_above)
        def _():
            bwd_copy(g, out_ref).wait_recv()
            carried = jnp.dot(bwd_buf[g], upper_ref[blk], preferred_element_type=f32).astype(bf16)
            out_ref[g] = (
                fronts[g].astype(f32) - jnp.dot(carried, pivot_ref[blk], preferred_element_type=f32)
            ).astype(bf16)

            @pl.when(has_below)
            def _():
                bwd_copy(g, out_ref).start()

        return carry

    lax.fori_loop(0, chunks, bwd_body, 0)

    @pl.when(jnp.logical_not(early))
    def _():
        image()

    def drain(g, carry):
        @pl.when(has_above)
        def _():
            fwd_copy(g).wait_send()

        @pl.when(has_below)
        def _():
            bwd_copy(g, out_ref).wait_send()

        return carry

    lax.fori_loop(0, chunks, drain, 0)

    @pl.when(has_below)
    def _():
        halo_down().wait_send()

    @pl.when(has_above)
    def _():
        halo_up().wait_send()

    @pl.when(has_dn)
    def _():
        for a in range(rims):
            rim_copy(a).wait_send()


def sweep(resid_l, dir_l, diag_l, lower_l, upper_l, pivot_l, downc_l, dc):
    n = lax.axis_size("elev")
    nd = lax.axis_size("down")
    chunks, rows, width = resid_l.shape
    blocks = lower_l.shape[0]
    per_block = chunks // blocks
    vmem = pl.BlockSpec(memory_space=pltpu.VMEM)
    flops = 2 * (2 * chunks * rows + 4 * dir_l.shape[0] * dir_l.shape[1]) * width * width
    weight_bytes = 6 * lower_l.size * lower_l.dtype.itemsize
    return pl.pallas_call(
        functools.partial(sweep_kernel, n=n, nd=nd, dc=dc, per_block=per_block),
        out_shape=(
            jax.ShapeDtypeStruct(resid_l.shape, resid_l.dtype),
            jax.ShapeDtypeStruct(dir_l.shape, jnp.float32),
        ),
        in_specs=[vmem] * 7,
        out_specs=(vmem, vmem),
        scratch_shapes=[
            pltpu.VMEM(resid_l.shape, resid_l.dtype),
            pltpu.VMEM(resid_l.shape, resid_l.dtype),
            pltpu.VMEM(resid_l.shape, resid_l.dtype),
            pltpu.VMEM(dir_l.shape, dir_l.dtype),
            pltpu.VMEM(dir_l.shape, dir_l.dtype),
            pltpu.VMEM((blocks // dc,) + dir_l.shape[1:], dir_l.dtype),
            pltpu.SemaphoreType.DMA((chunks,)),
            pltpu.SemaphoreType.DMA((chunks,)),
            pltpu.SemaphoreType.DMA((chunks,)),
            pltpu.SemaphoreType.DMA((chunks,)),
            pltpu.SemaphoreType.DMA((2,)),
            pltpu.SemaphoreType.DMA((2,)),
            pltpu.SemaphoreType.DMA((blocks // dc,)),
            pltpu.SemaphoreType.DMA((blocks // dc,)),
        ],
        compiler_params=pltpu.CompilerParams(collective_id=0, has_side_effects=True),
        cost_estimate=pl.CostEstimate(
            flops=flops, bytes_accessed=weight_bytes + 6 * resid_l.size * 2, transcendentals=0
        ),
    )(resid_l, dir_l, diag_l, lower_l, upper_l, pivot_l, downc_l)


def local(
    resid,
    direction,
    diag_blocks,
    lower_blocks,
    upper_blocks,
    inv_pivots,
    down_coupling,
    valley_coupling,
    coupled_column,
):
    va, dc, nr, bs = resid.shape[1:]
    blocks = va * dc
    chunk_shape = (blocks * ROW_SPLIT, nr // ROW_SPLIT, bs)
    flat = (blocks, bs, bs)
    solved, partial = sweep(
        resid[0].reshape(chunk_shape),
        direction[0].reshape(blocks, nr, bs),
        diag_blocks[0].reshape(flat),
        lower_blocks[0].reshape(flat),
        upper_blocks[0].reshape(flat),
        inv_pivots[0].reshape(flat),
        down_coupling[0].reshape(flat),
        dc,
    )

    current = direction[0]
    partner_index = coupled_column[0]
    piece = lax.all_gather(current, "valley", axis=0, tiled=True)
    count = piece.shape[0]
    columns = jnp.arange(count, dtype=jnp.int32)
    picker = (partner_index[:, :, None] == columns[None, None, :]).astype(jnp.bfloat16)
    partner_sum = jnp.einsum("pqc,cqrs->pqrs", picker, piece, preferred_element_type=jnp.float32)
    partner = partner_sum.astype(jnp.bfloat16)
    total = partial.reshape(current.shape) + apply_blocks(partner, valley_coupling[0])
    return (solved.reshape(resid.shape), total[None])


def solution(mesh):
    spec = P("elev", "valley", "down", None, None)
    in_specs = (spec,) * 8 + (P("elev", "valley", "down"),)
    out_specs = (spec, spec)
    return jax.shard_map(local, mesh=mesh, in_specs=in_specs, out_specs=out_specs, check_vma=False)
```

```python
import functools

import jax
import jax.numpy as jnp
from jax import lax
from jax.experimental import pallas as pl
from jax.experimental.pallas import tpu as pltpu
from jax.sharding import PartitionSpec as P

MESH = pl.DeviceIdType.MESH
ROW_SPLIT = 2


def sweep_kernel(
    resid_ref,
    dir_ref,
    diag_ref,
    lower_ref,
    upper_ref,
    pivot_ref,
    downc_ref,
    valc_ref,
    col_ref,
    out_ref,
    img_ref,
    fronts,
    fwd_buf,
    bwd_buf,
    below_buf,
    above_buf,
    rim_buf,
    gath,
    fsend,
    frecv,
    bsend,
    brecv,
    hsend,
    hrecv,
    rsend,
    rrecv,
    gsend,
    grecv,
    *,
    n,
    nv,
    nd,
    dc,
    per_block,
):
    f32 = jnp.float32
    bf16 = jnp.bfloat16
    h = lax.axis_index("elev")
    v = lax.axis_index("valley")
    d = lax.axis_index("down")
    chunks = resid_ref.shape[0]
    blocks = dir_ref.shape[0]
    rims = rim_buf.shape[0]
    va = blocks // dc
    has_below = h > 0
    has_above = h < n - 1
    has_up = d > 0
    has_dn = d < nd - 1

    barrier = pltpu.get_barrier_semaphore()
    peers = [
        (has_below, (h - 1, v, d)),
        (has_above, (h + 1, v, d)),
        (has_up, (h, v, d - 1)),
        (has_dn, (h, v, d + 1)),
    ] + [(v != p, (h, p, d)) for p in range(nv)]
    count = 0
    for cond, peer in peers:
        count = count + cond.astype(jnp.int32)

        @pl.when(cond)
        def _():
            pl.semaphore_signal(barrier, 1, device_id=peer, device_id_type=MESH)

    pl.semaphore_wait(barrier, count)

    def fwd_copy(g):
        return pltpu.make_async_remote_copy(
            src_ref=fronts.at[g],
            dst_ref=fwd_buf.at[g],
            send_sem=fsend.at[g],
            recv_sem=frecv.at[g],
            device_id=(h + 1, v, d),
            device_id_type=MESH,
        )

    def bwd_copy(g, src):
        return pltpu.make_async_remote_copy(
            src_ref=src.at[g],
            dst_ref=bwd_buf.at[g],
            send_sem=bsend.at[g],
            recv_sem=brecv.at[g],
            device_id=(h - 1, v, d),
            device_id_type=MESH,
        )

    def halo_down():
        return pltpu.make_async_remote_copy(
            src_ref=dir_ref,
            dst_ref=above_buf,
            send_sem=hsend.at[0],
            recv_sem=hrecv.at[0],
            device_id=(h - 1, v, d),
            device_id_type=MESH,
        )

    def halo_up():
        return pltpu.make_async_remote_copy(
            src_ref=dir_ref,
            dst_ref=below_buf,
            send_sem=hsend.at[1],
            recv_sem=hrecv.at[1],
            device_id=(h + 1, v, d),
            device_id_type=MESH,
        )

    def rim_copy(a):
        return pltpu.make_async_remote_copy(
            src_ref=dir_ref.at[a * dc + dc - 1],
            dst_ref=rim_buf.at[a],
            send_sem=rsend.at[a],
            recv_sem=rrecv.at[a],
            device_id=(h, v, d + 1),
            device_id_type=MESH,
        )

    def gather_copy(p):
        return pltpu.make_async_remote_copy(
            src_ref=dir_ref,
            dst_ref=gath.at[pl.ds(v * blocks, blocks)],
            send_sem=gsend.at[p],
            recv_sem=grecv.at[v],
            device_id=(h, p, d),
            device_id_type=MESH,
        )

    def gather_wait(p):
        return pltpu.make_async_remote_copy(
            src_ref=dir_ref,
            dst_ref=gath.at[pl.ds(p * blocks, blocks)],
            send_sem=gsend.at[p],
            recv_sem=grecv.at[p],
            device_id=(h, p, d),
            device_id_type=MESH,
        )

    for p in range(nv):

        @pl.when(v != p)
        def _():
            gather_copy(p).start()

    gath[pl.ds(v * blocks, blocks)] = dir_ref[...]

    @pl.when(has_below)
    def _():
        halo_down().start()

    @pl.when(has_dn)
    def _():
        for a in range(rims):
            rim_copy(a).start()

    @pl.when(jnp.logical_not(has_below))
    def _():
        below_buf[...] = jnp.zeros(below_buf.shape, bf16)

    @pl.when(jnp.logical_not(has_above))
    def _():
        above_buf[...] = jnp.zeros(above_buf.shape, bf16)

    @pl.when(jnp.logical_not(has_up))
    def _():
        rim_buf[...] = jnp.zeros(rim_buf.shape, bf16)

    def fwd_body(g, carry):
        blk = g // per_block

        @pl.when(has_below)
        def _():
            fwd_copy(g).wait_recv()
            inner = resid_ref[g].astype(f32) - jnp.dot(
                fwd_buf[g], lower_ref[blk], preferred_element_type=f32
            )
            fronts[g] = jnp.dot(
                inner.astype(bf16), pivot_ref[blk], preferred_element_type=f32
            ).astype(bf16)

        @pl.when(jnp.logical_not(has_below))
        def _():
            fronts[g] = jnp.dot(resid_ref[g], pivot_ref[blk], preferred_element_type=f32).astype(
                bf16
            )

        @pl.when(has_above)
        def _():
            fwd_copy(g).start()

        @pl.when(jnp.logical_not(has_above))
        def _():
            out_ref[g] = fronts[g]

        @pl.when(jnp.logical_and(jnp.logical_not(has_above), has_below))
        def _():
            bwd_copy(g, fronts).start()

        return carry

    lax.fori_loop(0, chunks, fwd_body, 0)

    @pl.when(has_above)
    def _():
        halo_up().start()

    def image_body(b, carry):
        a = b // dc
        c = b % dc
        acc = jnp.dot(dir_ref[b], diag_ref[b], preferred_element_type=f32)
        acc = acc + jnp.dot(below_buf[b], lower_ref[b], preferred_element_type=f32)
        acc = acc + jnp.dot(above_buf[b], upper_ref[b], preferred_element_type=f32)
        upstream = jnp.where(c == 0, rim_buf[a], dir_ref[jnp.maximum(b - 1, 0)])
        acc = acc + jnp.dot(upstream, downc_ref[b], preferred_element_type=f32)
        col = col_ref[b]
        partner = gath[(col // va) * blocks + (col % va) * dc + c]
        img_ref[b] = acc + jnp.dot(partner, valc_ref[b], preferred_element_type=f32)
        return carry

    def image():
        @pl.when(has_below)
        def _():
            halo_up().wait_recv()

        @pl.when(has_above)
        def _():
            halo_down().wait_recv()

        @pl.when(has_up)
        def _():
            for a in range(rims):
                rim_copy(a).wait_recv()

        for p in range(nv):

            @pl.when(v != p)
            def _():
                gather_wait(p).wait_recv()

        lax.fori_loop(0, blocks, image_body, 0)

    early = h < n // 2

    @pl.when(early)
    def _():
        image()

    def bwd_body(g, carry):
        blk = g // per_block

        @pl.when(has_above)
        def _():
            bwd_copy(g, out_ref).wait_recv()
            carried = jnp.dot(bwd_buf[g], upper_ref[blk], preferred_element_type=f32).astype(bf16)
            out_ref[g] = (
                fronts[g].astype(f32) - jnp.dot(carried, pivot_ref[blk], preferred_element_type=f32)
            ).astype(bf16)

            @pl.when(has_below)
            def _():
                bwd_copy(g, out_ref).start()

        return carry

    lax.fori_loop(0, chunks, bwd_body, 0)

    @pl.when(jnp.logical_not(early))
    def _():
        image()

    def drain(g, carry):
        @pl.when(has_above)
        def _():
            fwd_copy(g).wait_send()

        @pl.when(has_below)
        def _():
            bwd_copy(g, out_ref).wait_send()

        return carry

    lax.fori_loop(0, chunks, drain, 0)

    @pl.when(has_below)
    def _():
        halo_down().wait_send()

    @pl.when(has_above)
    def _():
        halo_up().wait_send()

    @pl.when(has_dn)
    def _():
        for a in range(rims):
            rim_copy(a).wait_send()

    for p in range(nv):

        @pl.when(v != p)
        def _():
            gather_copy(p).wait_send()


def sweep(resid_l, dir_l, diag_l, lower_l, upper_l, pivot_l, downc_l, valc_l, col_l, dc):
    n = lax.axis_size("elev")
    nv = lax.axis_size("valley")
    nd = lax.axis_size("down")
    chunks, rows, width = resid_l.shape
    blocks = lower_l.shape[0]
    per_block = chunks // blocks
    vmem = pl.BlockSpec(memory_space=pltpu.VMEM)
    flops = 2 * (2 * chunks * rows + 5 * dir_l.shape[0] * dir_l.shape[1]) * width * width
    weight_bytes = 7 * lower_l.size * lower_l.dtype.itemsize
    return pl.pallas_call(
        functools.partial(sweep_kernel, n=n, nv=nv, nd=nd, dc=dc, per_block=per_block),
        out_shape=(
            jax.ShapeDtypeStruct(resid_l.shape, resid_l.dtype),
            jax.ShapeDtypeStruct(dir_l.shape, jnp.float32),
        ),
        in_specs=[vmem] * 8 + [pl.BlockSpec(memory_space=pltpu.SMEM)],
        out_specs=(vmem, vmem),
        scratch_shapes=[
            pltpu.VMEM(resid_l.shape, resid_l.dtype),
            pltpu.VMEM(resid_l.shape, resid_l.dtype),
            pltpu.VMEM(resid_l.shape, resid_l.dtype),
            pltpu.VMEM(dir_l.shape, dir_l.dtype),
            pltpu.VMEM(dir_l.shape, dir_l.dtype),
            pltpu.VMEM((blocks // dc,) + dir_l.shape[1:], dir_l.dtype),
            pltpu.VMEM((nv * blocks,) + dir_l.shape[1:], dir_l.dtype),
            pltpu.SemaphoreType.DMA((chunks,)),
            pltpu.SemaphoreType.DMA((chunks,)),
            pltpu.SemaphoreType.DMA((chunks,)),
            pltpu.SemaphoreType.DMA((chunks,)),
            pltpu.SemaphoreType.DMA((2,)),
            pltpu.SemaphoreType.DMA((2,)),
            pltpu.SemaphoreType.DMA((blocks // dc,)),
            pltpu.SemaphoreType.DMA((blocks // dc,)),
            pltpu.SemaphoreType.DMA((nv,)),
            pltpu.SemaphoreType.DMA((nv,)),
        ],
        compiler_params=pltpu.CompilerParams(collective_id=0, has_side_effects=True),
        cost_estimate=pl.CostEstimate(
            flops=flops, bytes_accessed=weight_bytes + 6 * resid_l.size * 2, transcendentals=0
        ),
    )(resid_l, dir_l, diag_l, lower_l, upper_l, pivot_l, downc_l, valc_l, col_l)


def local(
    resid,
    direction,
    diag_blocks,
    lower_blocks,
    upper_blocks,
    inv_pivots,
    down_coupling,
    valley_coupling,
    coupled_column,
):
    va, dc, nr, bs = resid.shape[1:]
    blocks = va * dc
    chunk_shape = (blocks * ROW_SPLIT, nr // ROW_SPLIT, bs)
    flat = (blocks, bs, bs)
    solved, image = sweep(
        resid[0].reshape(chunk_shape),
        direction[0].reshape(blocks, nr, bs),
        diag_blocks[0].reshape(flat),
        lower_blocks[0].reshape(flat),
        upper_blocks[0].reshape(flat),
        inv_pivots[0].reshape(flat),
        down_coupling[0].reshape(flat),
        valley_coupling[0].reshape(flat),
        coupled_column[0].reshape(blocks),
        dc,
    )
    return (solved.reshape(resid.shape), image.reshape(resid.shape))


def solution(mesh):
    spec = P("elev", "valley", "down", None, None)
    in_specs = (spec,) * 8 + (P("elev", "valley", "down"),)
    out_specs = (spec, spec)
    return jax.shard_map(local, mesh=mesh, in_specs=in_specs, out_specs=out_specs, check_vma=False)
```

```python
import functools

import jax
import jax.numpy as jnp
from jax import lax
from jax.experimental import pallas as pl
from jax.experimental.pallas import tpu as pltpu
from jax.sharding import PartitionSpec as P

MESH = pl.DeviceIdType.MESH
ROW_SPLIT = 2


def sweep_kernel(
    resid_ref,
    dir_ref,
    diag_ref,
    lower_ref,
    upper_ref,
    pivot_ref,
    downc_ref,
    valc_ref,
    col_ref,
    out_ref,
    img_ref,
    fronts,
    fwd_buf,
    bwd_buf,
    below_buf,
    above_buf,
    rim_buf,
    gath,
    fsend,
    frecv,
    bsend,
    brecv,
    hsend,
    hrecv,
    rsend,
    rrecv,
    gsend,
    grecv,
    *,
    n,
    nv,
    nd,
    dc,
    per_block,
):
    f32 = jnp.float32
    bf16 = jnp.bfloat16
    h = lax.axis_index("elev")
    v = lax.axis_index("valley")
    d = lax.axis_index("down")
    chunks = resid_ref.shape[0]
    blocks = dir_ref.shape[0]
    rims = rim_buf.shape[0]
    va = blocks // dc
    has_below = h > 0
    has_above = h < n - 1
    has_up = d > 0
    has_dn = d < nd - 1

    barrier = pltpu.get_barrier_semaphore()
    peers = [
        (has_below, (h - 1, v, d)),
        (has_above, (h + 1, v, d)),
        (has_up, (h, v, d - 1)),
        (has_dn, (h, v, d + 1)),
    ] + [(v != p, (h, p, d)) for p in range(nv)]
    count = 0
    for cond, peer in peers:
        count = count + cond.astype(jnp.int32)

        @pl.when(cond)
        def _():
            pl.semaphore_signal(barrier, 1, device_id=peer, device_id_type=MESH)

    pl.semaphore_wait(barrier, count)

    def fwd_copy(g):
        return pltpu.make_async_remote_copy(
            src_ref=fronts.at[g],
            dst_ref=fwd_buf.at[g],
            send_sem=fsend.at[g],
            recv_sem=frecv.at[g],
            device_id=(h + 1, v, d),
            device_id_type=MESH,
        )

    def bwd_copy(g, src):
        return pltpu.make_async_remote_copy(
            src_ref=src.at[g],
            dst_ref=bwd_buf.at[g],
            send_sem=bsend.at[g],
            recv_sem=brecv.at[g],
            device_id=(h - 1, v, d),
            device_id_type=MESH,
        )

    def halo_down():
        return pltpu.make_async_remote_copy(
            src_ref=dir_ref,
            dst_ref=above_buf,
            send_sem=hsend.at[0],
            recv_sem=hrecv.at[0],
            device_id=(h - 1, v, d),
            device_id_type=MESH,
        )

    def halo_up():
        return pltpu.make_async_remote_copy(
            src_ref=dir_ref,
            dst_ref=below_buf,
            send_sem=hsend.at[1],
            recv_sem=hrecv.at[1],
            device_id=(h + 1, v, d),
            device_id_type=MESH,
        )

    def rim_copy(a):
        return pltpu.make_async_remote_copy(
            src_ref=dir_ref.at[a * dc + dc - 1],
            dst_ref=rim_buf.at[a],
            send_sem=rsend.at[a],
            recv_sem=rrecv.at[a],
            device_id=(h, v, d + 1),
            device_id_type=MESH,
        )

    def gather_copy(p):
        return pltpu.make_async_remote_copy(
            src_ref=dir_ref,
            dst_ref=gath.at[pl.ds(v * blocks, blocks)],
            send_sem=gsend.at[p],
            recv_sem=grecv.at[v],
            device_id=(h, p, d),
            device_id_type=MESH,
        )

    def gather_wait(p):
        return pltpu.make_async_remote_copy(
            src_ref=dir_ref,
            dst_ref=gath.at[pl.ds(p * blocks, blocks)],
            send_sem=gsend.at[p],
            recv_sem=grecv.at[p],
            device_id=(h, p, d),
            device_id_type=MESH,
        )

    for p in range(nv):

        @pl.when(v != p)
        def _():
            gather_copy(p).start()

    gath[pl.ds(v * blocks, blocks)] = dir_ref[...]

    @pl.when(has_below)
    def _():
        halo_down().start()

    @pl.when(has_dn)
    def _():
        for a in range(rims):
            rim_copy(a).start()

    @pl.when(jnp.logical_not(has_below))
    def _():
        below_buf[...] = jnp.zeros(below_buf.shape, bf16)

    @pl.when(jnp.logical_not(has_above))
    def _():
        above_buf[...] = jnp.zeros(above_buf.shape, bf16)

    @pl.when(jnp.logical_not(has_up))
    def _():
        rim_buf[...] = jnp.zeros(rim_buf.shape, bf16)

    def fwd_body(g, carry):
        blk = g // per_block

        @pl.when(has_below)
        def _():
            fwd_copy(g).wait_recv()
            inner = resid_ref[g].astype(f32) - jnp.dot(
                fwd_buf[g], lower_ref[blk], preferred_element_type=f32
            )
            fronts[g] = jnp.dot(
                inner.astype(bf16), pivot_ref[blk], preferred_element_type=f32
            ).astype(bf16)

        @pl.when(jnp.logical_not(has_below))
        def _():
            fronts[g] = jnp.dot(resid_ref[g], pivot_ref[blk], preferred_element_type=f32).astype(
                bf16
            )

        @pl.when(has_above)
        def _():
            fwd_copy(g).start()

        @pl.when(jnp.logical_not(has_above))
        def _():
            out_ref[g] = fronts[g]

        @pl.when(jnp.logical_and(jnp.logical_not(has_above), has_below))
        def _():
            bwd_copy(g, fronts).start()

        return carry

    lax.fori_loop(0, chunks, fwd_body, 0)

    @pl.when(has_above)
    def _():
        halo_up().start()

    def image_body(b, carry):
        a = b // dc
        c = b % dc
        acc = jnp.dot(dir_ref[b], diag_ref[b], preferred_element_type=f32)
        acc = acc + jnp.dot(below_buf[b], lower_ref[b], preferred_element_type=f32)
        acc = acc + jnp.dot(above_buf[b], upper_ref[b], preferred_element_type=f32)
        upstream = jnp.where(c == 0, rim_buf[a], dir_ref[jnp.maximum(b - 1, 0)])
        img_ref[b] = acc + jnp.dot(upstream, downc_ref[b], preferred_element_type=f32)
        return carry

    def partner_body(b, carry):
        c = b % dc
        col = col_ref[b]
        partner = gath[(col // va) * blocks + (col % va) * dc + c]
        img_ref[b] = img_ref[b] + jnp.dot(partner, valc_ref[b], preferred_element_type=f32)
        return carry

    def image():
        @pl.when(has_below)
        def _():
            halo_up().wait_recv()

        @pl.when(has_above)
        def _():
            halo_down().wait_recv()

        @pl.when(has_up)
        def _():
            for a in range(rims):
                rim_copy(a).wait_recv()

        lax.fori_loop(0, blocks, image_body, 0)

    early = h < n // 2

    @pl.when(early)
    def _():
        image()

    def bwd_body(g, carry):
        blk = g // per_block

        @pl.when(has_above)
        def _():
            bwd_copy(g, out_ref).wait_recv()
            carried = jnp.dot(bwd_buf[g], upper_ref[blk], preferred_element_type=f32).astype(bf16)
            out_ref[g] = (
                fronts[g].astype(f32) - jnp.dot(carried, pivot_ref[blk], preferred_element_type=f32)
            ).astype(bf16)

            @pl.when(has_below)
            def _():
                bwd_copy(g, out_ref).start()

        return carry

    lax.fori_loop(0, chunks, bwd_body, 0)

    @pl.when(jnp.logical_not(early))
    def _():
        image()

    for p in range(nv):

        @pl.when(v != p)
        def _():
            gather_wait(p).wait_recv()

    lax.fori_loop(0, blocks, partner_body, 0)

    def drain(g, carry):
        @pl.when(has_above)
        def _():
            fwd_copy(g).wait_send()

        @pl.when(has_below)
        def _():
            bwd_copy(g, out_ref).wait_send()

        return carry

    lax.fori_loop(0, chunks, drain, 0)

    @pl.when(has_below)
    def _():
        halo_down().wait_send()

    @pl.when(has_above)
    def _():
        halo_up().wait_send()

    @pl.when(has_dn)
    def _():
        for a in range(rims):
            rim_copy(a).wait_send()

    for p in range(nv):

        @pl.when(v != p)
        def _():
            gather_copy(p).wait_send()


def sweep(resid_l, dir_l, diag_l, lower_l, upper_l, pivot_l, downc_l, valc_l, col_l, dc):
    n = lax.axis_size("elev")
    nv = lax.axis_size("valley")
    nd = lax.axis_size("down")
    chunks, rows, width = resid_l.shape
    blocks = lower_l.shape[0]
    per_block = chunks // blocks
    vmem = pl.BlockSpec(memory_space=pltpu.VMEM)
    flops = 2 * (2 * chunks * rows + 5 * dir_l.shape[0] * dir_l.shape[1]) * width * width
    weight_bytes = 7 * lower_l.size * lower_l.dtype.itemsize
    return pl.pallas_call(
        functools.partial(sweep_kernel, n=n, nv=nv, nd=nd, dc=dc, per_block=per_block),
        out_shape=(
            jax.ShapeDtypeStruct(resid_l.shape, resid_l.dtype),
            jax.ShapeDtypeStruct(dir_l.shape, jnp.float32),
        ),
        in_specs=[vmem] * 8 + [pl.BlockSpec(memory_space=pltpu.SMEM)],
        out_specs=(vmem, vmem),
        scratch_shapes=[
            pltpu.VMEM(resid_l.shape, resid_l.dtype),
            pltpu.VMEM(resid_l.shape, resid_l.dtype),
            pltpu.VMEM(resid_l.shape, resid_l.dtype),
            pltpu.VMEM(dir_l.shape, dir_l.dtype),
            pltpu.VMEM(dir_l.shape, dir_l.dtype),
            pltpu.VMEM((blocks // dc,) + dir_l.shape[1:], dir_l.dtype),
            pltpu.VMEM((nv * blocks,) + dir_l.shape[1:], dir_l.dtype),
            pltpu.SemaphoreType.DMA((chunks,)),
            pltpu.SemaphoreType.DMA((chunks,)),
            pltpu.SemaphoreType.DMA((chunks,)),
            pltpu.SemaphoreType.DMA((chunks,)),
            pltpu.SemaphoreType.DMA((2,)),
            pltpu.SemaphoreType.DMA((2,)),
            pltpu.SemaphoreType.DMA((blocks // dc,)),
            pltpu.SemaphoreType.DMA((blocks // dc,)),
            pltpu.SemaphoreType.DMA((nv,)),
            pltpu.SemaphoreType.DMA((nv,)),
        ],
        compiler_params=pltpu.CompilerParams(collective_id=0, has_side_effects=True),
        cost_estimate=pl.CostEstimate(
            flops=flops, bytes_accessed=weight_bytes + 6 * resid_l.size * 2, transcendentals=0
        ),
    )(resid_l, dir_l, diag_l, lower_l, upper_l, pivot_l, downc_l, valc_l, col_l)


def local(
    resid,
    direction,
    diag_blocks,
    lower_blocks,
    upper_blocks,
    inv_pivots,
    down_coupling,
    valley_coupling,
    coupled_column,
):
    va, dc, nr, bs = resid.shape[1:]
    blocks = va * dc
    chunk_shape = (blocks * ROW_SPLIT, nr // ROW_SPLIT, bs)
    flat = (blocks, bs, bs)
    solved, image = sweep(
        resid[0].reshape(chunk_shape),
        direction[0].reshape(blocks, nr, bs),
        diag_blocks[0].reshape(flat),
        lower_blocks[0].reshape(flat),
        upper_blocks[0].reshape(flat),
        inv_pivots[0].reshape(flat),
        down_coupling[0].reshape(flat),
        valley_coupling[0].reshape(flat),
        coupled_column[0].reshape(blocks),
        dc,
    )
    return (solved.reshape(resid.shape), image.reshape(resid.shape))


def solution(mesh):
    spec = P("elev", "valley", "down", None, None)
    in_specs = (spec,) * 8 + (P("elev", "valley", "down"),)
    out_specs = (spec, spec)
    return jax.shard_map(local, mesh=mesh, in_specs=in_specs, out_specs=out_specs, check_vma=False)
```

```python
import functools

import jax
import jax.numpy as jnp
from jax import lax
from jax.experimental import pallas as pl
from jax.experimental.pallas import tpu as pltpu
from jax.sharding import PartitionSpec as P

MESH = pl.DeviceIdType.MESH
ROW_SPLIT = 4


def apply_blocks(vectors, blocks):
    return jnp.einsum("bqrs,bqst->bqrt", vectors, blocks, preferred_element_type=jnp.float32)


def sweep_kernel(
    resid_ref,
    dir_ref,
    diag_ref,
    lower_ref,
    upper_ref,
    pivot_ref,
    downc_ref,
    out_ref,
    img_ref,
    fronts,
    fwd_buf,
    bwd_buf,
    below_buf,
    above_buf,
    rim_buf,
    fsend,
    frecv,
    bsend,
    brecv,
    hsend,
    hrecv,
    rsend,
    rrecv,
    *,
    n,
    nd,
    dc,
    per_block,
):
    f32 = jnp.float32
    bf16 = jnp.bfloat16
    h = lax.axis_index("elev")
    v = lax.axis_index("valley")
    d = lax.axis_index("down")
    chunks = resid_ref.shape[0]
    blocks = dir_ref.shape[0]
    rims = rim_buf.shape[0]
    has_below = h > 0
    has_above = h < n - 1
    has_up = d > 0
    has_dn = d < nd - 1

    barrier = pltpu.get_barrier_semaphore()
    peers = [
        (has_below, (h - 1, v, d)),
        (has_above, (h + 1, v, d)),
        (has_up, (h, v, d - 1)),
        (has_dn, (h, v, d + 1)),
    ]
    count = 0
    for cond, peer in peers:
        count = count + cond.astype(jnp.int32)

        @pl.when(cond)
        def _():
            pl.semaphore_signal(barrier, 1, device_id=peer, device_id_type=MESH)

    pl.semaphore_wait(barrier, count)

    def fwd_copy(g):
        return pltpu.make_async_remote_copy(
            src_ref=fronts.at[g],
            dst_ref=fwd_buf.at[g],
            send_sem=fsend.at[g],
            recv_sem=frecv.at[g],
            device_id=(h + 1, v, d),
            device_id_type=MESH,
        )

    def bwd_copy(g, src):
        return pltpu.make_async_remote_copy(
            src_ref=src.at[g],
            dst_ref=bwd_buf.at[g],
            send_sem=bsend.at[g],
            recv_sem=brecv.at[g],
            device_id=(h - 1, v, d),
            device_id_type=MESH,
        )

    def halo_down():
        return pltpu.make_async_remote_copy(
            src_ref=dir_ref,
            dst_ref=above_buf,
            send_sem=hsend.at[0],
            recv_sem=hrecv.at[0],
            device_id=(h - 1, v, d),
            device_id_type=MESH,
        )

    def halo_up():
        return pltpu.make_async_remote_copy(
            src_ref=dir_ref,
            dst_ref=below_buf,
            send_sem=hsend.at[1],
            recv_sem=hrecv.at[1],
            device_id=(h + 1, v, d),
            device_id_type=MESH,
        )

    def rim_copy(a):
        return pltpu.make_async_remote_copy(
            src_ref=dir_ref.at[a * dc + dc - 1],
            dst_ref=rim_buf.at[a],
            send_sem=rsend.at[a],
            recv_sem=rrecv.at[a],
            device_id=(h, v, d + 1),
            device_id_type=MESH,
        )

    @pl.when(has_below)
    def _():
        halo_down().start()

    @pl.when(has_dn)
    def _():
        for a in range(rims):
            rim_copy(a).start()

    @pl.when(jnp.logical_not(has_below))
    def _():
        below_buf[...] = jnp.zeros(below_buf.shape, bf16)

    @pl.when(jnp.logical_not(has_above))
    def _():
        above_buf[...] = jnp.zeros(above_buf.shape, bf16)

    @pl.when(jnp.logical_not(has_up))
    def _():
        rim_buf[...] = jnp.zeros(rim_buf.shape, bf16)

    def fwd_body(g, carry):
        blk = g // per_block

        @pl.when(has_below)
        def _():
            fwd_copy(g).wait_recv()
            inner = resid_ref[g].astype(f32) - jnp.dot(
                fwd_buf[g], lower_ref[blk], preferred_element_type=f32
            )
            fronts[g] = jnp.dot(
                inner.astype(bf16), pivot_ref[blk], preferred_element_type=f32
            ).astype(bf16)

        @pl.when(jnp.logical_not(has_below))
        def _():
            fronts[g] = jnp.dot(resid_ref[g], pivot_ref[blk], preferred_element_type=f32).astype(
                bf16
            )

        @pl.when(has_above)
        def _():
            fwd_copy(g).start()

        @pl.when(jnp.logical_not(has_above))
        def _():
            out_ref[g] = fronts[g]

        @pl.when(jnp.logical_and(jnp.logical_not(has_above), has_below))
        def _():
            bwd_copy(g, fronts).start()

        return carry

    lax.fori_loop(0, chunks, fwd_body, 0)

    @pl.when(has_above)
    def _():
        halo_up().start()

    def image_body(b, carry):
        a = b // dc
        c = b % dc
        acc = jnp.dot(dir_ref[b], diag_ref[b], preferred_element_type=f32)
        acc = acc + jnp.dot(below_buf[b], lower_ref[b], preferred_element_type=f32)
        acc = acc + jnp.dot(above_buf[b], upper_ref[b], preferred_element_type=f32)
        upstream = jnp.where(c == 0, rim_buf[a], dir_ref[jnp.maximum(b - 1, 0)])
        img_ref[b] = acc + jnp.dot(upstream, downc_ref[b], preferred_element_type=f32)
        return carry

    def image():
        @pl.when(has_below)
        def _():
            halo_up().wait_recv()

        @pl.when(has_above)
        def _():
            halo_down().wait_recv()

        @pl.when(has_up)
        def _():
            for a in range(rims):
                rim_copy(a).wait_recv()

        lax.fori_loop(0, blocks, image_body, 0)

    early = h < n // 2

    @pl.when(early)
    def _():
        image()

    def bwd_body(g, carry):
        blk = g // per_block

        @pl.when(has_above)
        def _():
            bwd_copy(g, out_ref).wait_recv()
            carried = jnp.dot(bwd_buf[g], upper_ref[blk], preferred_element_type=f32).astype(bf16)
            out_ref[g] = (
                fronts[g].astype(f32) - jnp.dot(carried, pivot_ref[blk], preferred_element_type=f32)
            ).astype(bf16)

            @pl.when(has_below)
            def _():
                bwd_copy(g, out_ref).start()

        return carry

    lax.fori_loop(0, chunks, bwd_body, 0)

    @pl.when(jnp.logical_not(early))
    def _():
        image()

    def drain(g, carry):
        @pl.when(has_above)
        def _():
            fwd_copy(g).wait_send()

        @pl.when(has_below)
        def _():
            bwd_copy(g, out_ref).wait_send()

        return carry

    lax.fori_loop(0, chunks, drain, 0)

    @pl.when(has_below)
    def _():
        halo_down().wait_send()

    @pl.when(has_above)
    def _():
        halo_up().wait_send()

    @pl.when(has_dn)
    def _():
        for a in range(rims):
            rim_copy(a).wait_send()


def sweep(resid_l, dir_l, diag_l, lower_l, upper_l, pivot_l, downc_l, dc):
    n = lax.axis_size("elev")
    nd = lax.axis_size("down")
    chunks, rows, width = resid_l.shape
    blocks = lower_l.shape[0]
    per_block = chunks // blocks
    vmem = pl.BlockSpec(memory_space=pltpu.VMEM)
    flops = 2 * (2 * chunks * rows + 4 * dir_l.shape[0] * dir_l.shape[1]) * width * width
    weight_bytes = 6 * lower_l.size * lower_l.dtype.itemsize
    return pl.pallas_call(
        functools.partial(sweep_kernel, n=n, nd=nd, dc=dc, per_block=per_block),
        out_shape=(
            jax.ShapeDtypeStruct(resid_l.shape, resid_l.dtype),
            jax.ShapeDtypeStruct(dir_l.shape, jnp.float32),
        ),
        in_specs=[vmem] * 7,
        out_specs=(vmem, vmem),
        scratch_shapes=[
            pltpu.VMEM(resid_l.shape, resid_l.dtype),
            pltpu.VMEM(resid_l.shape, resid_l.dtype),
            pltpu.VMEM(resid_l.shape, resid_l.dtype),
            pltpu.VMEM(dir_l.shape, dir_l.dtype),
            pltpu.VMEM(dir_l.shape, dir_l.dtype),
            pltpu.VMEM((blocks // dc,) + dir_l.shape[1:], dir_l.dtype),
            pltpu.SemaphoreType.DMA((chunks,)),
            pltpu.SemaphoreType.DMA((chunks,)),
            pltpu.SemaphoreType.DMA((chunks,)),
            pltpu.SemaphoreType.DMA((chunks,)),
            pltpu.SemaphoreType.DMA((2,)),
            pltpu.SemaphoreType.DMA((2,)),
            pltpu.SemaphoreType.DMA((blocks // dc,)),
            pltpu.SemaphoreType.DMA((blocks // dc,)),
        ],
        compiler_params=pltpu.CompilerParams(collective_id=0, has_side_effects=True),
        cost_estimate=pl.CostEstimate(
            flops=flops, bytes_accessed=weight_bytes + 6 * resid_l.size * 2, transcendentals=0
        ),
    )(resid_l, dir_l, diag_l, lower_l, upper_l, pivot_l, downc_l)


def local(
    resid,
    direction,
    diag_blocks,
    lower_blocks,
    upper_blocks,
    inv_pivots,
    down_coupling,
    valley_coupling,
    coupled_column,
):
    va, dc, nr, bs = resid.shape[1:]
    blocks = va * dc
    chunk_shape = (blocks * ROW_SPLIT, nr // ROW_SPLIT, bs)
    flat = (blocks, bs, bs)
    solved, partial = sweep(
        resid[0].reshape(chunk_shape),
        direction[0].reshape(blocks, nr, bs),
        diag_blocks[0].reshape(flat),
        lower_blocks[0].reshape(flat),
        upper_blocks[0].reshape(flat),
        inv_pivots[0].reshape(flat),
        down_coupling[0].reshape(flat),
        dc,
    )

    current = direction[0]
    partner_index = coupled_column[0]
    piece = lax.all_gather(current, "valley", axis=0, tiled=True)
    rows = partner_index * dc + jnp.arange(dc, dtype=jnp.int32)[None, :]
    partner = jnp.take(
        piece.reshape((-1,) + piece.shape[2:]), rows.reshape(-1), axis=0, mode="clip"
    ).reshape(current.shape)
    total = partial.reshape(current.shape) + apply_blocks(partner, valley_coupling[0])
    return (solved.reshape(resid.shape), total[None])


def solution(mesh):
    spec = P("elev", "valley", "down", None, None)
    in_specs = (spec,) * 8 + (P("elev", "valley", "down"),)
    out_specs = (spec, spec)
    return jax.shard_map(local, mesh=mesh, in_specs=in_specs, out_specs=out_specs, check_vma=False)
```

```python
import functools

import jax
import jax.numpy as jnp
from jax import lax
from jax.experimental import pallas as pl
from jax.experimental.pallas import tpu as pltpu
from jax.sharding import PartitionSpec as P

MESH = pl.DeviceIdType.MESH
ROW_SPLIT = 2


def apply_blocks(vectors, blocks):
    return jnp.einsum("bqrs,bqst->bqrt", vectors, blocks, preferred_element_type=jnp.float32)


def sweep_kernel(
    resid_ref,
    dir_ref,
    diag_ref,
    lower_ref,
    upper_ref,
    pivot_ref,
    downc_ref,
    out_ref,
    img_ref,
    fronts,
    fwd_buf,
    bwd_buf,
    below_buf,
    above_buf,
    rim_buf,
    fsend,
    frecv,
    bsend,
    brecv,
    hsend,
    hrecv,
    rsend,
    rrecv,
    *,
    n,
    nd,
    dc,
    per_block,
):
    f32 = jnp.float32
    bf16 = jnp.bfloat16
    h = lax.axis_index("elev")
    v = lax.axis_index("valley")
    d = lax.axis_index("down")
    chunks = resid_ref.shape[0]
    blocks = dir_ref.shape[0]
    rims = rim_buf.shape[0]
    has_below = h > 0
    has_above = h < n - 1
    has_up = d > 0
    has_dn = d < nd - 1

    barrier = pltpu.get_barrier_semaphore()
    peers = [
        (has_below, (h - 1, v, d)),
        (has_above, (h + 1, v, d)),
        (has_up, (h, v, d - 1)),
        (has_dn, (h, v, d + 1)),
    ]
    count = 0
    for cond, peer in peers:
        count = count + cond.astype(jnp.int32)

        @pl.when(cond)
        def _():
            pl.semaphore_signal(barrier, 1, device_id=peer, device_id_type=MESH)

    pl.semaphore_wait(barrier, count)

    def fwd_copy(g):
        return pltpu.make_async_remote_copy(
            src_ref=fronts.at[g],
            dst_ref=fwd_buf.at[g],
            send_sem=fsend.at[g],
            recv_sem=frecv.at[g],
            device_id=(h + 1, v, d),
            device_id_type=MESH,
        )

    def bwd_copy(g, src):
        return pltpu.make_async_remote_copy(
            src_ref=src.at[g],
            dst_ref=bwd_buf.at[g],
            send_sem=bsend.at[g],
            recv_sem=brecv.at[g],
            device_id=(h - 1, v, d),
            device_id_type=MESH,
        )

    def halo_down():
        return pltpu.make_async_remote_copy(
            src_ref=dir_ref,
            dst_ref=above_buf,
            send_sem=hsend.at[0],
            recv_sem=hrecv.at[0],
            device_id=(h - 1, v, d),
            device_id_type=MESH,
        )

    def halo_up():
        return pltpu.make_async_remote_copy(
            src_ref=dir_ref,
            dst_ref=below_buf,
            send_sem=hsend.at[1],
            recv_sem=hrecv.at[1],
            device_id=(h + 1, v, d),
            device_id_type=MESH,
        )

    def rim_copy(a):
        return pltpu.make_async_remote_copy(
            src_ref=dir_ref.at[a * dc + dc - 1],
            dst_ref=rim_buf.at[a],
            send_sem=rsend.at[a],
            recv_sem=rrecv.at[a],
            device_id=(h, v, d + 1),
            device_id_type=MESH,
        )

    @pl.when(has_below)
    def _():
        halo_down().start()

    @pl.when(has_dn)
    def _():
        for a in range(rims):
            rim_copy(a).start()

    @pl.when(jnp.logical_not(has_below))
    def _():
        below_buf[...] = jnp.zeros(below_buf.shape, bf16)

    @pl.when(jnp.logical_not(has_above))
    def _():
        above_buf[...] = jnp.zeros(above_buf.shape, bf16)

    @pl.when(jnp.logical_not(has_up))
    def _():
        rim_buf[...] = jnp.zeros(rim_buf.shape, bf16)

    def fwd_body(g, carry):
        blk = g // per_block

        @pl.when(has_below)
        def _():
            fwd_copy(g).wait_recv()
            inner = resid_ref[g].astype(f32) - jnp.dot(
                fwd_buf[g], lower_ref[blk], preferred_element_type=f32
            )
            fronts[g] = jnp.dot(
                inner.astype(bf16), pivot_ref[blk], preferred_element_type=f32
            ).astype(bf16)

        @pl.when(jnp.logical_not(has_below))
        def _():
            fronts[g] = jnp.dot(resid_ref[g], pivot_ref[blk], preferred_element_type=f32).astype(
                bf16
            )

        @pl.when(has_above)
        def _():
            fwd_copy(g).start()

        @pl.when(jnp.logical_not(has_above))
        def _():
            out_ref[g] = fronts[g]

        @pl.when(jnp.logical_and(jnp.logical_not(has_above), has_below))
        def _():
            bwd_copy(g, fronts).start()

        return carry

    lax.fori_loop(0, chunks, fwd_body, 0)

    @pl.when(has_above)
    def _():
        halo_up().start()

    def image_body(b, carry):
        a = b // dc
        c = b % dc
        acc = jnp.dot(dir_ref[b], diag_ref[b], preferred_element_type=f32)
        acc = acc + jnp.dot(below_buf[b], lower_ref[b], preferred_element_type=f32)
        acc = acc + jnp.dot(above_buf[b], upper_ref[b], preferred_element_type=f32)
        upstream = jnp.where(c == 0, rim_buf[a], dir_ref[jnp.maximum(b - 1, 0)])
        img_ref[b] = acc + jnp.dot(upstream, downc_ref[b], preferred_element_type=f32)
        return carry

    def image():
        @pl.when(has_below)
        def _():
            halo_up().wait_recv()

        @pl.when(has_above)
        def _():
            halo_down().wait_recv()

        @pl.when(has_up)
        def _():
            for a in range(rims):
                rim_copy(a).wait_recv()

        lax.fori_loop(0, blocks, image_body, 0)

    early = h < n // 2

    @pl.when(early)
    def _():
        image()

    def bwd_body(g, carry):
        blk = g // per_block

        @pl.when(has_above)
        def _():
            bwd_copy(g, out_ref).wait_recv()
            carried = jnp.dot(bwd_buf[g], upper_ref[blk], preferred_element_type=f32).astype(bf16)
            out_ref[g] = (
                fronts[g].astype(f32) - jnp.dot(carried, pivot_ref[blk], preferred_element_type=f32)
            ).astype(bf16)

            @pl.when(has_below)
            def _():
                bwd_copy(g, out_ref).start()

        return carry

    lax.fori_loop(0, chunks, bwd_body, 0)

    @pl.when(jnp.logical_not(early))
    def _():
        image()

    def drain(g, carry):
        @pl.when(has_above)
        def _():
            fwd_copy(g).wait_send()

        @pl.when(has_below)
        def _():
            bwd_copy(g, out_ref).wait_send()

        return carry

    lax.fori_loop(0, chunks, drain, 0)

    @pl.when(has_below)
    def _():
        halo_down().wait_send()

    @pl.when(has_above)
    def _():
        halo_up().wait_send()

    @pl.when(has_dn)
    def _():
        for a in range(rims):
            rim_copy(a).wait_send()


def sweep(resid_l, dir_l, diag_l, lower_l, upper_l, pivot_l, downc_l, dc):
    n = lax.axis_size("elev")
    nd = lax.axis_size("down")
    chunks, rows, width = resid_l.shape
    blocks = lower_l.shape[0]
    per_block = chunks // blocks
    vmem = pl.BlockSpec(memory_space=pltpu.VMEM)
    flops = 2 * (2 * chunks * rows + 4 * dir_l.shape[0] * dir_l.shape[1]) * width * width
    weight_bytes = 6 * lower_l.size * lower_l.dtype.itemsize
    return pl.pallas_call(
        functools.partial(sweep_kernel, n=n, nd=nd, dc=dc, per_block=per_block),
        out_shape=(
            jax.ShapeDtypeStruct(resid_l.shape, resid_l.dtype),
            jax.ShapeDtypeStruct(dir_l.shape, jnp.float32),
        ),
        in_specs=[vmem] * 7,
        out_specs=(vmem, vmem),
        scratch_shapes=[
            pltpu.VMEM(resid_l.shape, resid_l.dtype),
            pltpu.VMEM(resid_l.shape, resid_l.dtype),
            pltpu.VMEM(resid_l.shape, resid_l.dtype),
            pltpu.VMEM(dir_l.shape, dir_l.dtype),
            pltpu.VMEM(dir_l.shape, dir_l.dtype),
            pltpu.VMEM((blocks // dc,) + dir_l.shape[1:], dir_l.dtype),
            pltpu.SemaphoreType.DMA((chunks,)),
            pltpu.SemaphoreType.DMA((chunks,)),
            pltpu.SemaphoreType.DMA((chunks,)),
            pltpu.SemaphoreType.DMA((chunks,)),
            pltpu.SemaphoreType.DMA((2,)),
            pltpu.SemaphoreType.DMA((2,)),
            pltpu.SemaphoreType.DMA((blocks // dc,)),
            pltpu.SemaphoreType.DMA((blocks // dc,)),
        ],
        compiler_params=pltpu.CompilerParams(collective_id=0, has_side_effects=True),
        cost_estimate=pl.CostEstimate(
            flops=flops, bytes_accessed=weight_bytes + 6 * resid_l.size * 2, transcendentals=0
        ),
    )(resid_l, dir_l, diag_l, lower_l, upper_l, pivot_l, downc_l)


def partner_kernel(col_ref, piece_ref, valc_ref, partial_ref, out_ref):
    out_ref[...] = partial_ref[...] + jnp.dot(
        piece_ref[0], valc_ref[0], preferred_element_type=jnp.float32
    )[None]


def add_partner(cols, piece, valc, partial, dc):
    blocks, rows, width = partial.shape
    spec = pl.BlockSpec((1, rows, width), lambda b, col: (b, 0, 0))
    return pl.pallas_call(
        partner_kernel,
        out_shape=jax.ShapeDtypeStruct(partial.shape, partial.dtype),
        grid_spec=pltpu.PrefetchScalarGridSpec(
            num_scalar_prefetch=1,
            grid=(blocks,),
            in_specs=[
                pl.BlockSpec((1, rows, width), lambda b, col: (col[b] * dc + b % dc, 0, 0)),
                pl.BlockSpec((1, width, width), lambda b, col: (b, 0, 0)),
                spec,
            ],
            out_specs=spec,
        ),
        cost_estimate=pl.CostEstimate(
            flops=2 * blocks * rows * width * width,
            bytes_accessed=blocks * (rows * width * 10 + width * width * 2),
            transcendentals=0,
        ),
    )(cols, piece, valc, partial)


def local(
    resid,
    direction,
    diag_blocks,
    lower_blocks,
    upper_blocks,
    inv_pivots,
    down_coupling,
    valley_coupling,
    coupled_column,
):
    va, dc, nr, bs = resid.shape[1:]
    blocks = va * dc
    chunk_shape = (blocks * ROW_SPLIT, nr // ROW_SPLIT, bs)
    flat = (blocks, bs, bs)
    solved, partial = sweep(
        resid[0].reshape(chunk_shape),
        direction[0].reshape(blocks, nr, bs),
        diag_blocks[0].reshape(flat),
        lower_blocks[0].reshape(flat),
        upper_blocks[0].reshape(flat),
        inv_pivots[0].reshape(flat),
        down_coupling[0].reshape(flat),
        dc,
    )

    current = direction[0]
    piece = lax.all_gather(current, "valley", axis=0, tiled=True)
    image = add_partner(
        coupled_column[0].reshape(blocks),
        piece.reshape((-1, nr, bs)),
        valley_coupling[0].reshape(flat),
        partial,
        dc,
    )
    return (solved.reshape(resid.shape), image.reshape(resid.shape))


def solution(mesh):
    spec = P("elev", "valley", "down", None, None)
    in_specs = (spec,) * 8 + (P("elev", "valley", "down"),)
    out_specs = (spec, spec)
    return jax.shard_map(local, mesh=mesh, in_specs=in_specs, out_specs=out_specs, check_vma=False)
```

```python
import functools

import jax
import jax.numpy as jnp
from jax import lax
from jax.experimental import pallas as pl
from jax.experimental.pallas import tpu as pltpu
from jax.sharding import PartitionSpec as P

MESH = pl.DeviceIdType.MESH
ROW_SPLIT = 2


def apply_blocks(vectors, blocks):
    return jnp.einsum("bqrs,bqst->bqrt", vectors, blocks, preferred_element_type=jnp.float32)


def sweep_kernel(
    resid_ref,
    dir_ref,
    diag_ref,
    lower_ref,
    upper_ref,
    pivot_ref,
    downc_ref,
    out_ref,
    img_ref,
    fronts,
    fwd_buf,
    bwd_buf,
    below_buf,
    above_buf,
    rim_buf,
    fsend,
    frecv,
    bsend,
    brecv,
    hsend,
    hrecv,
    rsend,
    rrecv,
    *,
    n,
    nd,
    dc,
    per_block,
):
    f32 = jnp.float32
    bf16 = jnp.bfloat16
    h = lax.axis_index("elev")
    v = lax.axis_index("valley")
    d = lax.axis_index("down")
    chunks = resid_ref.shape[0]
    blocks = dir_ref.shape[0]
    rims = rim_buf.shape[0]
    has_below = h > 0
    has_above = h < n - 1
    has_up = d > 0
    has_dn = d < nd - 1

    barrier = pltpu.get_barrier_semaphore()
    peers = [
        (has_below, (h - 1, v, d)),
        (has_above, (h + 1, v, d)),
        (has_up, (h, v, d - 1)),
        (has_dn, (h, v, d + 1)),
    ]
    count = 0
    for cond, peer in peers:
        count = count + cond.astype(jnp.int32)

        @pl.when(cond)
        def _():
            pl.semaphore_signal(barrier, 1, device_id=peer, device_id_type=MESH)

    pl.semaphore_wait(barrier, count)

    def fwd_copy(g):
        return pltpu.make_async_remote_copy(
            src_ref=fronts.at[g],
            dst_ref=fwd_buf.at[g],
            send_sem=fsend.at[g],
            recv_sem=frecv.at[g],
            device_id=(h + 1, v, d),
            device_id_type=MESH,
        )

    def bwd_copy(g, src):
        return pltpu.make_async_remote_copy(
            src_ref=src.at[g],
            dst_ref=bwd_buf.at[g],
            send_sem=bsend.at[g],
            recv_sem=brecv.at[g],
            device_id=(h - 1, v, d),
            device_id_type=MESH,
        )

    def halo_down():
        return pltpu.make_async_remote_copy(
            src_ref=dir_ref,
            dst_ref=above_buf,
            send_sem=hsend.at[0],
            recv_sem=hrecv.at[0],
            device_id=(h - 1, v, d),
            device_id_type=MESH,
        )

    def halo_up():
        return pltpu.make_async_remote_copy(
            src_ref=dir_ref,
            dst_ref=below_buf,
            send_sem=hsend.at[1],
            recv_sem=hrecv.at[1],
            device_id=(h + 1, v, d),
            device_id_type=MESH,
        )

    def rim_copy(a):
        return pltpu.make_async_remote_copy(
            src_ref=dir_ref.at[a * dc + dc - 1],
            dst_ref=rim_buf.at[a],
            send_sem=rsend.at[a],
            recv_sem=rrecv.at[a],
            device_id=(h, v, d + 1),
            device_id_type=MESH,
        )

    @pl.when(has_below)
    def _():
        halo_down().start()

    @pl.when(has_dn)
    def _():
        for a in range(rims):
            rim_copy(a).start()

    @pl.when(jnp.logical_not(has_below))
    def _():
        below_buf[...] = jnp.zeros(below_buf.shape, bf16)

    @pl.when(jnp.logical_not(has_above))
    def _():
        above_buf[...] = jnp.zeros(above_buf.shape, bf16)

    @pl.when(jnp.logical_not(has_up))
    def _():
        rim_buf[...] = jnp.zeros(rim_buf.shape, bf16)

    def fwd_body(g, carry):
        blk = g // per_block

        @pl.when(has_below)
        def _():
            fwd_copy(g).wait_recv()
            inner = resid_ref[g].astype(f32) - jnp.dot(
                fwd_buf[g], lower_ref[blk], preferred_element_type=f32
            )
            fronts[g] = jnp.dot(
                inner.astype(bf16), pivot_ref[blk], preferred_element_type=f32
            ).astype(bf16)

        @pl.when(jnp.logical_not(has_below))
        def _():
            fronts[g] = jnp.dot(resid_ref[g], pivot_ref[blk], preferred_element_type=f32).astype(
                bf16
            )

        @pl.when(has_above)
        def _():
            fwd_copy(g).start()

        @pl.when(jnp.logical_not(has_above))
        def _():
            out_ref[g] = fronts[g]

        @pl.when(jnp.logical_and(jnp.logical_not(has_above), has_below))
        def _():
            bwd_copy(g, fronts).start()

        return carry

    lax.fori_loop(0, chunks, fwd_body, 0)

    @pl.when(has_above)
    def _():
        halo_up().start()

    def image_body(b, carry):
        a = b // dc
        c = b % dc
        acc = jnp.dot(dir_ref[b], diag_ref[b], preferred_element_type=f32)
        acc = acc + jnp.dot(below_buf[b], lower_ref[b], preferred_element_type=f32)
        acc = acc + jnp.dot(above_buf[b], upper_ref[b], preferred_element_type=f32)
        upstream = jnp.where(c == 0, rim_buf[a], dir_ref[jnp.maximum(b - 1, 0)])
        img_ref[b] = acc + jnp.dot(upstream, downc_ref[b], preferred_element_type=f32)
        return carry

    def image():
        @pl.when(has_below)
        def _():
            halo_up().wait_recv()

        @pl.when(has_above)
        def _():
            halo_down().wait_recv()

        @pl.when(has_up)
        def _():
            for a in range(rims):
                rim_copy(a).wait_recv()

        lax.fori_loop(0, blocks, image_body, 0)

    early = h < n // 2

    @pl.when(early)
    def _():
        image()

    def bwd_body(g, carry):
        blk = g // per_block

        @pl.when(has_above)
        def _():
            bwd_copy(g, out_ref).wait_recv()
            carried = jnp.dot(bwd_buf[g], upper_ref[blk], preferred_element_type=f32).astype(bf16)
            out_ref[g] = (
                fronts[g].astype(f32) - jnp.dot(carried, pivot_ref[blk], preferred_element_type=f32)
            ).astype(bf16)

            @pl.when(has_below)
            def _():
                bwd_copy(g, out_ref).start()

        return carry

    lax.fori_loop(0, chunks, bwd_body, 0)

    @pl.when(jnp.logical_not(early))
    def _():
        image()

    def drain(g, carry):
        @pl.when(has_above)
        def _():
            fwd_copy(g).wait_send()

        @pl.when(has_below)
        def _():
            bwd_copy(g, out_ref).wait_send()

        return carry

    lax.fori_loop(0, chunks, drain, 0)

    @pl.when(has_below)
    def _():
        halo_down().wait_send()

    @pl.when(has_above)
    def _():
        halo_up().wait_send()

    @pl.when(has_dn)
    def _():
        for a in range(rims):
            rim_copy(a).wait_send()


def sweep(resid_l, dir_l, diag_l, lower_l, upper_l, pivot_l, downc_l, dc):
    n = lax.axis_size("elev")
    nd = lax.axis_size("down")
    chunks, rows, width = resid_l.shape
    blocks = lower_l.shape[0]
    per_block = chunks // blocks
    vmem = pl.BlockSpec(memory_space=pltpu.VMEM)
    flops = 2 * (2 * chunks * rows + 4 * dir_l.shape[0] * dir_l.shape[1]) * width * width
    weight_bytes = 6 * lower_l.size * lower_l.dtype.itemsize
    return pl.pallas_call(
        functools.partial(sweep_kernel, n=n, nd=nd, dc=dc, per_block=per_block),
        out_shape=(
            jax.ShapeDtypeStruct(resid_l.shape, resid_l.dtype),
            jax.ShapeDtypeStruct(dir_l.shape, jnp.float32),
        ),
        in_specs=[vmem] * 7,
        out_specs=(vmem, vmem),
        scratch_shapes=[
            pltpu.VMEM(resid_l.shape, resid_l.dtype),
            pltpu.VMEM(resid_l.shape, resid_l.dtype),
            pltpu.VMEM(resid_l.shape, resid_l.dtype),
            pltpu.VMEM(dir_l.shape, dir_l.dtype),
            pltpu.VMEM(dir_l.shape, dir_l.dtype),
            pltpu.VMEM((blocks // dc,) + dir_l.shape[1:], dir_l.dtype),
            pltpu.SemaphoreType.DMA((chunks,)),
            pltpu.SemaphoreType.DMA((chunks,)),
            pltpu.SemaphoreType.DMA((chunks,)),
            pltpu.SemaphoreType.DMA((chunks,)),
            pltpu.SemaphoreType.DMA((2,)),
            pltpu.SemaphoreType.DMA((2,)),
            pltpu.SemaphoreType.DMA((blocks // dc,)),
            pltpu.SemaphoreType.DMA((blocks // dc,)),
        ],
        compiler_params=pltpu.CompilerParams(collective_id=0, has_side_effects=True),
        cost_estimate=pl.CostEstimate(
            flops=flops, bytes_accessed=weight_bytes + 6 * resid_l.size * 2, transcendentals=0
        ),
    )(resid_l, dir_l, diag_l, lower_l, upper_l, pivot_l, downc_l)


def partner_kernel(col_ref, piece_ref, valc_ref, partial_ref, out_ref, held, sems, *, dc):
    blocks = held.shape[0]
    copies = []
    for b in range(blocks):
        col = col_ref[0, b // dc, b % dc]
        copy = pltpu.make_async_copy(piece_ref.at[col * dc + b % dc], held.at[b], sems.at[b])
        copy.start()
        copies.append(copy)
    for b in range(blocks):
        copies[b].wait()
        out_ref[b] = partial_ref[b] + jnp.dot(
            held[b], valc_ref[b], preferred_element_type=jnp.float32
        )


def add_partner(cols, piece, valc, partial, dc):
    blocks, rows, width = partial.shape
    vmem = pl.BlockSpec(memory_space=pltpu.VMEM)
    return pl.pallas_call(
        functools.partial(partner_kernel, dc=dc),
        out_shape=jax.ShapeDtypeStruct(partial.shape, partial.dtype),
        in_specs=[
            pl.BlockSpec(memory_space=pltpu.SMEM),
            pl.BlockSpec(memory_space=pl.ANY),
            vmem,
            vmem,
        ],
        out_specs=vmem,
        scratch_shapes=[
            pltpu.VMEM((blocks, rows, width), piece.dtype),
            pltpu.SemaphoreType.DMA((blocks,)),
        ],
        cost_estimate=pl.CostEstimate(
            flops=2 * blocks * rows * width * width,
            bytes_accessed=blocks * (rows * width * 10 + width * width * 2),
            transcendentals=0,
        ),
    )(cols, piece, valc, partial)


def local(
    resid,
    direction,
    diag_blocks,
    lower_blocks,
    upper_blocks,
    inv_pivots,
    down_coupling,
    valley_coupling,
    coupled_column,
):
    va, dc, nr, bs = resid.shape[1:]
    blocks = va * dc
    chunk_shape = (blocks * ROW_SPLIT, nr // ROW_SPLIT, bs)
    flat = (blocks, bs, bs)
    solved, partial = sweep(
        resid[0].reshape(chunk_shape),
        direction[0].reshape(blocks, nr, bs),
        diag_blocks[0].reshape(flat),
        lower_blocks[0].reshape(flat),
        upper_blocks[0].reshape(flat),
        inv_pivots[0].reshape(flat),
        down_coupling[0].reshape(flat),
        dc,
    )

    current = direction[0]
    piece = lax.all_gather(current, "valley", axis=0, tiled=True)
    image = add_partner(
        coupled_column,
        piece.reshape((-1, nr, bs)),
        valley_coupling[0].reshape(flat),
        partial,
        dc,
    )
    return (solved.reshape(resid.shape), image.reshape(resid.shape))


def solution(mesh):
    spec = P("elev", "valley", "down", None, None)
    in_specs = (spec,) * 8 + (P("elev", "valley", "down"),)
    out_specs = (spec, spec)
    return jax.shard_map(local, mesh=mesh, in_specs=in_specs, out_specs=out_specs, check_vma=False)
```

```python
import functools

import jax
import jax.numpy as jnp
from jax import lax
from jax.experimental import pallas as pl
from jax.experimental.pallas import tpu as pltpu
from jax.sharding import PartitionSpec as P

MESH = pl.DeviceIdType.MESH
ROW_SPLIT = 2


def apply_blocks(vectors, blocks):
    return jnp.einsum("bqrs,bqst->bqrt", vectors, blocks, preferred_element_type=jnp.float32)


def sweep_kernel(
    resid_ref,
    dir_ref,
    diag_ref,
    lower_ref,
    upper_ref,
    pivot_ref,
    downc_ref,
    out_ref,
    img_ref,
    gath,
    fronts,
    fwd_buf,
    bwd_buf,
    below_buf,
    above_buf,
    rim_buf,
    fsend,
    frecv,
    bsend,
    brecv,
    hsend,
    hrecv,
    rsend,
    rrecv,
    gsend,
    grecv,
    own_sem,
    *,
    n,
    nv,
    nd,
    dc,
    per_block,
):
    f32 = jnp.float32
    bf16 = jnp.bfloat16
    h = lax.axis_index("elev")
    v = lax.axis_index("valley")
    d = lax.axis_index("down")
    chunks = resid_ref.shape[0]
    blocks = dir_ref.shape[0]
    rims = rim_buf.shape[0]
    has_below = h > 0
    has_above = h < n - 1
    has_up = d > 0
    has_dn = d < nd - 1

    barrier = pltpu.get_barrier_semaphore()
    peers = [
        (has_below, (h - 1, v, d)),
        (has_above, (h + 1, v, d)),
        (has_up, (h, v, d - 1)),
        (has_dn, (h, v, d + 1)),
    ] + [(v != p, (h, p, d)) for p in range(nv)]
    count = 0
    for cond, peer in peers:
        count = count + cond.astype(jnp.int32)

        @pl.when(cond)
        def _():
            pl.semaphore_signal(barrier, 1, device_id=peer, device_id_type=MESH)

    pl.semaphore_wait(barrier, count)

    def fwd_copy(g):
        return pltpu.make_async_remote_copy(
            src_ref=fronts.at[g],
            dst_ref=fwd_buf.at[g],
            send_sem=fsend.at[g],
            recv_sem=frecv.at[g],
            device_id=(h + 1, v, d),
            device_id_type=MESH,
        )

    def bwd_copy(g, src):
        return pltpu.make_async_remote_copy(
            src_ref=src.at[g],
            dst_ref=bwd_buf.at[g],
            send_sem=bsend.at[g],
            recv_sem=brecv.at[g],
            device_id=(h - 1, v, d),
            device_id_type=MESH,
        )

    def halo_down():
        return pltpu.make_async_remote_copy(
            src_ref=dir_ref,
            dst_ref=above_buf,
            send_sem=hsend.at[0],
            recv_sem=hrecv.at[0],
            device_id=(h - 1, v, d),
            device_id_type=MESH,
        )

    def halo_up():
        return pltpu.make_async_remote_copy(
            src_ref=dir_ref,
            dst_ref=below_buf,
            send_sem=hsend.at[1],
            recv_sem=hrecv.at[1],
            device_id=(h + 1, v, d),
            device_id_type=MESH,
        )

    def rim_copy(a):
        return pltpu.make_async_remote_copy(
            src_ref=dir_ref.at[a * dc + dc - 1],
            dst_ref=rim_buf.at[a],
            send_sem=rsend.at[a],
            recv_sem=rrecv.at[a],
            device_id=(h, v, d + 1),
            device_id_type=MESH,
        )

    def gather_copy(p, slot):
        return pltpu.make_async_remote_copy(
            src_ref=dir_ref,
            dst_ref=gath.at[pl.ds(slot * blocks, blocks)],
            send_sem=gsend.at[p],
            recv_sem=grecv.at[slot],
            device_id=(h, p, d),
            device_id_type=MESH,
        )

    for p in range(nv):

        @pl.when(v != p)
        def _():
            gather_copy(p, v).start()

    own_copy = pltpu.make_async_copy(dir_ref, gath.at[pl.ds(v * blocks, blocks)], own_sem.at[0])
    own_copy.start()

    @pl.when(has_below)
    def _():
        halo_down().start()

    @pl.when(has_dn)
    def _():
        for a in range(rims):
            rim_copy(a).start()

    @pl.when(jnp.logical_not(has_below))
    def _():
        below_buf[...] = jnp.zeros(below_buf.shape, bf16)

    @pl.when(jnp.logical_not(has_above))
    def _():
        above_buf[...] = jnp.zeros(above_buf.shape, bf16)

    @pl.when(jnp.logical_not(has_up))
    def _():
        rim_buf[...] = jnp.zeros(rim_buf.shape, bf16)

    def fwd_body(g, carry):
        blk = g // per_block

        @pl.when(has_below)
        def _():
            fwd_copy(g).wait_recv()
            inner = resid_ref[g].astype(f32) - jnp.dot(
                fwd_buf[g], lower_ref[blk], preferred_element_type=f32
            )
            fronts[g] = jnp.dot(
                inner.astype(bf16), pivot_ref[blk], preferred_element_type=f32
            ).astype(bf16)

        @pl.when(jnp.logical_not(has_below))
        def _():
            fronts[g] = jnp.dot(resid_ref[g], pivot_ref[blk], preferred_element_type=f32).astype(
                bf16
            )

        @pl.when(has_above)
        def _():
            fwd_copy(g).start()

        @pl.when(jnp.logical_not(has_above))
        def _():
            out_ref[g] = fronts[g]

        @pl.when(jnp.logical_and(jnp.logical_not(has_above), has_below))
        def _():
            bwd_copy(g, fronts).start()

        return carry

    lax.fori_loop(0, chunks, fwd_body, 0)

    @pl.when(has_above)
    def _():
        halo_up().start()

    def image_body(b, carry):
        a = b // dc
        c = b % dc
        acc = jnp.dot(dir_ref[b], diag_ref[b], preferred_element_type=f32)
        acc = acc + jnp.dot(below_buf[b], lower_ref[b], preferred_element_type=f32)
        acc = acc + jnp.dot(above_buf[b], upper_ref[b], preferred_element_type=f32)
        upstream = jnp.where(c == 0, rim_buf[a], dir_ref[jnp.maximum(b - 1, 0)])
        img_ref[b] = acc + jnp.dot(upstream, downc_ref[b], preferred_element_type=f32)
        return carry

    def image():
        @pl.when(has_below)
        def _():
            halo_up().wait_recv()

        @pl.when(has_above)
        def _():
            halo_down().wait_recv()

        @pl.when(has_up)
        def _():
            for a in range(rims):
                rim_copy(a).wait_recv()

        lax.fori_loop(0, blocks, image_body, 0)

    early = h < n // 2

    @pl.when(early)
    def _():
        image()

    def bwd_body(g, carry):
        blk = g // per_block

        @pl.when(has_above)
        def _():
            bwd_copy(g, out_ref).wait_recv()
            carried = jnp.dot(bwd_buf[g], upper_ref[blk], preferred_element_type=f32).astype(bf16)
            out_ref[g] = (
                fronts[g].astype(f32) - jnp.dot(carried, pivot_ref[blk], preferred_element_type=f32)
            ).astype(bf16)

            @pl.when(has_below)
            def _():
                bwd_copy(g, out_ref).start()

        return carry

    lax.fori_loop(0, chunks, bwd_body, 0)

    @pl.when(jnp.logical_not(early))
    def _():
        image()

    def drain(g, carry):
        @pl.when(has_above)
        def _():
            fwd_copy(g).wait_send()

        @pl.when(has_below)
        def _():
            bwd_copy(g, out_ref).wait_send()

        return carry

    lax.fori_loop(0, chunks, drain, 0)

    @pl.when(has_below)
    def _():
        halo_down().wait_send()

    @pl.when(has_above)
    def _():
        halo_up().wait_send()

    @pl.when(has_dn)
    def _():
        for a in range(rims):
            rim_copy(a).wait_send()

    for p in range(nv):

        @pl.when(v != p)
        def _():
            gather_copy(p, p).wait_recv()
            gather_copy(p, v).wait_send()

    own_copy.wait()


def sweep(resid_l, dir_l, diag_l, lower_l, upper_l, pivot_l, downc_l, dc):
    n = lax.axis_size("elev")
    nv = lax.axis_size("valley")
    nd = lax.axis_size("down")
    chunks, rows, width = resid_l.shape
    blocks = lower_l.shape[0]
    per_block = chunks // blocks
    vmem = pl.BlockSpec(memory_space=pltpu.VMEM)
    flops = 2 * (2 * chunks * rows + 4 * dir_l.shape[0] * dir_l.shape[1]) * width * width
    weight_bytes = 6 * lower_l.size * lower_l.dtype.itemsize
    return pl.pallas_call(
        functools.partial(sweep_kernel, n=n, nv=nv, nd=nd, dc=dc, per_block=per_block),
        out_shape=(
            jax.ShapeDtypeStruct(resid_l.shape, resid_l.dtype),
            jax.ShapeDtypeStruct(dir_l.shape, jnp.float32),
            jax.ShapeDtypeStruct((nv * blocks,) + dir_l.shape[1:], dir_l.dtype),
        ),
        in_specs=[vmem] * 7,
        out_specs=(vmem, vmem, pl.BlockSpec(memory_space=pl.ANY)),
        scratch_shapes=[
            pltpu.VMEM(resid_l.shape, resid_l.dtype),
            pltpu.VMEM(resid_l.shape, resid_l.dtype),
            pltpu.VMEM(resid_l.shape, resid_l.dtype),
            pltpu.VMEM(dir_l.shape, dir_l.dtype),
            pltpu.VMEM(dir_l.shape, dir_l.dtype),
            pltpu.VMEM((blocks // dc,) + dir_l.shape[1:], dir_l.dtype),
            pltpu.SemaphoreType.DMA((chunks,)),
            pltpu.SemaphoreType.DMA((chunks,)),
            pltpu.SemaphoreType.DMA((chunks,)),
            pltpu.SemaphoreType.DMA((chunks,)),
            pltpu.SemaphoreType.DMA((2,)),
            pltpu.SemaphoreType.DMA((2,)),
            pltpu.SemaphoreType.DMA((blocks // dc,)),
            pltpu.SemaphoreType.DMA((blocks // dc,)),
            pltpu.SemaphoreType.DMA((nv,)),
            pltpu.SemaphoreType.DMA((nv,)),
            pltpu.SemaphoreType.DMA((1,)),
        ],
        compiler_params=pltpu.CompilerParams(collective_id=0, has_side_effects=True),
        cost_estimate=pl.CostEstimate(
            flops=flops, bytes_accessed=weight_bytes + 6 * resid_l.size * 2, transcendentals=0
        ),
    )(resid_l, dir_l, diag_l, lower_l, upper_l, pivot_l, downc_l)


def partner_kernel(col_ref, piece_ref, valc_ref, partial_ref, out_ref, held, sems, *, dc):
    blocks = held.shape[0]
    copies = []
    for b in range(blocks):
        col = col_ref[0, b // dc, b % dc]
        copy = pltpu.make_async_copy(piece_ref.at[col * dc + b % dc], held.at[b], sems.at[b])
        copy.start()
        copies.append(copy)
    for b in range(blocks):
        copies[b].wait()
        out_ref[b] = partial_ref[b] + jnp.dot(
            held[b], valc_ref[b], preferred_element_type=jnp.float32
        )


def add_partner(cols, piece, valc, partial, dc):
    blocks, rows, width = partial.shape
    vmem = pl.BlockSpec(memory_space=pltpu.VMEM)
    return pl.pallas_call(
        functools.partial(partner_kernel, dc=dc),
        out_shape=jax.ShapeDtypeStruct(partial.shape, partial.dtype),
        in_specs=[
            pl.BlockSpec(memory_space=pltpu.SMEM),
            pl.BlockSpec(memory_space=pl.ANY),
            vmem,
            vmem,
        ],
        out_specs=vmem,
        scratch_shapes=[
            pltpu.VMEM((blocks, rows, width), piece.dtype),
            pltpu.SemaphoreType.DMA((blocks,)),
        ],
        cost_estimate=pl.CostEstimate(
            flops=2 * blocks * rows * width * width,
            bytes_accessed=blocks * (rows * width * 10 + width * width * 2),
            transcendentals=0,
        ),
    )(cols, piece, valc, partial)


def local(
    resid,
    direction,
    diag_blocks,
    lower_blocks,
    upper_blocks,
    inv_pivots,
    down_coupling,
    valley_coupling,
    coupled_column,
):
    va, dc, nr, bs = resid.shape[1:]
    blocks = va * dc
    chunk_shape = (blocks * ROW_SPLIT, nr // ROW_SPLIT, bs)
    flat = (blocks, bs, bs)
    solved, partial, piece = sweep(
        resid[0].reshape(chunk_shape),
        direction[0].reshape(blocks, nr, bs),
        diag_blocks[0].reshape(flat),
        lower_blocks[0].reshape(flat),
        upper_blocks[0].reshape(flat),
        inv_pivots[0].reshape(flat),
        down_coupling[0].reshape(flat),
        dc,
    )

    image = add_partner(
        coupled_column,
        piece,
        valley_coupling[0].reshape(flat),
        partial,
        dc,
    )
    return (solved.reshape(resid.shape), image.reshape(resid.shape))


def solution(mesh):
    spec = P("elev", "valley", "down", None, None)
    in_specs = (spec,) * 8 + (P("elev", "valley", "down"),)
    out_specs = (spec, spec)
    return jax.shard_map(local, mesh=mesh, in_specs=in_specs, out_specs=out_specs, check_vma=False)
```

```python
import functools

import jax
import jax.numpy as jnp
from jax import lax
from jax.experimental import pallas as pl
from jax.experimental.pallas import tpu as pltpu
from jax.sharding import PartitionSpec as P

MESH = pl.DeviceIdType.MESH
ROW_SPLIT = 2


def apply_blocks(vectors, blocks):
    return jnp.einsum("bqrs,bqst->bqrt", vectors, blocks, preferred_element_type=jnp.float32)


def sweep_kernel(
    resid_ref,
    dir_ref,
    diag_ref,
    lower_ref,
    upper_ref,
    pivot_ref,
    downc_ref,
    out_ref,
    img_ref,
    fronts,
    fwd_buf,
    bwd_buf,
    below_buf,
    above_buf,
    rim_buf,
    fsend,
    frecv,
    bsend,
    brecv,
    hsend,
    hrecv,
    rsend,
    rrecv,
    *,
    n,
    nd,
    dc,
    per_block,
):
    f32 = jnp.float32
    bf16 = jnp.bfloat16
    h = lax.axis_index("elev")
    v = lax.axis_index("valley")
    d = lax.axis_index("down")
    chunks = resid_ref.shape[0]
    blocks = dir_ref.shape[0]
    rims = rim_buf.shape[0]
    has_below = h > 0
    has_above = h < n - 1
    has_up = d > 0
    has_dn = d < nd - 1

    barrier = pltpu.get_barrier_semaphore()
    peers = [
        (has_below, (h - 1, v, d)),
        (has_above, (h + 1, v, d)),
        (has_up, (h, v, d - 1)),
        (has_dn, (h, v, d + 1)),
    ]
    count = 0
    for cond, peer in peers:
        count = count + cond.astype(jnp.int32)

        @pl.when(cond)
        def _():
            pl.semaphore_signal(barrier, 1, device_id=peer, device_id_type=MESH)

    pl.semaphore_wait(barrier, count)

    def fwd_copy(g):
        return pltpu.make_async_remote_copy(
            src_ref=fronts.at[g],
            dst_ref=fwd_buf.at[g],
            send_sem=fsend.at[g],
            recv_sem=frecv.at[g],
            device_id=(h + 1, v, d),
            device_id_type=MESH,
        )

    def bwd_copy(g, src):
        return pltpu.make_async_remote_copy(
            src_ref=src.at[g],
            dst_ref=bwd_buf.at[g],
            send_sem=bsend.at[g],
            recv_sem=brecv.at[g],
            device_id=(h - 1, v, d),
            device_id_type=MESH,
        )

    def halo_down():
        return pltpu.make_async_remote_copy(
            src_ref=dir_ref,
            dst_ref=above_buf,
            send_sem=hsend.at[0],
            recv_sem=hrecv.at[0],
            device_id=(h - 1, v, d),
            device_id_type=MESH,
        )

    def halo_up():
        return pltpu.make_async_remote_copy(
            src_ref=dir_ref,
            dst_ref=below_buf,
            send_sem=hsend.at[1],
            recv_sem=hrecv.at[1],
            device_id=(h + 1, v, d),
            device_id_type=MESH,
        )

    def rim_copy(a):
        return pltpu.make_async_remote_copy(
            src_ref=dir_ref.at[a * dc + dc - 1],
            dst_ref=rim_buf.at[a],
            send_sem=rsend.at[a],
            recv_sem=rrecv.at[a],
            device_id=(h, v, d + 1),
            device_id_type=MESH,
        )

    @pl.when(has_below)
    def _():
        halo_down().start()

    @pl.when(has_dn)
    def _():
        for a in range(rims):
            rim_copy(a).start()

    @pl.when(jnp.logical_not(has_below))
    def _():
        below_buf[...] = jnp.zeros(below_buf.shape, bf16)

    @pl.when(jnp.logical_not(has_above))
    def _():
        above_buf[...] = jnp.zeros(above_buf.shape, bf16)

    @pl.when(jnp.logical_not(has_up))
    def _():
        rim_buf[...] = jnp.zeros(rim_buf.shape, bf16)

    def fwd_body(g, carry):
        blk = g // per_block

        @pl.when(has_below)
        def _():
            fwd_copy(g).wait_recv()
            inner = resid_ref[g].astype(f32) - jnp.dot(
                fwd_buf[g], lower_ref[blk], preferred_element_type=f32
            )
            fronts[g] = jnp.dot(
                inner.astype(bf16), pivot_ref[blk], preferred_element_type=f32
            ).astype(bf16)

        @pl.when(jnp.logical_not(has_below))
        def _():
            fronts[g] = jnp.dot(resid_ref[g], pivot_ref[blk], preferred_element_type=f32).astype(
                bf16
            )

        @pl.when(has_above)
        def _():
            fwd_copy(g).start()

        @pl.when(jnp.logical_not(has_above))
        def _():
            out_ref[g] = fronts[g]

        @pl.when(jnp.logical_and(jnp.logical_not(has_above), has_below))
        def _():
            bwd_copy(g, fronts).start()

        return carry

    lax.fori_loop(0, chunks, fwd_body, 0)

    @pl.when(has_above)
    def _():
        halo_up().start()

    def image_body(b, carry):
        a = b // dc
        c = b % dc
        acc = jnp.dot(dir_ref[b], diag_ref[b], preferred_element_type=f32)
        acc = acc + jnp.dot(below_buf[b], lower_ref[b], preferred_element_type=f32)
        acc = acc + jnp.dot(above_buf[b], upper_ref[b], preferred_element_type=f32)
        upstream = jnp.where(c == 0, rim_buf[a], dir_ref[jnp.maximum(b - 1, 0)])
        img_ref[b] = acc + jnp.dot(upstream, downc_ref[b], preferred_element_type=f32)
        return carry

    def image():
        @pl.when(has_below)
        def _():
            halo_up().wait_recv()

        @pl.when(has_above)
        def _():
            halo_down().wait_recv()

        @pl.when(has_up)
        def _():
            for a in range(rims):
                rim_copy(a).wait_recv()

        lax.fori_loop(0, blocks, image_body, 0)

    early = h < n // 2

    @pl.when(early)
    def _():
        image()

    def bwd_body(g, carry):
        blk = g // per_block

        @pl.when(has_above)
        def _():
            bwd_copy(g, out_ref).wait_recv()
            carried = jnp.dot(bwd_buf[g], upper_ref[blk], preferred_element_type=f32).astype(bf16)
            out_ref[g] = (
                fronts[g].astype(f32) - jnp.dot(carried, pivot_ref[blk], preferred_element_type=f32)
            ).astype(bf16)

            @pl.when(has_below)
            def _():
                bwd_copy(g, out_ref).start()

        return carry

    lax.fori_loop(0, chunks, bwd_body, 0)

    @pl.when(jnp.logical_not(early))
    def _():
        image()

    def drain(g, carry):
        @pl.when(has_above)
        def _():
            fwd_copy(g).wait_send()

        @pl.when(has_below)
        def _():
            bwd_copy(g, out_ref).wait_send()

        return carry

    lax.fori_loop(0, chunks, drain, 0)

    @pl.when(has_below)
    def _():
        halo_down().wait_send()

    @pl.when(has_above)
    def _():
        halo_up().wait_send()

    @pl.when(has_dn)
    def _():
        for a in range(rims):
            rim_copy(a).wait_send()


def sweep(resid_l, dir_l, diag_l, lower_l, upper_l, pivot_l, downc_l, dc):
    n = lax.axis_size("elev")
    nd = lax.axis_size("down")
    chunks, rows, width = resid_l.shape
    blocks = lower_l.shape[0]
    per_block = chunks // blocks
    vmem = pl.BlockSpec(memory_space=pltpu.VMEM)
    flops = 2 * (2 * chunks * rows + 4 * dir_l.shape[0] * dir_l.shape[1]) * width * width
    weight_bytes = 6 * lower_l.size * lower_l.dtype.itemsize
    return pl.pallas_call(
        functools.partial(sweep_kernel, n=n, nd=nd, dc=dc, per_block=per_block),
        out_shape=(
            jax.ShapeDtypeStruct(resid_l.shape, resid_l.dtype),
            jax.ShapeDtypeStruct(dir_l.shape, jnp.float32),
        ),
        in_specs=[vmem] * 7,
        out_specs=(vmem, vmem),
        scratch_shapes=[
            pltpu.VMEM(resid_l.shape, resid_l.dtype),
            pltpu.VMEM(resid_l.shape, resid_l.dtype),
            pltpu.VMEM(resid_l.shape, resid_l.dtype),
            pltpu.VMEM(dir_l.shape, dir_l.dtype),
            pltpu.VMEM(dir_l.shape, dir_l.dtype),
            pltpu.VMEM((blocks // dc,) + dir_l.shape[1:], dir_l.dtype),
            pltpu.SemaphoreType.DMA((chunks,)),
            pltpu.SemaphoreType.DMA((chunks,)),
            pltpu.SemaphoreType.DMA((chunks,)),
            pltpu.SemaphoreType.DMA((chunks,)),
            pltpu.SemaphoreType.DMA((2,)),
            pltpu.SemaphoreType.DMA((2,)),
            pltpu.SemaphoreType.DMA((blocks // dc,)),
            pltpu.SemaphoreType.DMA((blocks // dc,)),
        ],
        compiler_params=pltpu.CompilerParams(collective_id=0, has_side_effects=True),
        cost_estimate=pl.CostEstimate(
            flops=flops, bytes_accessed=weight_bytes + 6 * resid_l.size * 2, transcendentals=0
        ),
    )(resid_l, dir_l, diag_l, lower_l, upper_l, pivot_l, downc_l)


def partner_kernel(
    col_ref, piece_ref, valc_ref, partial_ref, solved_ref, out_ref, solved_out,
    held, vbuf, pbuf, sbuf, sems, *, dc
):
    blocks = held.shape[0]
    solved_in = pltpu.make_async_copy(solved_ref, sbuf, sems.at[0])
    solved_in.start()
    copies = []
    for b in range(blocks):
        col = col_ref[0, b // dc, b % dc]
        trio = (
            pltpu.make_async_copy(piece_ref.at[col * dc + b % dc], held.at[b], sems.at[1 + 3 * b]),
            pltpu.make_async_copy(valc_ref.at[b], vbuf.at[b], sems.at[2 + 3 * b]),
            pltpu.make_async_copy(partial_ref.at[b], pbuf.at[b], sems.at[3 + 3 * b]),
        )
        for copy in trio:
            copy.start()
        copies.append(trio)
    solved_in.wait()
    solved_back = pltpu.make_async_copy(sbuf, solved_out, sems.at[1 + 3 * blocks])
    solved_back.start()
    for b in range(blocks):
        for copy in copies[b]:
            copy.wait()
        out_ref[b] = pbuf[b] + jnp.dot(held[b], vbuf[b], preferred_element_type=jnp.float32)
    solved_back.wait()


def add_partner(cols, piece, valc, partial, solved, dc):
    blocks, rows, width = partial.shape
    hbm = pl.BlockSpec(memory_space=pl.ANY)
    return pl.pallas_call(
        functools.partial(partner_kernel, dc=dc),
        out_shape=(
            jax.ShapeDtypeStruct(partial.shape, partial.dtype),
            jax.ShapeDtypeStruct(solved.shape, solved.dtype),
        ),
        in_specs=[pl.BlockSpec(memory_space=pltpu.SMEM), hbm, hbm, hbm, hbm],
        out_specs=(pl.BlockSpec(memory_space=pltpu.VMEM), hbm),
        scratch_shapes=[
            pltpu.VMEM((blocks, rows, width), piece.dtype),
            pltpu.VMEM(valc.shape, valc.dtype),
            pltpu.VMEM(partial.shape, partial.dtype),
            pltpu.VMEM(solved.shape, solved.dtype),
            pltpu.SemaphoreType.DMA((2 + 3 * blocks,)),
        ],
        cost_estimate=pl.CostEstimate(
            flops=2 * blocks * rows * width * width,
            bytes_accessed=blocks * (rows * width * 10 + width * width * 2) + 4 * solved.size,
            transcendentals=0,
        ),
    )(cols, piece, valc, partial, solved)


def local(
    resid,
    direction,
    diag_blocks,
    lower_blocks,
    upper_blocks,
    inv_pivots,
    down_coupling,
    valley_coupling,
    coupled_column,
):
    va, dc, nr, bs = resid.shape[1:]
    blocks = va * dc
    chunk_shape = (blocks * ROW_SPLIT, nr // ROW_SPLIT, bs)
    flat = (blocks, bs, bs)
    solved, partial = sweep(
        resid[0].reshape(chunk_shape),
        direction[0].reshape(blocks, nr, bs),
        diag_blocks[0].reshape(flat),
        lower_blocks[0].reshape(flat),
        upper_blocks[0].reshape(flat),
        inv_pivots[0].reshape(flat),
        down_coupling[0].reshape(flat),
        dc,
    )

    current = direction[0]
    piece = lax.all_gather(current, "valley", axis=0, tiled=True)
    image, solved = add_partner(
        coupled_column,
        piece.reshape((-1, nr, bs)),
        valley_coupling[0].reshape(flat),
        partial,
        solved,
        dc,
    )
    return (solved.reshape(resid.shape), image.reshape(resid.shape))


def solution(mesh):
    spec = P("elev", "valley", "down", None, None)
    in_specs = (spec,) * 8 + (P("elev", "valley", "down"),)
    out_specs = (spec, spec)
    return jax.shard_map(local, mesh=mesh, in_specs=in_specs, out_specs=out_specs, check_vma=False)
```

```python
import functools

import jax
import jax.numpy as jnp
from jax import lax
from jax.experimental import pallas as pl
from jax.experimental.pallas import tpu as pltpu
from jax.sharding import PartitionSpec as P

MESH = pl.DeviceIdType.MESH
ROW_SPLIT = 2


def apply_blocks(vectors, blocks):
    return jnp.einsum("bqrs,bqst->bqrt", vectors, blocks, preferred_element_type=jnp.float32)


def sweep_kernel(
    resid_hbm,
    dir_hbm,
    diag_hbm,
    lower_hbm,
    upper_hbm,
    pivot_hbm,
    downc_hbm,
    out_ref,
    img_ref,
    fronts,
    fwd_buf,
    bwd_buf,
    below_buf,
    above_buf,
    rim_buf,
    fsend,
    frecv,
    bsend,
    brecv,
    hsend,
    hrecv,
    rsend,
    rrecv,
    resid_ref,
    dir_ref,
    diag_ref,
    lower_ref,
    upper_ref,
    pivot_ref,
    downc_ref,
    load_sems,
    *,
    n,
    nd,
    dc,
    per_block,
):
    f32 = jnp.float32
    bf16 = jnp.bfloat16
    loads = [
        pltpu.make_async_copy(src, dst, load_sems.at[i])
        for i, (src, dst) in enumerate(
            [
                (resid_hbm, resid_ref),
                (pivot_hbm, pivot_ref),
                (lower_hbm, lower_ref),
                (dir_hbm, dir_ref),
                (upper_hbm, upper_ref),
                (diag_hbm, diag_ref),
                (downc_hbm, downc_ref),
            ]
        )
    ]
    for load in loads:
        load.start()
    h = lax.axis_index("elev")
    v = lax.axis_index("valley")
    d = lax.axis_index("down")
    chunks = resid_ref.shape[0]
    blocks = dir_ref.shape[0]
    rims = rim_buf.shape[0]
    has_below = h > 0
    has_above = h < n - 1
    has_up = d > 0
    has_dn = d < nd - 1

    barrier = pltpu.get_barrier_semaphore()
    peers = [
        (has_below, (h - 1, v, d)),
        (has_above, (h + 1, v, d)),
        (has_up, (h, v, d - 1)),
        (has_dn, (h, v, d + 1)),
    ]
    count = 0
    for cond, peer in peers:
        count = count + cond.astype(jnp.int32)

        @pl.when(cond)
        def _():
            pl.semaphore_signal(barrier, 1, device_id=peer, device_id_type=MESH)

    pl.semaphore_wait(barrier, count)

    def fwd_copy(g):
        return pltpu.make_async_remote_copy(
            src_ref=fronts.at[g],
            dst_ref=fwd_buf.at[g],
            send_sem=fsend.at[g],
            recv_sem=frecv.at[g],
            device_id=(h + 1, v, d),
            device_id_type=MESH,
        )

    def bwd_copy(g, src):
        return pltpu.make_async_remote_copy(
            src_ref=src.at[g],
            dst_ref=bwd_buf.at[g],
            send_sem=bsend.at[g],
            recv_sem=brecv.at[g],
            device_id=(h - 1, v, d),
            device_id_type=MESH,
        )

    def halo_down():
        return pltpu.make_async_remote_copy(
            src_ref=dir_ref,
            dst_ref=above_buf,
            send_sem=hsend.at[0],
            recv_sem=hrecv.at[0],
            device_id=(h - 1, v, d),
            device_id_type=MESH,
        )

    def halo_up():
        return pltpu.make_async_remote_copy(
            src_ref=dir_ref,
            dst_ref=below_buf,
            send_sem=hsend.at[1],
            recv_sem=hrecv.at[1],
            device_id=(h + 1, v, d),
            device_id_type=MESH,
        )

    def rim_copy(a):
        return pltpu.make_async_remote_copy(
            src_ref=dir_ref.at[a * dc + dc - 1],
            dst_ref=rim_buf.at[a],
            send_sem=rsend.at[a],
            recv_sem=rrecv.at[a],
            device_id=(h, v, d + 1),
            device_id_type=MESH,
        )

    @pl.when(jnp.logical_not(has_below))
    def _():
        below_buf[...] = jnp.zeros(below_buf.shape, bf16)

    @pl.when(jnp.logical_not(has_above))
    def _():
        above_buf[...] = jnp.zeros(above_buf.shape, bf16)

    @pl.when(jnp.logical_not(has_up))
    def _():
        rim_buf[...] = jnp.zeros(rim_buf.shape, bf16)

    def fwd_body(g, carry):
        blk = g // per_block

        @pl.when(has_below)
        def _():
            fwd_copy(g).wait_recv()
            inner = resid_ref[g].astype(f32) - jnp.dot(
                fwd_buf[g], lower_ref[blk], preferred_element_type=f32
            )
            fronts[g] = jnp.dot(
                inner.astype(bf16), pivot_ref[blk], preferred_element_type=f32
            ).astype(bf16)

        @pl.when(jnp.logical_not(has_below))
        def _():
            fronts[g] = jnp.dot(resid_ref[g], pivot_ref[blk], preferred_element_type=f32).astype(
                bf16
            )

        @pl.when(has_above)
        def _():
            fwd_copy(g).start()

        @pl.when(jnp.logical_not(has_above))
        def _():
            out_ref[g] = fronts[g]

        @pl.when(jnp.logical_and(jnp.logical_not(has_above), has_below))
        def _():
            bwd_copy(g, fronts).start()

        return carry

    for load in loads[:3]:
        load.wait()

    lax.fori_loop(0, chunks, fwd_body, 0)

    for load in loads[3:]:
        load.wait()

    @pl.when(has_below)
    def _():
        halo_down().start()

    @pl.when(has_dn)
    def _():
        for a in range(rims):
            rim_copy(a).start()

    @pl.when(has_above)
    def _():
        halo_up().start()

    def image_body(b, carry):
        a = b // dc
        c = b % dc
        acc = jnp.dot(dir_ref[b], diag_ref[b], preferred_element_type=f32)
        acc = acc + jnp.dot(below_buf[b], lower_ref[b], preferred_element_type=f32)
        acc = acc + jnp.dot(above_buf[b], upper_ref[b], preferred_element_type=f32)
        upstream = jnp.where(c == 0, rim_buf[a], dir_ref[jnp.maximum(b - 1, 0)])
        img_ref[b] = acc + jnp.dot(upstream, downc_ref[b], preferred_element_type=f32)
        return carry

    def image():
        @pl.when(has_below)
        def _():
            halo_up().wait_recv()

        @pl.when(has_above)
        def _():
            halo_down().wait_recv()

        @pl.when(has_up)
        def _():
            for a in range(rims):
                rim_copy(a).wait_recv()

        lax.fori_loop(0, blocks, image_body, 0)

    early = h < n // 2

    @pl.when(early)
    def _():
        image()

    def bwd_body(g, carry):
        blk = g // per_block

        @pl.when(has_above)
        def _():
            bwd_copy(g, out_ref).wait_recv()
            carried = jnp.dot(bwd_buf[g], upper_ref[blk], preferred_element_type=f32).astype(bf16)
            out_ref[g] = (
                fronts[g].astype(f32) - jnp.dot(carried, pivot_ref[blk], preferred_element_type=f32)
            ).astype(bf16)

            @pl.when(has_below)
            def _():
                bwd_copy(g, out_ref).start()

        return carry

    lax.fori_loop(0, chunks, bwd_body, 0)

    @pl.when(jnp.logical_not(early))
    def _():
        image()

    def drain(g, carry):
        @pl.when(has_above)
        def _():
            fwd_copy(g).wait_send()

        @pl.when(has_below)
        def _():
            bwd_copy(g, out_ref).wait_send()

        return carry

    lax.fori_loop(0, chunks, drain, 0)

    @pl.when(has_below)
    def _():
        halo_down().wait_send()

    @pl.when(has_above)
    def _():
        halo_up().wait_send()

    @pl.when(has_dn)
    def _():
        for a in range(rims):
            rim_copy(a).wait_send()


def sweep(resid_l, dir_l, diag_l, lower_l, upper_l, pivot_l, downc_l, dc):
    n = lax.axis_size("elev")
    nd = lax.axis_size("down")
    chunks, rows, width = resid_l.shape
    blocks = lower_l.shape[0]
    per_block = chunks // blocks
    vmem = pl.BlockSpec(memory_space=pltpu.VMEM)
    flops = 2 * (2 * chunks * rows + 4 * dir_l.shape[0] * dir_l.shape[1]) * width * width
    weight_bytes = 6 * lower_l.size * lower_l.dtype.itemsize
    return pl.pallas_call(
        functools.partial(sweep_kernel, n=n, nd=nd, dc=dc, per_block=per_block),
        out_shape=(
            jax.ShapeDtypeStruct(resid_l.shape, resid_l.dtype),
            jax.ShapeDtypeStruct(dir_l.shape, jnp.float32),
        ),
        in_specs=[pl.BlockSpec(memory_space=pl.ANY)] * 7,
        out_specs=(vmem, vmem),
        scratch_shapes=[
            pltpu.VMEM(resid_l.shape, resid_l.dtype),
            pltpu.VMEM(resid_l.shape, resid_l.dtype),
            pltpu.VMEM(resid_l.shape, resid_l.dtype),
            pltpu.VMEM(dir_l.shape, dir_l.dtype),
            pltpu.VMEM(dir_l.shape, dir_l.dtype),
            pltpu.VMEM((blocks // dc,) + dir_l.shape[1:], dir_l.dtype),
            pltpu.SemaphoreType.DMA((chunks,)),
            pltpu.SemaphoreType.DMA((chunks,)),
            pltpu.SemaphoreType.DMA((chunks,)),
            pltpu.SemaphoreType.DMA((chunks,)),
            pltpu.SemaphoreType.DMA((2,)),
            pltpu.SemaphoreType.DMA((2,)),
            pltpu.SemaphoreType.DMA((blocks // dc,)),
            pltpu.SemaphoreType.DMA((blocks // dc,)),
            pltpu.VMEM(resid_l.shape, resid_l.dtype),
            pltpu.VMEM(dir_l.shape, dir_l.dtype),
            pltpu.VMEM(diag_l.shape, diag_l.dtype),
            pltpu.VMEM(lower_l.shape, lower_l.dtype),
            pltpu.VMEM(upper_l.shape, upper_l.dtype),
            pltpu.VMEM(pivot_l.shape, pivot_l.dtype),
            pltpu.VMEM(downc_l.shape, downc_l.dtype),
            pltpu.SemaphoreType.DMA((7,)),
        ],
        compiler_params=pltpu.CompilerParams(collective_id=0, has_side_effects=True),
        cost_estimate=pl.CostEstimate(
            flops=flops, bytes_accessed=weight_bytes + 6 * resid_l.size * 2, transcendentals=0
        ),
    )(resid_l, dir_l, diag_l, lower_l, upper_l, pivot_l, downc_l)


def partner_kernel(
    col_ref, piece_ref, valc_ref, partial_ref, solved_ref, out_ref, solved_out,
    held, vbuf, pbuf, sbuf, sems, *, dc
):
    blocks = held.shape[0]
    solved_in = pltpu.make_async_copy(solved_ref, sbuf, sems.at[0])
    solved_in.start()
    copies = []
    for b in range(blocks):
        col = col_ref[0, b // dc, b % dc]
        trio = (
            pltpu.make_async_copy(piece_ref.at[col * dc + b % dc], held.at[b], sems.at[1 + 3 * b]),
            pltpu.make_async_copy(valc_ref.at[b], vbuf.at[b], sems.at[2 + 3 * b]),
            pltpu.make_async_copy(partial_ref.at[b], pbuf.at[b], sems.at[3 + 3 * b]),
        )
        for copy in trio:
            copy.start()
        copies.append(trio)
    solved_in.wait()
    solved_back = pltpu.make_async_copy(sbuf, solved_out, sems.at[1 + 3 * blocks])
    solved_back.start()
    for b in range(blocks):
        for copy in copies[b]:
            copy.wait()
        out_ref[b] = pbuf[b] + jnp.dot(held[b], vbuf[b], preferred_element_type=jnp.float32)
    solved_back.wait()


def add_partner(cols, piece, valc, partial, solved, dc):
    blocks, rows, width = partial.shape
    hbm = pl.BlockSpec(memory_space=pl.ANY)
    return pl.pallas_call(
        functools.partial(partner_kernel, dc=dc),
        out_shape=(
            jax.ShapeDtypeStruct(partial.shape, partial.dtype),
            jax.ShapeDtypeStruct(solved.shape, solved.dtype),
        ),
        in_specs=[pl.BlockSpec(memory_space=pltpu.SMEM), hbm, hbm, hbm, hbm],
        out_specs=(pl.BlockSpec(memory_space=pltpu.VMEM), hbm),
        scratch_shapes=[
            pltpu.VMEM((blocks, rows, width), piece.dtype),
            pltpu.VMEM(valc.shape, valc.dtype),
            pltpu.VMEM(partial.shape, partial.dtype),
            pltpu.VMEM(solved.shape, solved.dtype),
            pltpu.SemaphoreType.DMA((2 + 3 * blocks,)),
        ],
        cost_estimate=pl.CostEstimate(
            flops=2 * blocks * rows * width * width,
            bytes_accessed=blocks * (rows * width * 10 + width * width * 2) + 4 * solved.size,
            transcendentals=0,
        ),
    )(cols, piece, valc, partial, solved)


def local(
    resid,
    direction,
    diag_blocks,
    lower_blocks,
    upper_blocks,
    inv_pivots,
    down_coupling,
    valley_coupling,
    coupled_column,
):
    va, dc, nr, bs = resid.shape[1:]
    blocks = va * dc
    chunk_shape = (blocks * ROW_SPLIT, nr // ROW_SPLIT, bs)
    flat = (blocks, bs, bs)
    solved, partial = sweep(
        resid[0].reshape(chunk_shape),
        direction[0].reshape(blocks, nr, bs),
        diag_blocks[0].reshape(flat),
        lower_blocks[0].reshape(flat),
        upper_blocks[0].reshape(flat),
        inv_pivots[0].reshape(flat),
        down_coupling[0].reshape(flat),
        dc,
    )

    current = direction[0]
    piece = lax.all_gather(current, "valley", axis=0, tiled=True)
    image, solved = add_partner(
        coupled_column,
        piece.reshape((-1, nr, bs)),
        valley_coupling[0].reshape(flat),
        partial,
        solved,
        dc,
    )
    return (solved.reshape(resid.shape), image.reshape(resid.shape))


def solution(mesh):
    spec = P("elev", "valley", "down", None, None)
    in_specs = (spec,) * 8 + (P("elev", "valley", "down"),)
    out_specs = (spec, spec)
    return jax.shard_map(local, mesh=mesh, in_specs=in_specs, out_specs=out_specs, check_vma=False)
```

```python
import functools

import jax
import jax.numpy as jnp
from jax import lax
from jax.experimental import pallas as pl
from jax.experimental.pallas import tpu as pltpu
from jax.sharding import PartitionSpec as P

MESH = pl.DeviceIdType.MESH
ROW_SPLIT = 2


def apply_blocks(vectors, blocks):
    return jnp.einsum("bqrs,bqst->bqrt", vectors, blocks, preferred_element_type=jnp.float32)


def sweep_kernel(
    resid_hbm,
    dir_hbm,
    diag_hbm,
    lower_hbm,
    upper_hbm,
    pivot_hbm,
    downc_hbm,
    out_ref,
    img_ref,
    fronts,
    fwd_buf,
    bwd_buf,
    below_buf,
    above_buf,
    rim_buf,
    fsend,
    frecv,
    bsend,
    brecv,
    hsend,
    hrecv,
    rsend,
    rrecv,
    resid_ref,
    dir_ref,
    diag_ref,
    lower_ref,
    upper_ref,
    pivot_ref,
    downc_ref,
    load_sems,
    *,
    n,
    nd,
    dc,
    per_block,
):
    f32 = jnp.float32
    bf16 = jnp.bfloat16
    loads = [
        pltpu.make_async_copy(src, dst, load_sems.at[i])
        for i, (src, dst) in enumerate(
            [
                (dir_hbm, dir_ref),
                (resid_hbm, resid_ref),
                (pivot_hbm, pivot_ref),
                (lower_hbm, lower_ref),
                (upper_hbm, upper_ref),
                (diag_hbm, diag_ref),
                (downc_hbm, downc_ref),
            ]
        )
    ]
    for load in loads:
        load.start()
    h = lax.axis_index("elev")
    v = lax.axis_index("valley")
    d = lax.axis_index("down")
    chunks = resid_ref.shape[0]
    blocks = dir_ref.shape[0]
    rims = rim_buf.shape[0]
    has_below = h > 0
    has_above = h < n - 1
    has_up = d > 0
    has_dn = d < nd - 1

    barrier = pltpu.get_barrier_semaphore()
    peers = [
        (has_below, (h - 1, v, d)),
        (has_above, (h + 1, v, d)),
        (has_up, (h, v, d - 1)),
        (has_dn, (h, v, d + 1)),
    ]
    count = 0
    for cond, peer in peers:
        count = count + cond.astype(jnp.int32)

        @pl.when(cond)
        def _():
            pl.semaphore_signal(barrier, 1, device_id=peer, device_id_type=MESH)

    pl.semaphore_wait(barrier, count)

    def fwd_copy(g):
        return pltpu.make_async_remote_copy(
            src_ref=fronts.at[g],
            dst_ref=fwd_buf.at[g],
            send_sem=fsend.at[g],
            recv_sem=frecv.at[g],
            device_id=(h + 1, v, d),
            device_id_type=MESH,
        )

    def bwd_copy(g, src):
        return pltpu.make_async_remote_copy(
            src_ref=src.at[g],
            dst_ref=bwd_buf.at[g],
            send_sem=bsend.at[g],
            recv_sem=brecv.at[g],
            device_id=(h - 1, v, d),
            device_id_type=MESH,
        )

    def halo_down():
        return pltpu.make_async_remote_copy(
            src_ref=dir_ref,
            dst_ref=above_buf,
            send_sem=hsend.at[0],
            recv_sem=hrecv.at[0],
            device_id=(h - 1, v, d),
            device_id_type=MESH,
        )

    def halo_up():
        return pltpu.make_async_remote_copy(
            src_ref=dir_ref,
            dst_ref=below_buf,
            send_sem=hsend.at[1],
            recv_sem=hrecv.at[1],
            device_id=(h + 1, v, d),
            device_id_type=MESH,
        )

    def rim_copy(a):
        return pltpu.make_async_remote_copy(
            src_ref=dir_ref.at[a * dc + dc - 1],
            dst_ref=rim_buf.at[a],
            send_sem=rsend.at[a],
            recv_sem=rrecv.at[a],
            device_id=(h, v, d + 1),
            device_id_type=MESH,
        )

    @pl.when(jnp.logical_not(has_below))
    def _():
        below_buf[...] = jnp.zeros(below_buf.shape, bf16)

    @pl.when(jnp.logical_not(has_above))
    def _():
        above_buf[...] = jnp.zeros(above_buf.shape, bf16)

    @pl.when(jnp.logical_not(has_up))
    def _():
        rim_buf[...] = jnp.zeros(rim_buf.shape, bf16)

    def fwd_body(g, carry):
        blk = g // per_block

        @pl.when(has_below)
        def _():
            fwd_copy(g).wait_recv()
            inner = resid_ref[g].astype(f32) - jnp.dot(
                fwd_buf[g], lower_ref[blk], preferred_element_type=f32
            )
            fronts[g] = jnp.dot(
                inner.astype(bf16), pivot_ref[blk], preferred_element_type=f32
            ).astype(bf16)

        @pl.when(jnp.logical_not(has_below))
        def _():
            fronts[g] = jnp.dot(resid_ref[g], pivot_ref[blk], preferred_element_type=f32).astype(
                bf16
            )

        @pl.when(has_above)
        def _():
            fwd_copy(g).start()

        @pl.when(jnp.logical_not(has_above))
        def _():
            out_ref[g] = fronts[g]

        @pl.when(jnp.logical_and(jnp.logical_not(has_above), has_below))
        def _():
            bwd_copy(g, fronts).start()

        return carry

    loads[0].wait()

    @pl.when(has_below)
    def _():
        halo_down().start()

    @pl.when(has_dn)
    def _():
        for a in range(rims):
            rim_copy(a).start()

    for load in loads[1:4]:
        load.wait()

    lax.fori_loop(0, chunks, fwd_body, 0)

    for load in loads[4:]:
        load.wait()

    @pl.when(has_above)
    def _():
        halo_up().start()

    def image_body(b, carry):
        a = b // dc
        c = b % dc
        acc = jnp.dot(dir_ref[b], diag_ref[b], preferred_element_type=f32)
        acc = acc + jnp.dot(below_buf[b], lower_ref[b], preferred_element_type=f32)
        acc = acc + jnp.dot(above_buf[b], upper_ref[b], preferred_element_type=f32)
        upstream = jnp.where(c == 0, rim_buf[a], dir_ref[jnp.maximum(b - 1, 0)])
        img_ref[b] = acc + jnp.dot(upstream, downc_ref[b], preferred_element_type=f32)
        return carry

    def image():
        @pl.when(has_below)
        def _():
            halo_up().wait_recv()

        @pl.when(has_above)
        def _():
            halo_down().wait_recv()

        @pl.when(has_up)
        def _():
            for a in range(rims):
                rim_copy(a).wait_recv()

        lax.fori_loop(0, blocks, image_body, 0)

    early = h < n // 2

    @pl.when(early)
    def _():
        image()

    def bwd_body(g, carry):
        blk = g // per_block

        @pl.when(has_above)
        def _():
            bwd_copy(g, out_ref).wait_recv()
            carried = jnp.dot(bwd_buf[g], upper_ref[blk], preferred_element_type=f32).astype(bf16)
            out_ref[g] = (
                fronts[g].astype(f32) - jnp.dot(carried, pivot_ref[blk], preferred_element_type=f32)
            ).astype(bf16)

            @pl.when(has_below)
            def _():
                bwd_copy(g, out_ref).start()

        return carry

    lax.fori_loop(0, chunks, bwd_body, 0)

    @pl.when(jnp.logical_not(early))
    def _():
        image()

    def drain(g, carry):
        @pl.when(has_above)
        def _():
            fwd_copy(g).wait_send()

        @pl.when(has_below)
        def _():
            bwd_copy(g, out_ref).wait_send()

        return carry

    lax.fori_loop(0, chunks, drain, 0)

    @pl.when(has_below)
    def _():
        halo_down().wait_send()

    @pl.when(has_above)
    def _():
        halo_up().wait_send()

    @pl.when(has_dn)
    def _():
        for a in range(rims):
            rim_copy(a).wait_send()


def sweep(resid_l, dir_l, diag_l, lower_l, upper_l, pivot_l, downc_l, dc):
    n = lax.axis_size("elev")
    nd = lax.axis_size("down")
    chunks, rows, width = resid_l.shape
    blocks = lower_l.shape[0]
    per_block = chunks // blocks
    vmem = pl.BlockSpec(memory_space=pltpu.VMEM)
    flops = 2 * (2 * chunks * rows + 4 * dir_l.shape[0] * dir_l.shape[1]) * width * width
    weight_bytes = 6 * lower_l.size * lower_l.dtype.itemsize
    return pl.pallas_call(
        functools.partial(sweep_kernel, n=n, nd=nd, dc=dc, per_block=per_block),
        out_shape=(
            jax.ShapeDtypeStruct(resid_l.shape, resid_l.dtype),
            jax.ShapeDtypeStruct(dir_l.shape, jnp.float32),
        ),
        in_specs=[pl.BlockSpec(memory_space=pl.ANY)] * 7,
        out_specs=(vmem, vmem),
        scratch_shapes=[
            pltpu.VMEM(resid_l.shape, resid_l.dtype),
            pltpu.VMEM(resid_l.shape, resid_l.dtype),
            pltpu.VMEM(resid_l.shape, resid_l.dtype),
            pltpu.VMEM(dir_l.shape, dir_l.dtype),
            pltpu.VMEM(dir_l.shape, dir_l.dtype),
            pltpu.VMEM((blocks // dc,) + dir_l.shape[1:], dir_l.dtype),
            pltpu.SemaphoreType.DMA((chunks,)),
            pltpu.SemaphoreType.DMA((chunks,)),
            pltpu.SemaphoreType.DMA((chunks,)),
            pltpu.SemaphoreType.DMA((chunks,)),
            pltpu.SemaphoreType.DMA((2,)),
            pltpu.SemaphoreType.DMA((2,)),
            pltpu.SemaphoreType.DMA((blocks // dc,)),
            pltpu.SemaphoreType.DMA((blocks // dc,)),
            pltpu.VMEM(resid_l.shape, resid_l.dtype),
            pltpu.VMEM(dir_l.shape, dir_l.dtype),
            pltpu.VMEM(diag_l.shape, diag_l.dtype),
            pltpu.VMEM(lower_l.shape, lower_l.dtype),
            pltpu.VMEM(upper_l.shape, upper_l.dtype),
            pltpu.VMEM(pivot_l.shape, pivot_l.dtype),
            pltpu.VMEM(downc_l.shape, downc_l.dtype),
            pltpu.SemaphoreType.DMA((7,)),
        ],
        compiler_params=pltpu.CompilerParams(collective_id=0, has_side_effects=True),
        cost_estimate=pl.CostEstimate(
            flops=flops, bytes_accessed=weight_bytes + 6 * resid_l.size * 2, transcendentals=0
        ),
    )(resid_l, dir_l, diag_l, lower_l, upper_l, pivot_l, downc_l)


def partner_kernel(
    col_ref, piece_ref, valc_ref, partial_ref, solved_ref, out_ref, solved_out,
    held, vbuf, pbuf, sbuf, sems, *, dc
):
    blocks = held.shape[0]
    solved_in = pltpu.make_async_copy(solved_ref, sbuf, sems.at[0])
    solved_in.start()
    copies = []
    for b in range(blocks):
        col = col_ref[0, b // dc, b % dc]
        trio = (
            pltpu.make_async_copy(piece_ref.at[col * dc + b % dc], held.at[b], sems.at[1 + 3 * b]),
            pltpu.make_async_copy(valc_ref.at[b], vbuf.at[b], sems.at[2 + 3 * b]),
            pltpu.make_async_copy(partial_ref.at[b], pbuf.at[b], sems.at[3 + 3 * b]),
        )
        for copy in trio:
            copy.start()
        copies.append(trio)
    solved_in.wait()
    solved_back = pltpu.make_async_copy(sbuf, solved_out, sems.at[1 + 3 * blocks])
    solved_back.start()
    for b in range(blocks):
        for copy in copies[b]:
            copy.wait()
        out_ref[b] = pbuf[b] + jnp.dot(held[b], vbuf[b], preferred_element_type=jnp.float32)
    solved_back.wait()


def add_partner(cols, piece, valc, partial, solved, dc):
    blocks, rows, width = partial.shape
    hbm = pl.BlockSpec(memory_space=pl.ANY)
    return pl.pallas_call(
        functools.partial(partner_kernel, dc=dc),
        out_shape=(
            jax.ShapeDtypeStruct(partial.shape, partial.dtype),
            jax.ShapeDtypeStruct(solved.shape, solved.dtype),
        ),
        in_specs=[pl.BlockSpec(memory_space=pltpu.SMEM), hbm, hbm, hbm, hbm],
        out_specs=(pl.BlockSpec(memory_space=pltpu.VMEM), hbm),
        scratch_shapes=[
            pltpu.VMEM((blocks, rows, width), piece.dtype),
            pltpu.VMEM(valc.shape, valc.dtype),
            pltpu.VMEM(partial.shape, partial.dtype),
            pltpu.VMEM(solved.shape, solved.dtype),
            pltpu.SemaphoreType.DMA((2 + 3 * blocks,)),
        ],
        cost_estimate=pl.CostEstimate(
            flops=2 * blocks * rows * width * width,
            bytes_accessed=blocks * (rows * width * 10 + width * width * 2) + 4 * solved.size,
            transcendentals=0,
        ),
    )(cols, piece, valc, partial, solved)


def local(
    resid,
    direction,
    diag_blocks,
    lower_blocks,
    upper_blocks,
    inv_pivots,
    down_coupling,
    valley_coupling,
    coupled_column,
):
    va, dc, nr, bs = resid.shape[1:]
    blocks = va * dc
    chunk_shape = (blocks * ROW_SPLIT, nr // ROW_SPLIT, bs)
    flat = (blocks, bs, bs)
    solved, partial = sweep(
        resid[0].reshape(chunk_shape),
        direction[0].reshape(blocks, nr, bs),
        diag_blocks[0].reshape(flat),
        lower_blocks[0].reshape(flat),
        upper_blocks[0].reshape(flat),
        inv_pivots[0].reshape(flat),
        down_coupling[0].reshape(flat),
        dc,
    )

    current = direction[0]
    piece = lax.all_gather(current, "valley", axis=0, tiled=True)
    image, solved = add_partner(
        coupled_column,
        piece.reshape((-1, nr, bs)),
        valley_coupling[0].reshape(flat),
        partial,
        solved,
        dc,
    )
    return (solved.reshape(resid.shape), image.reshape(resid.shape))


def solution(mesh):
    spec = P("elev", "valley", "down", None, None)
    in_specs = (spec,) * 8 + (P("elev", "valley", "down"),)
    out_specs = (spec, spec)
    return jax.shard_map(local, mesh=mesh, in_specs=in_specs, out_specs=out_specs, check_vma=False)
```

```python
import functools

import jax
import jax.numpy as jnp
from jax import lax
from jax.experimental import pallas as pl
from jax.experimental.pallas import tpu as pltpu
from jax.sharding import PartitionSpec as P

MESH = pl.DeviceIdType.MESH
ROW_SPLIT = 2
LAG = 3


def apply_blocks(vectors, blocks):
    return jnp.einsum("bqrs,bqst->bqrt", vectors, blocks, preferred_element_type=jnp.float32)


def sweep_kernel(
    resid_hbm,
    dir_hbm,
    diag_hbm,
    lower_hbm,
    upper_hbm,
    pivot_hbm,
    downc_hbm,
    out_ref,
    img_ref,
    fronts,
    fwd_buf,
    bwd_buf,
    below_buf,
    above_buf,
    rim_buf,
    fsend,
    frecv,
    bsend,
    brecv,
    hsend,
    hrecv,
    rsend,
    rrecv,
    resid_ref,
    dir_ref,
    diag_ref,
    lower_ref,
    upper_ref,
    pivot_ref,
    downc_ref,
    load_sems,
    *,
    n,
    nd,
    dc,
    per_block,
):
    f32 = jnp.float32
    bf16 = jnp.bfloat16
    loads = [
        pltpu.make_async_copy(src, dst, load_sems.at[i])
        for i, (src, dst) in enumerate(
            [
                (dir_hbm, dir_ref),
                (resid_hbm, resid_ref),
                (pivot_hbm, pivot_ref),
                (lower_hbm, lower_ref),
                (upper_hbm, upper_ref),
                (diag_hbm, diag_ref),
                (downc_hbm, downc_ref),
            ]
        )
    ]
    for load in loads:
        load.start()
    h = lax.axis_index("elev")
    v = lax.axis_index("valley")
    d = lax.axis_index("down")
    chunks = resid_ref.shape[0]
    blocks = dir_ref.shape[0]
    rims = rim_buf.shape[0]
    has_below = h > 0
    has_above = h < n - 1
    has_up = d > 0
    has_dn = d < nd - 1

    barrier = pltpu.get_barrier_semaphore()
    peers = [
        (has_below, (h - 1, v, d)),
        (has_above, (h + 1, v, d)),
        (has_up, (h, v, d - 1)),
        (has_dn, (h, v, d + 1)),
    ]
    count = 0
    for cond, peer in peers:
        count = count + cond.astype(jnp.int32)

        @pl.when(cond)
        def _():
            pl.semaphore_signal(barrier, 1, device_id=peer, device_id_type=MESH)

    pl.semaphore_wait(barrier, count)

    def fwd_copy(g):
        return pltpu.make_async_remote_copy(
            src_ref=fronts.at[g],
            dst_ref=fwd_buf.at[g],
            send_sem=fsend.at[g],
            recv_sem=frecv.at[g],
            device_id=(h + 1, v, d),
            device_id_type=MESH,
        )

    def bwd_copy(g, src):
        return pltpu.make_async_remote_copy(
            src_ref=src.at[g],
            dst_ref=bwd_buf.at[g],
            send_sem=bsend.at[g],
            recv_sem=brecv.at[g],
            device_id=(h - 1, v, d),
            device_id_type=MESH,
        )

    def halo_down():
        return pltpu.make_async_remote_copy(
            src_ref=dir_ref,
            dst_ref=above_buf,
            send_sem=hsend.at[0],
            recv_sem=hrecv.at[0],
            device_id=(h - 1, v, d),
            device_id_type=MESH,
        )

    def halo_up():
        return pltpu.make_async_remote_copy(
            src_ref=dir_ref,
            dst_ref=below_buf,
            send_sem=hsend.at[1],
            recv_sem=hrecv.at[1],
            device_id=(h + 1, v, d),
            device_id_type=MESH,
        )

    def rim_copy(a):
        return pltpu.make_async_remote_copy(
            src_ref=dir_ref.at[a * dc + dc - 1],
            dst_ref=rim_buf.at[a],
            send_sem=rsend.at[a],
            recv_sem=rrecv.at[a],
            device_id=(h, v, d + 1),
            device_id_type=MESH,
        )

    @pl.when(jnp.logical_not(has_below))
    def _():
        below_buf[...] = jnp.zeros(below_buf.shape, bf16)

    @pl.when(jnp.logical_not(has_above))
    def _():
        above_buf[...] = jnp.zeros(above_buf.shape, bf16)

    @pl.when(jnp.logical_not(has_up))
    def _():
        rim_buf[...] = jnp.zeros(rim_buf.shape, bf16)

    def fwd_body(g, carry):
        fwd_step(g)
        return carry

    def fwd_step(g):
        blk = g // per_block

        @pl.when(has_below)
        def _():
            fwd_copy(g).wait_recv()
            inner = resid_ref[g].astype(f32) - jnp.dot(
                fwd_buf[g], lower_ref[blk], preferred_element_type=f32
            )
            fronts[g] = jnp.dot(
                inner.astype(bf16), pivot_ref[blk], preferred_element_type=f32
            ).astype(bf16)

        @pl.when(jnp.logical_not(has_below))
        def _():
            fronts[g] = jnp.dot(resid_ref[g], pivot_ref[blk], preferred_element_type=f32).astype(
                bf16
            )

        @pl.when(has_above)
        def _():
            fwd_copy(g).start()

        @pl.when(jnp.logical_not(has_above))
        def _():
            out_ref[g] = fronts[g]

        @pl.when(jnp.logical_and(jnp.logical_not(has_above), has_below))
        def _():
            bwd_copy(g, fronts).start()

    loads[0].wait()

    @pl.when(has_below)
    def _():
        halo_down().start()

    @pl.when(has_dn)
    def _():
        for a in range(rims):
            rim_copy(a).start()

    for load in loads[1:4]:
        load.wait()

    def bwd_body(g, carry):
        bwd_step(g)
        return carry

    def bwd_step(g):
        blk = g // per_block

        @pl.when(has_above)
        def _():
            bwd_copy(g, out_ref).wait_recv()
            carried = jnp.dot(bwd_buf[g], upper_ref[blk], preferred_element_type=f32).astype(bf16)
            out_ref[g] = (
                fronts[g].astype(f32) - jnp.dot(carried, pivot_ref[blk], preferred_element_type=f32)
            ).astype(bf16)

            @pl.when(has_below)
            def _():
                bwd_copy(g, out_ref).start()

    is_turn = h == n - 2

    def turn_body(i, carry):
        @pl.when(i < chunks)
        def _():
            fwd_step(i)

        @pl.when(i >= LAG)
        def _():
            bwd_step(i - LAG)

        return carry

    @pl.when(is_turn)
    def _():
        for load in loads[4:]:
            load.wait()
        lax.fori_loop(0, chunks + LAG, turn_body, 0)

    @pl.when(jnp.logical_not(is_turn))
    def _():
        lax.fori_loop(0, chunks, fwd_body, 0)
        for load in loads[4:]:
            load.wait()

    @pl.when(has_above)
    def _():
        halo_up().start()

    def image_body(b, carry):
        a = b // dc
        c = b % dc
        acc = jnp.dot(dir_ref[b], diag_ref[b], preferred_element_type=f32)
        acc = acc + jnp.dot(below_buf[b], lower_ref[b], preferred_element_type=f32)
        acc = acc + jnp.dot(above_buf[b], upper_ref[b], preferred_element_type=f32)
        upstream = jnp.where(c == 0, rim_buf[a], dir_ref[jnp.maximum(b - 1, 0)])
        img_ref[b] = acc + jnp.dot(upstream, downc_ref[b], preferred_element_type=f32)
        return carry

    def image():
        @pl.when(has_below)
        def _():
            halo_up().wait_recv()

        @pl.when(has_above)
        def _():
            halo_down().wait_recv()

        @pl.when(has_up)
        def _():
            for a in range(rims):
                rim_copy(a).wait_recv()

        lax.fori_loop(0, blocks, image_body, 0)

    early = h < n // 2

    @pl.when(early)
    def _():
        image()

    @pl.when(jnp.logical_not(is_turn))
    def _():
        lax.fori_loop(0, chunks, bwd_body, 0)

    @pl.when(jnp.logical_not(early))
    def _():
        image()

    def drain(g, carry):
        @pl.when(has_above)
        def _():
            fwd_copy(g).wait_send()

        @pl.when(has_below)
        def _():
            bwd_copy(g, out_ref).wait_send()

        return carry

    lax.fori_loop(0, chunks, drain, 0)

    @pl.when(has_below)
    def _():
        halo_down().wait_send()

    @pl.when(has_above)
    def _():
        halo_up().wait_send()

    @pl.when(has_dn)
    def _():
        for a in range(rims):
            rim_copy(a).wait_send()


def sweep(resid_l, dir_l, diag_l, lower_l, upper_l, pivot_l, downc_l, dc):
    n = lax.axis_size("elev")
    nd = lax.axis_size("down")
    chunks, rows, width = resid_l.shape
    blocks = lower_l.shape[0]
    per_block = chunks // blocks
    vmem = pl.BlockSpec(memory_space=pltpu.VMEM)
    flops = 2 * (2 * chunks * rows + 4 * dir_l.shape[0] * dir_l.shape[1]) * width * width
    weight_bytes = 6 * lower_l.size * lower_l.dtype.itemsize
    return pl.pallas_call(
        functools.partial(sweep_kernel, n=n, nd=nd, dc=dc, per_block=per_block),
        out_shape=(
            jax.ShapeDtypeStruct(resid_l.shape, resid_l.dtype),
            jax.ShapeDtypeStruct(dir_l.shape, jnp.float32),
        ),
        in_specs=[pl.BlockSpec(memory_space=pl.ANY)] * 7,
        out_specs=(vmem, vmem),
        scratch_shapes=[
            pltpu.VMEM(resid_l.shape, resid_l.dtype),
            pltpu.VMEM(resid_l.shape, resid_l.dtype),
            pltpu.VMEM(resid_l.shape, resid_l.dtype),
            pltpu.VMEM(dir_l.shape, dir_l.dtype),
            pltpu.VMEM(dir_l.shape, dir_l.dtype),
            pltpu.VMEM((blocks // dc,) + dir_l.shape[1:], dir_l.dtype),
            pltpu.SemaphoreType.DMA((chunks,)),
            pltpu.SemaphoreType.DMA((chunks,)),
            pltpu.SemaphoreType.DMA((chunks,)),
            pltpu.SemaphoreType.DMA((chunks,)),
            pltpu.SemaphoreType.DMA((2,)),
            pltpu.SemaphoreType.DMA((2,)),
            pltpu.SemaphoreType.DMA((blocks // dc,)),
            pltpu.SemaphoreType.DMA((blocks // dc,)),
            pltpu.VMEM(resid_l.shape, resid_l.dtype),
            pltpu.VMEM(dir_l.shape, dir_l.dtype),
            pltpu.VMEM(diag_l.shape, diag_l.dtype),
            pltpu.VMEM(lower_l.shape, lower_l.dtype),
            pltpu.VMEM(upper_l.shape, upper_l.dtype),
            pltpu.VMEM(pivot_l.shape, pivot_l.dtype),
            pltpu.VMEM(downc_l.shape, downc_l.dtype),
            pltpu.SemaphoreType.DMA((7,)),
        ],
        compiler_params=pltpu.CompilerParams(collective_id=0, has_side_effects=True),
        cost_estimate=pl.CostEstimate(
            flops=flops, bytes_accessed=weight_bytes + 6 * resid_l.size * 2, transcendentals=0
        ),
    )(resid_l, dir_l, diag_l, lower_l, upper_l, pivot_l, downc_l)


def partner_kernel(
    col_ref, piece_ref, valc_ref, partial_ref, solved_ref, out_ref, solved_out,
    held, vbuf, pbuf, sbuf, sems, *, dc
):
    blocks = held.shape[0]
    solved_in = pltpu.make_async_copy(solved_ref, sbuf, sems.at[0])
    solved_in.start()
    copies = []
    for b in range(blocks):
        col = col_ref[0, b // dc, b % dc]
        trio = (
            pltpu.make_async_copy(piece_ref.at[col * dc + b % dc], held.at[b], sems.at[1 + 3 * b]),
            pltpu.make_async_copy(valc_ref.at[b], vbuf.at[b], sems.at[2 + 3 * b]),
            pltpu.make_async_copy(partial_ref.at[b], pbuf.at[b], sems.at[3 + 3 * b]),
        )
        for copy in trio:
            copy.start()
        copies.append(trio)
    solved_in.wait()
    solved_back = pltpu.make_async_copy(sbuf, solved_out, sems.at[1 + 3 * blocks])
    solved_back.start()
    for b in range(blocks):
        for copy in copies[b]:
            copy.wait()
        out_ref[b] = pbuf[b] + jnp.dot(held[b], vbuf[b], preferred_element_type=jnp.float32)
    solved_back.wait()


def add_partner(cols, piece, valc, partial, solved, dc):
    blocks, rows, width = partial.shape
    hbm = pl.BlockSpec(memory_space=pl.ANY)
    return pl.pallas_call(
        functools.partial(partner_kernel, dc=dc),
        out_shape=(
            jax.ShapeDtypeStruct(partial.shape, partial.dtype),
            jax.ShapeDtypeStruct(solved.shape, solved.dtype),
        ),
        in_specs=[pl.BlockSpec(memory_space=pltpu.SMEM), hbm, hbm, hbm, hbm],
        out_specs=(pl.BlockSpec(memory_space=pltpu.VMEM), hbm),
        scratch_shapes=[
            pltpu.VMEM((blocks, rows, width), piece.dtype),
            pltpu.VMEM(valc.shape, valc.dtype),
            pltpu.VMEM(partial.shape, partial.dtype),
            pltpu.VMEM(solved.shape, solved.dtype),
            pltpu.SemaphoreType.DMA((2 + 3 * blocks,)),
        ],
        cost_estimate=pl.CostEstimate(
            flops=2 * blocks * rows * width * width,
            bytes_accessed=blocks * (rows * width * 10 + width * width * 2) + 4 * solved.size,
            transcendentals=0,
        ),
    )(cols, piece, valc, partial, solved)


def local(
    resid,
    direction,
    diag_blocks,
    lower_blocks,
    upper_blocks,
    inv_pivots,
    down_coupling,
    valley_coupling,
    coupled_column,
):
    va, dc, nr, bs = resid.shape[1:]
    blocks = va * dc
    chunk_shape = (blocks * ROW_SPLIT, nr // ROW_SPLIT, bs)
    flat = (blocks, bs, bs)
    solved, partial = sweep(
        resid[0].reshape(chunk_shape),
        direction[0].reshape(blocks, nr, bs),
        diag_blocks[0].reshape(flat),
        lower_blocks[0].reshape(flat),
        upper_blocks[0].reshape(flat),
        inv_pivots[0].reshape(flat),
        down_coupling[0].reshape(flat),
        dc,
    )

    current = direction[0]
    piece = lax.all_gather(current, "valley", axis=0, tiled=True)
    image, solved = add_partner(
        coupled_column,
        piece.reshape((-1, nr, bs)),
        valley_coupling[0].reshape(flat),
        partial,
        solved,
        dc,
    )
    return (solved.reshape(resid.shape), image.reshape(resid.shape))


def solution(mesh):
    spec = P("elev", "valley", "down", None, None)
    in_specs = (spec,) * 8 + (P("elev", "valley", "down"),)
    out_specs = (spec, spec)
    return jax.shard_map(local, mesh=mesh, in_specs=in_specs, out_specs=out_specs, check_vma=False)
```

```python
import functools

import jax
import jax.numpy as jnp
from jax import lax
from jax.experimental import pallas as pl
from jax.experimental.pallas import tpu as pltpu
from jax.sharding import PartitionSpec as P

MESH = pl.DeviceIdType.MESH
ROW_SPLIT = 2


def apply_blocks(vectors, blocks):
    return jnp.einsum("bqrs,bqst->bqrt", vectors, blocks, preferred_element_type=jnp.float32)


def sweep_kernel(
    resid_hbm,
    dir_hbm,
    diag_hbm,
    lower_hbm,
    upper_hbm,
    pivot_hbm,
    downc_hbm,
    out_ref,
    img_ref,
    fronts,
    fwd_buf,
    bwd_buf,
    below_buf,
    above_buf,
    rim_buf,
    fsend,
    frecv,
    bsend,
    brecv,
    hsend,
    hrecv,
    rsend,
    rrecv,
    resid_ref,
    dir_ref,
    diag_ref,
    lower_ref,
    upper_ref,
    pivot_ref,
    downc_ref,
    load_sems,
    *,
    n,
    nd,
    dc,
    per_block,
):
    f32 = jnp.float32
    bf16 = jnp.bfloat16
    loads = [
        pltpu.make_async_copy(src, dst, load_sems.at[i])
        for i, (src, dst) in enumerate(
            [
                (dir_hbm, dir_ref),
                (resid_hbm, resid_ref),
                (pivot_hbm, pivot_ref),
                (lower_hbm, lower_ref),
                (upper_hbm, upper_ref),
                (diag_hbm, diag_ref),
                (downc_hbm, downc_ref),
            ]
        )
    ]
    for load in loads:
        load.start()
    h = lax.axis_index("elev")
    v = lax.axis_index("valley")
    d = lax.axis_index("down")
    chunks = resid_ref.shape[0]
    blocks = dir_ref.shape[0]
    rims = rim_buf.shape[0]
    has_below = h > 0
    has_above = h < n - 1
    has_up = d > 0
    has_dn = d < nd - 1

    barrier = pltpu.get_barrier_semaphore()
    peers = [
        (has_below, (h - 1, v, d)),
        (has_above, (h + 1, v, d)),
        (has_up, (h, v, d - 1)),
        (has_dn, (h, v, d + 1)),
    ]
    count = 0
    for cond, peer in peers:
        count = count + cond.astype(jnp.int32)

        @pl.when(cond)
        def _():
            pl.semaphore_signal(barrier, 1, device_id=peer, device_id_type=MESH)

    pl.semaphore_wait(barrier, count)

    def fwd_copy(g):
        return pltpu.make_async_remote_copy(
            src_ref=fronts.at[g],
            dst_ref=fwd_buf.at[g],
            send_sem=fsend.at[g],
            recv_sem=frecv.at[g],
            device_id=(h + 1, v, d),
            device_id_type=MESH,
        )

    def bwd_copy(g, src):
        return pltpu.make_async_remote_copy(
            src_ref=src.at[g],
            dst_ref=bwd_buf.at[g],
            send_sem=bsend.at[g],
            recv_sem=brecv.at[g],
            device_id=(h - 1, v, d),
            device_id_type=MESH,
        )

    def halo_down():
        return pltpu.make_async_remote_copy(
            src_ref=dir_ref,
            dst_ref=above_buf,
            send_sem=hsend.at[0],
            recv_sem=hrecv.at[0],
            device_id=(h - 1, v, d),
            device_id_type=MESH,
        )

    def halo_up():
        return pltpu.make_async_remote_copy(
            src_ref=dir_ref,
            dst_ref=below_buf,
            send_sem=hsend.at[1],
            recv_sem=hrecv.at[1],
            device_id=(h + 1, v, d),
            device_id_type=MESH,
        )

    def rim_copy(a):
        return pltpu.make_async_remote_copy(
            src_ref=dir_ref.at[a * dc + dc - 1],
            dst_ref=rim_buf.at[a],
            send_sem=rsend.at[a],
            recv_sem=rrecv.at[a],
            device_id=(h, v, d + 1),
            device_id_type=MESH,
        )

    @pl.when(jnp.logical_not(has_below))
    def _():
        below_buf[...] = jnp.zeros(below_buf.shape, bf16)

    @pl.when(jnp.logical_not(has_above))
    def _():
        above_buf[...] = jnp.zeros(above_buf.shape, bf16)

    @pl.when(jnp.logical_not(has_up))
    def _():
        rim_buf[...] = jnp.zeros(rim_buf.shape, bf16)

    def fwd_body(g, carry):
        blk = g // per_block

        @pl.when(has_below)
        def _():
            fwd_copy(g).wait_recv()
            inner = resid_ref[g].astype(f32) - jnp.dot(
                fwd_buf[g], lower_ref[blk], preferred_element_type=f32
            )
            fronts[g] = jnp.dot(
                inner.astype(bf16), pivot_ref[blk], preferred_element_type=f32
            ).astype(bf16)

        @pl.when(jnp.logical_not(has_below))
        def _():
            fronts[g] = jnp.dot(resid_ref[g], pivot_ref[blk], preferred_element_type=f32).astype(
                bf16
            )

        @pl.when(has_above)
        def _():
            fwd_copy(g).start()

        @pl.when(jnp.logical_not(has_above))
        def _():
            out_ref[g] = fronts[g]

        @pl.when(jnp.logical_and(jnp.logical_not(has_above), has_below))
        def _():
            bwd_copy(g, fronts).start()

        return carry

    loads[0].wait()
    send_early = h >= n // 2

    def send_halos(when):
        @pl.when(jnp.logical_and(has_below, when))
        def _():
            halo_down().start()

        @pl.when(jnp.logical_and(has_dn, when))
        def _():
            for a in range(rims):
                rim_copy(a).start()

    send_halos(send_early)

    for load in loads[1:4]:
        load.wait()

    lax.fori_loop(0, chunks, fwd_body, 0)

    for load in loads[4:]:
        load.wait()

    send_halos(jnp.logical_not(send_early))

    @pl.when(has_above)
    def _():
        halo_up().start()

    def image_body(b, carry):
        a = b // dc
        c = b % dc
        acc = jnp.dot(dir_ref[b], diag_ref[b], preferred_element_type=f32)
        acc = acc + jnp.dot(below_buf[b], lower_ref[b], preferred_element_type=f32)
        acc = acc + jnp.dot(above_buf[b], upper_ref[b], preferred_element_type=f32)
        upstream = jnp.where(c == 0, rim_buf[a], dir_ref[jnp.maximum(b - 1, 0)])
        img_ref[b] = acc + jnp.dot(upstream, downc_ref[b], preferred_element_type=f32)
        return carry

    def image():
        @pl.when(has_below)
        def _():
            halo_up().wait_recv()

        @pl.when(has_above)
        def _():
            halo_down().wait_recv()

        @pl.when(has_up)
        def _():
            for a in range(rims):
                rim_copy(a).wait_recv()

        lax.fori_loop(0, blocks, image_body, 0)

    early = h < n // 2

    @pl.when(early)
    def _():
        image()

    def bwd_body(g, carry):
        blk = g // per_block

        @pl.when(has_above)
        def _():
            bwd_copy(g, out_ref).wait_recv()
            carried = jnp.dot(bwd_buf[g], upper_ref[blk], preferred_element_type=f32).astype(bf16)
            out_ref[g] = (
                fronts[g].astype(f32) - jnp.dot(carried, pivot_ref[blk], preferred_element_type=f32)
            ).astype(bf16)

            @pl.when(has_below)
            def _():
                bwd_copy(g, out_ref).start()

        return carry

    lax.fori_loop(0, chunks, bwd_body, 0)

    @pl.when(jnp.logical_not(early))
    def _():
        image()

    def drain(g, carry):
        @pl.when(has_above)
        def _():
            fwd_copy(g).wait_send()

        @pl.when(has_below)
        def _():
            bwd_copy(g, out_ref).wait_send()

        return carry

    lax.fori_loop(0, chunks, drain, 0)

    @pl.when(has_below)
    def _():
        halo_down().wait_send()

    @pl.when(has_above)
    def _():
        halo_up().wait_send()

    @pl.when(has_dn)
    def _():
        for a in range(rims):
            rim_copy(a).wait_send()


def sweep(resid_l, dir_l, diag_l, lower_l, upper_l, pivot_l, downc_l, dc):
    n = lax.axis_size("elev")
    nd = lax.axis_size("down")
    chunks, rows, width = resid_l.shape
    blocks = lower_l.shape[0]
    per_block = chunks // blocks
    vmem = pl.BlockSpec(memory_space=pltpu.VMEM)
    flops = 2 * (2 * chunks * rows + 4 * dir_l.shape[0] * dir_l.shape[1]) * width * width
    weight_bytes = 6 * lower_l.size * lower_l.dtype.itemsize
    return pl.pallas_call(
        functools.partial(sweep_kernel, n=n, nd=nd, dc=dc, per_block=per_block),
        out_shape=(
            jax.ShapeDtypeStruct(resid_l.shape, resid_l.dtype),
            jax.ShapeDtypeStruct(dir_l.shape, jnp.float32),
        ),
        in_specs=[pl.BlockSpec(memory_space=pl.ANY)] * 7,
        out_specs=(vmem, vmem),
        scratch_shapes=[
            pltpu.VMEM(resid_l.shape, resid_l.dtype),
            pltpu.VMEM(resid_l.shape, resid_l.dtype),
            pltpu.VMEM(resid_l.shape, resid_l.dtype),
            pltpu.VMEM(dir_l.shape, dir_l.dtype),
            pltpu.VMEM(dir_l.shape, dir_l.dtype),
            pltpu.VMEM((blocks // dc,) + dir_l.shape[1:], dir_l.dtype),
            pltpu.SemaphoreType.DMA((chunks,)),
            pltpu.SemaphoreType.DMA((chunks,)),
            pltpu.SemaphoreType.DMA((chunks,)),
            pltpu.SemaphoreType.DMA((chunks,)),
            pltpu.SemaphoreType.DMA((2,)),
            pltpu.SemaphoreType.DMA((2,)),
            pltpu.SemaphoreType.DMA((blocks // dc,)),
            pltpu.SemaphoreType.DMA((blocks // dc,)),
            pltpu.VMEM(resid_l.shape, resid_l.dtype),
            pltpu.VMEM(dir_l.shape, dir_l.dtype),
            pltpu.VMEM(diag_l.shape, diag_l.dtype),
            pltpu.VMEM(lower_l.shape, lower_l.dtype),
            pltpu.VMEM(upper_l.shape, upper_l.dtype),
            pltpu.VMEM(pivot_l.shape, pivot_l.dtype),
            pltpu.VMEM(downc_l.shape, downc_l.dtype),
            pltpu.SemaphoreType.DMA((7,)),
        ],
        compiler_params=pltpu.CompilerParams(collective_id=0, has_side_effects=True),
        cost_estimate=pl.CostEstimate(
            flops=flops, bytes_accessed=weight_bytes + 6 * resid_l.size * 2, transcendentals=0
        ),
    )(resid_l, dir_l, diag_l, lower_l, upper_l, pivot_l, downc_l)


def partner_kernel(
    col_ref, piece_ref, valc_ref, partial_ref, solved_ref, out_ref, solved_out,
    held, vbuf, pbuf, sbuf, sems, *, dc
):
    blocks = held.shape[0]
    solved_in = pltpu.make_async_copy(solved_ref, sbuf, sems.at[0])
    solved_in.start()
    copies = []
    for b in range(blocks):
        col = col_ref[0, b // dc, b % dc]
        trio = (
            pltpu.make_async_copy(piece_ref.at[col * dc + b % dc], held.at[b], sems.at[1 + 3 * b]),
            pltpu.make_async_copy(valc_ref.at[b], vbuf.at[b], sems.at[2 + 3 * b]),
            pltpu.make_async_copy(partial_ref.at[b], pbuf.at[b], sems.at[3 + 3 * b]),
        )
        for copy in trio:
            copy.start()
        copies.append(trio)
    solved_in.wait()
    solved_back = pltpu.make_async_copy(sbuf, solved_out, sems.at[1 + 3 * blocks])
    solved_back.start()
    for b in range(blocks):
        for copy in copies[b]:
            copy.wait()
        out_ref[b] = pbuf[b] + jnp.dot(held[b], vbuf[b], preferred_element_type=jnp.float32)
    solved_back.wait()


def add_partner(cols, piece, valc, partial, solved, dc):
    blocks, rows, width = partial.shape
    hbm = pl.BlockSpec(memory_space=pl.ANY)
    return pl.pallas_call(
        functools.partial(partner_kernel, dc=dc),
        out_shape=(
            jax.ShapeDtypeStruct(partial.shape, partial.dtype),
            jax.ShapeDtypeStruct(solved.shape, solved.dtype),
        ),
        in_specs=[pl.BlockSpec(memory_space=pltpu.SMEM), hbm, hbm, hbm, hbm],
        out_specs=(pl.BlockSpec(memory_space=pltpu.VMEM), hbm),
        scratch_shapes=[
            pltpu.VMEM((blocks, rows, width), piece.dtype),
            pltpu.VMEM(valc.shape, valc.dtype),
            pltpu.VMEM(partial.shape, partial.dtype),
            pltpu.VMEM(solved.shape, solved.dtype),
            pltpu.SemaphoreType.DMA((2 + 3 * blocks,)),
        ],
        cost_estimate=pl.CostEstimate(
            flops=2 * blocks * rows * width * width,
            bytes_accessed=blocks * (rows * width * 10 + width * width * 2) + 4 * solved.size,
            transcendentals=0,
        ),
    )(cols, piece, valc, partial, solved)


def local(
    resid,
    direction,
    diag_blocks,
    lower_blocks,
    upper_blocks,
    inv_pivots,
    down_coupling,
    valley_coupling,
    coupled_column,
):
    va, dc, nr, bs = resid.shape[1:]
    blocks = va * dc
    chunk_shape = (blocks * ROW_SPLIT, nr // ROW_SPLIT, bs)
    flat = (blocks, bs, bs)
    solved, partial = sweep(
        resid[0].reshape(chunk_shape),
        direction[0].reshape(blocks, nr, bs),
        diag_blocks[0].reshape(flat),
        lower_blocks[0].reshape(flat),
        upper_blocks[0].reshape(flat),
        inv_pivots[0].reshape(flat),
        down_coupling[0].reshape(flat),
        dc,
    )

    current = direction[0]
    piece = lax.all_gather(current, "valley", axis=0, tiled=True)
    image, solved = add_partner(
        coupled_column,
        piece.reshape((-1, nr, bs)),
        valley_coupling[0].reshape(flat),
        partial,
        solved,
        dc,
    )
    return (solved.reshape(resid.shape), image.reshape(resid.shape))


def solution(mesh):
    spec = P("elev", "valley", "down", None, None)
    in_specs = (spec,) * 8 + (P("elev", "valley", "down"),)
    out_specs = (spec, spec)
    return jax.shard_map(local, mesh=mesh, in_specs=in_specs, out_specs=out_specs, check_vma=False)
```

```python
import functools

import jax
import jax.numpy as jnp
from jax import lax
from jax.experimental import pallas as pl
from jax.experimental.pallas import tpu as pltpu
from jax.sharding import PartitionSpec as P

MESH = pl.DeviceIdType.MESH
ROW_SPLIT = 2


def apply_blocks(vectors, blocks):
    return jnp.einsum("bqrs,bqst->bqrt", vectors, blocks, preferred_element_type=jnp.float32)


def sweep_kernel(
    resid_hbm,
    dir_hbm,
    diag_hbm,
    lower_hbm,
    upper_hbm,
    pivot_hbm,
    downc_hbm,
    out_ref,
    img_ref,
    fronts,
    fwd_buf,
    bwd_buf,
    below_buf,
    above_buf,
    rim_buf,
    fsend,
    frecv,
    bsend,
    brecv,
    hsend,
    hrecv,
    rsend,
    rrecv,
    resid_ref,
    dir_ref,
    diag_ref,
    lower_ref,
    upper_ref,
    pivot_ref,
    downc_ref,
    load_sems,
    *,
    n,
    nd,
    dc,
    per_block,
):
    f32 = jnp.float32
    bf16 = jnp.bfloat16
    loads = [
        pltpu.make_async_copy(src, dst, load_sems.at[i])
        for i, (src, dst) in enumerate(
            [
                (dir_hbm, dir_ref),
                (resid_hbm, resid_ref),
                (pivot_hbm, pivot_ref),
                (lower_hbm, lower_ref),
                (upper_hbm, upper_ref),
                (diag_hbm, diag_ref),
                (downc_hbm, downc_ref),
            ]
        )
    ]
    for load in loads:
        load.start()
    h = lax.axis_index("elev")
    v = lax.axis_index("valley")
    d = lax.axis_index("down")
    chunks = resid_ref.shape[0]
    blocks = dir_ref.shape[0]
    rims = rim_buf.shape[0]
    has_below = h > 0
    has_above = h < n - 1
    has_up = d > 0
    has_dn = d < nd - 1

    barrier = pltpu.get_barrier_semaphore()
    peers = [
        (has_below, (h - 1, v, d)),
        (has_above, (h + 1, v, d)),
        (has_up, (h, v, d - 1)),
        (has_dn, (h, v, d + 1)),
    ]
    count = 0
    for cond, peer in peers:
        count = count + cond.astype(jnp.int32)

        @pl.when(cond)
        def _():
            pl.semaphore_signal(barrier, 1, device_id=peer, device_id_type=MESH)

    pl.semaphore_wait(barrier, count)

    def fwd_copy(g):
        return pltpu.make_async_remote_copy(
            src_ref=fronts.at[g],
            dst_ref=fwd_buf.at[g],
            send_sem=fsend.at[g],
            recv_sem=frecv.at[g],
            device_id=(h + 1, v, d),
            device_id_type=MESH,
        )

    def bwd_copy(g, src):
        return pltpu.make_async_remote_copy(
            src_ref=src.at[g],
            dst_ref=bwd_buf.at[g],
            send_sem=bsend.at[g],
            recv_sem=brecv.at[g],
            device_id=(h - 1, v, d),
            device_id_type=MESH,
        )

    def halo_down():
        return pltpu.make_async_remote_copy(
            src_ref=dir_ref,
            dst_ref=above_buf,
            send_sem=hsend.at[0],
            recv_sem=hrecv.at[0],
            device_id=(h - 1, v, d),
            device_id_type=MESH,
        )

    def halo_up():
        return pltpu.make_async_remote_copy(
            src_ref=dir_ref,
            dst_ref=below_buf,
            send_sem=hsend.at[1],
            recv_sem=hrecv.at[1],
            device_id=(h + 1, v, d),
            device_id_type=MESH,
        )

    def rim_copy(a):
        return pltpu.make_async_remote_copy(
            src_ref=dir_ref.at[a * dc + dc - 1],
            dst_ref=rim_buf.at[a],
            send_sem=rsend.at[a],
            recv_sem=rrecv.at[a],
            device_id=(h, v, d + 1),
            device_id_type=MESH,
        )

    @pl.when(jnp.logical_not(has_below))
    def _():
        below_buf[...] = jnp.zeros(below_buf.shape, bf16)

    @pl.when(jnp.logical_not(has_above))
    def _():
        above_buf[...] = jnp.zeros(above_buf.shape, bf16)

    @pl.when(jnp.logical_not(has_up))
    def _():
        rim_buf[...] = jnp.zeros(rim_buf.shape, bf16)

    def fwd_body(g, carry):
        blk = g // per_block

        @pl.when(has_below)
        def _():
            fwd_copy(g).wait_recv()
            inner = resid_ref[g].astype(f32) - jnp.dot(
                fwd_buf[g], lower_ref[blk], preferred_element_type=f32
            )
            fronts[g] = jnp.dot(
                inner.astype(bf16), pivot_ref[blk], preferred_element_type=f32
            ).astype(bf16)

        @pl.when(jnp.logical_not(has_below))
        def _():
            fronts[g] = jnp.dot(resid_ref[g], pivot_ref[blk], preferred_element_type=f32).astype(
                bf16
            )

        @pl.when(has_above)
        def _():
            fwd_copy(g).start()

        @pl.when(jnp.logical_not(has_above))
        def _():
            out_ref[g] = fronts[g]

        @pl.when(jnp.logical_and(jnp.logical_not(has_above), has_below))
        def _():
            bwd_copy(g, fronts).start()

        return carry

    loads[0].wait()
    send_early = h >= n // 2

    def send_halos(when):
        @pl.when(jnp.logical_and(has_below, when))
        def _():
            halo_down().start()

        @pl.when(jnp.logical_and(has_dn, when))
        def _():
            for a in range(rims):
                rim_copy(a).start()

    send_halos(send_early)
    up_early = h >= n // 4

    @pl.when(jnp.logical_and(has_above, up_early))
    def _():
        halo_up().start()

    for load in loads[1:4]:
        load.wait()

    lax.fori_loop(0, chunks, fwd_body, 0)

    for load in loads[4:]:
        load.wait()

    send_halos(jnp.logical_not(send_early))

    @pl.when(jnp.logical_and(has_above, jnp.logical_not(up_early)))
    def _():
        halo_up().start()

    def image_body(b, carry):
        a = b // dc
        c = b % dc
        acc = jnp.dot(dir_ref[b], diag_ref[b], preferred_element_type=f32)
        acc = acc + jnp.dot(below_buf[b], lower_ref[b], preferred_element_type=f32)
        acc = acc + jnp.dot(above_buf[b], upper_ref[b], preferred_element_type=f32)
        upstream = jnp.where(c == 0, rim_buf[a], dir_ref[jnp.maximum(b - 1, 0)])
        img_ref[b] = acc + jnp.dot(upstream, downc_ref[b], preferred_element_type=f32)
        return carry

    def image():
        @pl.when(has_below)
        def _():
            halo_up().wait_recv()

        @pl.when(has_above)
        def _():
            halo_down().wait_recv()

        @pl.when(has_up)
        def _():
            for a in range(rims):
                rim_copy(a).wait_recv()

        lax.fori_loop(0, blocks, image_body, 0)

    early = h < n // 2

    @pl.when(early)
    def _():
        image()

    def bwd_body(g, carry):
        blk = g // per_block

        @pl.when(has_above)
        def _():
            bwd_copy(g, out_ref).wait_recv()
            carried = jnp.dot(bwd_buf[g], upper_ref[blk], preferred_element_type=f32).astype(bf16)
            out_ref[g] = (
                fronts[g].astype(f32) - jnp.dot(carried, pivot_ref[blk], preferred_element_type=f32)
            ).astype(bf16)

            @pl.when(has_below)
            def _():
                bwd_copy(g, out_ref).start()

        return carry

    lax.fori_loop(0, chunks, bwd_body, 0)

    @pl.when(jnp.logical_not(early))
    def _():
        image()

    def drain(g, carry):
        @pl.when(has_above)
        def _():
            fwd_copy(g).wait_send()

        @pl.when(has_below)
        def _():
            bwd_copy(g, out_ref).wait_send()

        return carry

    lax.fori_loop(0, chunks, drain, 0)

    @pl.when(has_below)
    def _():
        halo_down().wait_send()

    @pl.when(has_above)
    def _():
        halo_up().wait_send()

    @pl.when(has_dn)
    def _():
        for a in range(rims):
            rim_copy(a).wait_send()


def sweep(resid_l, dir_l, diag_l, lower_l, upper_l, pivot_l, downc_l, dc):
    n = lax.axis_size("elev")
    nd = lax.axis_size("down")
    chunks, rows, width = resid_l.shape
    blocks = lower_l.shape[0]
    per_block = chunks // blocks
    vmem = pl.BlockSpec(memory_space=pltpu.VMEM)
    flops = 2 * (2 * chunks * rows + 4 * dir_l.shape[0] * dir_l.shape[1]) * width * width
    weight_bytes = 6 * lower_l.size * lower_l.dtype.itemsize
    return pl.pallas_call(
        functools.partial(sweep_kernel, n=n, nd=nd, dc=dc, per_block=per_block),
        out_shape=(
            jax.ShapeDtypeStruct(resid_l.shape, resid_l.dtype),
            jax.ShapeDtypeStruct(dir_l.shape, jnp.float32),
        ),
        in_specs=[pl.BlockSpec(memory_space=pl.ANY)] * 7,
        out_specs=(vmem, vmem),
        scratch_shapes=[
            pltpu.VMEM(resid_l.shape, resid_l.dtype),
            pltpu.VMEM(resid_l.shape, resid_l.dtype),
            pltpu.VMEM(resid_l.shape, resid_l.dtype),
            pltpu.VMEM(dir_l.shape, dir_l.dtype),
            pltpu.VMEM(dir_l.shape, dir_l.dtype),
            pltpu.VMEM((blocks // dc,) + dir_l.shape[1:], dir_l.dtype),
            pltpu.SemaphoreType.DMA((chunks,)),
            pltpu.SemaphoreType.DMA((chunks,)),
            pltpu.SemaphoreType.DMA((chunks,)),
            pltpu.SemaphoreType.DMA((chunks,)),
            pltpu.SemaphoreType.DMA((2,)),
            pltpu.SemaphoreType.DMA((2,)),
            pltpu.SemaphoreType.DMA((blocks // dc,)),
            pltpu.SemaphoreType.DMA((blocks // dc,)),
            pltpu.VMEM(resid_l.shape, resid_l.dtype),
            pltpu.VMEM(dir_l.shape, dir_l.dtype),
            pltpu.VMEM(diag_l.shape, diag_l.dtype),
            pltpu.VMEM(lower_l.shape, lower_l.dtype),
            pltpu.VMEM(upper_l.shape, upper_l.dtype),
            pltpu.VMEM(pivot_l.shape, pivot_l.dtype),
            pltpu.VMEM(downc_l.shape, downc_l.dtype),
            pltpu.SemaphoreType.DMA((7,)),
        ],
        compiler_params=pltpu.CompilerParams(collective_id=0, has_side_effects=True),
        cost_estimate=pl.CostEstimate(
            flops=flops, bytes_accessed=weight_bytes + 6 * resid_l.size * 2, transcendentals=0
        ),
    )(resid_l, dir_l, diag_l, lower_l, upper_l, pivot_l, downc_l)


def partner_kernel(
    col_ref, piece_ref, valc_ref, partial_ref, solved_ref, out_ref, solved_out,
    held, vbuf, pbuf, sbuf, sems, *, dc
):
    blocks = held.shape[0]
    solved_in = pltpu.make_async_copy(solved_ref, sbuf, sems.at[0])
    solved_in.start()
    copies = []
    for b in range(blocks):
        col = col_ref[0, b // dc, b % dc]
        trio = (
            pltpu.make_async_copy(piece_ref.at[col * dc + b % dc], held.at[b], sems.at[1 + 3 * b]),
            pltpu.make_async_copy(valc_ref.at[b], vbuf.at[b], sems.at[2 + 3 * b]),
            pltpu.make_async_copy(partial_ref.at[b], pbuf.at[b], sems.at[3 + 3 * b]),
        )
        for copy in trio:
            copy.start()
        copies.append(trio)
    solved_in.wait()
    solved_back = pltpu.make_async_copy(sbuf, solved_out, sems.at[1 + 3 * blocks])
    solved_back.start()
    for b in range(blocks):
        for copy in copies[b]:
            copy.wait()
        out_ref[b] = pbuf[b] + jnp.dot(held[b], vbuf[b], preferred_element_type=jnp.float32)
    solved_back.wait()


def add_partner(cols, piece, valc, partial, solved, dc):
    blocks, rows, width = partial.shape
    hbm = pl.BlockSpec(memory_space=pl.ANY)
    return pl.pallas_call(
        functools.partial(partner_kernel, dc=dc),
        out_shape=(
            jax.ShapeDtypeStruct(partial.shape, partial.dtype),
            jax.ShapeDtypeStruct(solved.shape, solved.dtype),
        ),
        in_specs=[pl.BlockSpec(memory_space=pltpu.SMEM), hbm, hbm, hbm, hbm],
        out_specs=(pl.BlockSpec(memory_space=pltpu.VMEM), hbm),
        scratch_shapes=[
            pltpu.VMEM((blocks, rows, width), piece.dtype),
            pltpu.VMEM(valc.shape, valc.dtype),
            pltpu.VMEM(partial.shape, partial.dtype),
            pltpu.VMEM(solved.shape, solved.dtype),
            pltpu.SemaphoreType.DMA((2 + 3 * blocks,)),
        ],
        cost_estimate=pl.CostEstimate(
            flops=2 * blocks * rows * width * width,
            bytes_accessed=blocks * (rows * width * 10 + width * width * 2) + 4 * solved.size,
            transcendentals=0,
        ),
    )(cols, piece, valc, partial, solved)


def local(
    resid,
    direction,
    diag_blocks,
    lower_blocks,
    upper_blocks,
    inv_pivots,
    down_coupling,
    valley_coupling,
    coupled_column,
):
    va, dc, nr, bs = resid.shape[1:]
    blocks = va * dc
    chunk_shape = (blocks * ROW_SPLIT, nr // ROW_SPLIT, bs)
    flat = (blocks, bs, bs)
    solved, partial = sweep(
        resid[0].reshape(chunk_shape),
        direction[0].reshape(blocks, nr, bs),
        diag_blocks[0].reshape(flat),
        lower_blocks[0].reshape(flat),
        upper_blocks[0].reshape(flat),
        inv_pivots[0].reshape(flat),
        down_coupling[0].reshape(flat),
        dc,
    )

    current = direction[0]
    piece = lax.all_gather(current, "valley", axis=0, tiled=True)
    image, solved = add_partner(
        coupled_column,
        piece.reshape((-1, nr, bs)),
        valley_coupling[0].reshape(flat),
        partial,
        solved,
        dc,
    )
    return (solved.reshape(resid.shape), image.reshape(resid.shape))


def solution(mesh):
    spec = P("elev", "valley", "down", None, None)
    in_specs = (spec,) * 8 + (P("elev", "valley", "down"),)
    out_specs = (spec, spec)
    return jax.shard_map(local, mesh=mesh, in_specs=in_specs, out_specs=out_specs, check_vma=False)
```

```python
import functools

import jax
import jax.numpy as jnp
from jax import lax
from jax.experimental import pallas as pl
from jax.experimental.pallas import tpu as pltpu
from jax.sharding import PartitionSpec as P

MESH = pl.DeviceIdType.MESH
ROW_SPLIT = 2


def apply_blocks(vectors, blocks):
    return jnp.einsum("bqrs,bqst->bqrt", vectors, blocks, preferred_element_type=jnp.float32)


def sweep_kernel(
    resid_hbm,
    dir_hbm,
    diag_hbm,
    lower_hbm,
    upper_hbm,
    pivot_hbm,
    downc_hbm,
    out_ref,
    img_ref,
    fronts,
    fwd_buf,
    bwd_buf,
    below_buf,
    above_buf,
    rim_buf,
    fsend,
    frecv,
    bsend,
    brecv,
    hsend,
    hrecv,
    rsend,
    rrecv,
    resid_ref,
    dir_ref,
    diag_ref,
    lower_ref,
    upper_ref,
    pivot_ref,
    downc_ref,
    load_sems,
    *,
    n,
    nd,
    dc,
    per_block,
):
    f32 = jnp.float32
    bf16 = jnp.bfloat16
    loads = [
        pltpu.make_async_copy(src, dst, load_sems.at[i])
        for i, (src, dst) in enumerate(
            [
                (dir_hbm, dir_ref),
                (resid_hbm, resid_ref),
                (pivot_hbm, pivot_ref),
                (lower_hbm, lower_ref),
                (upper_hbm, upper_ref),
                (diag_hbm, diag_ref),
                (downc_hbm, downc_ref),
            ]
        )
    ]
    for load in loads:
        load.start()
    h = lax.axis_index("elev")
    v = lax.axis_index("valley")
    d = lax.axis_index("down")
    chunks = resid_ref.shape[0]
    blocks = dir_ref.shape[0]
    rims = rim_buf.shape[0]
    has_below = h > 0
    has_above = h < n - 1
    has_up = d > 0
    has_dn = d < nd - 1

    barrier = pltpu.get_barrier_semaphore()
    peers = [
        (has_below, (h - 1, v, d)),
        (has_above, (h + 1, v, d)),
        (has_up, (h, v, d - 1)),
        (has_dn, (h, v, d + 1)),
    ]
    count = 0
    for cond, peer in peers:
        count = count + cond.astype(jnp.int32)

        @pl.when(cond)
        def _():
            pl.semaphore_signal(barrier, 1, device_id=peer, device_id_type=MESH)

    pl.semaphore_wait(barrier, count)

    def fwd_copy(g):
        return pltpu.make_async_remote_copy(
            src_ref=fronts.at[g],
            dst_ref=fwd_buf.at[g],
            send_sem=fsend.at[g],
            recv_sem=frecv.at[g],
            device_id=(h + 1, v, d),
            device_id_type=MESH,
        )

    def bwd_copy(g, src):
        return pltpu.make_async_remote_copy(
            src_ref=src.at[g],
            dst_ref=bwd_buf.at[g],
            send_sem=bsend.at[g],
            recv_sem=brecv.at[g],
            device_id=(h - 1, v, d),
            device_id_type=MESH,
        )

    def halo_down():
        return pltpu.make_async_remote_copy(
            src_ref=dir_ref,
            dst_ref=above_buf,
            send_sem=hsend.at[0],
            recv_sem=hrecv.at[0],
            device_id=(h - 1, v, d),
            device_id_type=MESH,
        )

    def halo_up():
        return pltpu.make_async_remote_copy(
            src_ref=dir_ref,
            dst_ref=below_buf,
            send_sem=hsend.at[1],
            recv_sem=hrecv.at[1],
            device_id=(h + 1, v, d),
            device_id_type=MESH,
        )

    def rim_copy(a):
        return pltpu.make_async_remote_copy(
            src_ref=dir_ref.at[a * dc + dc - 1],
            dst_ref=rim_buf.at[a],
            send_sem=rsend.at[a],
            recv_sem=rrecv.at[a],
            device_id=(h, v, d + 1),
            device_id_type=MESH,
        )

    @pl.when(jnp.logical_not(has_below))
    def _():
        below_buf[...] = jnp.zeros(below_buf.shape, bf16)

    @pl.when(jnp.logical_not(has_above))
    def _():
        above_buf[...] = jnp.zeros(above_buf.shape, bf16)

    @pl.when(jnp.logical_not(has_up))
    def _():
        rim_buf[...] = jnp.zeros(rim_buf.shape, bf16)

    def fwd_body(g, carry):
        blk = g // per_block

        @pl.when(has_below)
        def _():
            fwd_copy(g).wait_recv()
            inner = resid_ref[g].astype(f32) - jnp.dot(
                fwd_buf[g], lower_ref[blk], preferred_element_type=f32
            )
            fronts[g] = jnp.dot(
                inner.astype(bf16), pivot_ref[blk], preferred_element_type=f32
            ).astype(bf16)

        @pl.when(jnp.logical_not(has_below))
        def _():
            fronts[g] = jnp.dot(resid_ref[g], pivot_ref[blk], preferred_element_type=f32).astype(
                bf16
            )

        @pl.when(has_above)
        def _():
            fwd_copy(g).start()

        @pl.when(jnp.logical_not(has_above))
        def _():
            out_ref[g] = fronts[g]

        @pl.when(jnp.logical_and(jnp.logical_not(has_above), has_below))
        def _():
            bwd_copy(g, fronts).start()

        return carry

    loads[0].wait()
    send_early = h >= n // 2

    def send_halos(when):
        @pl.when(jnp.logical_and(has_below, when))
        def _():
            halo_down().start()

        @pl.when(jnp.logical_and(has_dn, when))
        def _():
            for a in range(rims):
                rim_copy(a).start()

    send_halos(send_early)

    for load in loads[1:4]:
        load.wait()

    lax.fori_loop(0, chunks, fwd_body, 0)

    for load in loads[4:]:
        load.wait()

    send_halos(jnp.logical_not(send_early))

    @pl.when(has_above)
    def _():
        halo_up().start()

    def image_body(b, carry):
        a = b // dc
        c = b % dc
        acc = jnp.dot(dir_ref[b], diag_ref[b], preferred_element_type=f32)
        acc = acc + jnp.dot(below_buf[b], lower_ref[b], preferred_element_type=f32)
        acc = acc + jnp.dot(above_buf[b], upper_ref[b], preferred_element_type=f32)
        upstream = jnp.where(c == 0, rim_buf[a], dir_ref[jnp.maximum(b - 1, 0)])
        img_ref[b] = acc + jnp.dot(upstream, downc_ref[b], preferred_element_type=f32)
        return carry

    def image():
        @pl.when(has_below)
        def _():
            halo_up().wait_recv()

        @pl.when(has_above)
        def _():
            halo_down().wait_recv()

        @pl.when(has_up)
        def _():
            for a in range(rims):
                rim_copy(a).wait_recv()

        lax.fori_loop(0, blocks, image_body, 0)

    early = h < n // 2

    @pl.when(early)
    def _():
        image()

    def bwd_body(g, carry):
        blk = g // per_block

        @pl.when(has_above)
        def _():
            bwd_copy(g, out_ref).wait_recv()
            carried = jnp.dot(bwd_buf[g], upper_ref[blk], preferred_element_type=f32).astype(bf16)
            out_ref[g] = (
                fronts[g].astype(f32) - jnp.dot(carried, pivot_ref[blk], preferred_element_type=f32)
            ).astype(bf16)

            @pl.when(has_below)
            def _():
                bwd_copy(g, out_ref).start()

        return carry

    lax.fori_loop(0, chunks, bwd_body, 0)

    @pl.when(jnp.logical_not(early))
    def _():
        image()

    def drain(g, carry):
        @pl.when(has_above)
        def _():
            fwd_copy(g).wait_send()

        @pl.when(has_below)
        def _():
            bwd_copy(g, out_ref).wait_send()

        return carry

    lax.fori_loop(0, chunks, drain, 0)

    @pl.when(has_below)
    def _():
        halo_down().wait_send()

    @pl.when(has_above)
    def _():
        halo_up().wait_send()

    @pl.when(has_dn)
    def _():
        for a in range(rims):
            rim_copy(a).wait_send()


def sweep(resid_l, dir_l, diag_l, lower_l, upper_l, pivot_l, downc_l, dc):
    n = lax.axis_size("elev")
    nd = lax.axis_size("down")
    chunks, rows, width = resid_l.shape
    blocks = lower_l.shape[0]
    per_block = chunks // blocks
    vmem = pl.BlockSpec(memory_space=pltpu.VMEM)
    flops = 2 * (2 * chunks * rows + 4 * dir_l.shape[0] * dir_l.shape[1]) * width * width
    weight_bytes = 6 * lower_l.size * lower_l.dtype.itemsize
    return pl.pallas_call(
        functools.partial(sweep_kernel, n=n, nd=nd, dc=dc, per_block=per_block),
        out_shape=(
            jax.ShapeDtypeStruct(resid_l.shape, resid_l.dtype),
            jax.ShapeDtypeStruct(dir_l.shape, jnp.float32),
        ),
        in_specs=[pl.BlockSpec(memory_space=pl.ANY)] * 7,
        out_specs=(vmem, vmem),
        scratch_shapes=[
            pltpu.VMEM(resid_l.shape, resid_l.dtype),
            pltpu.VMEM(resid_l.shape, resid_l.dtype),
            pltpu.VMEM(resid_l.shape, resid_l.dtype),
            pltpu.VMEM(dir_l.shape, dir_l.dtype),
            pltpu.VMEM(dir_l.shape, dir_l.dtype),
            pltpu.VMEM((blocks // dc,) + dir_l.shape[1:], dir_l.dtype),
            pltpu.SemaphoreType.DMA((chunks,)),
            pltpu.SemaphoreType.DMA((chunks,)),
            pltpu.SemaphoreType.DMA((chunks,)),
            pltpu.SemaphoreType.DMA((chunks,)),
            pltpu.SemaphoreType.DMA((2,)),
            pltpu.SemaphoreType.DMA((2,)),
            pltpu.SemaphoreType.DMA((blocks // dc,)),
            pltpu.SemaphoreType.DMA((blocks // dc,)),
            pltpu.VMEM(resid_l.shape, resid_l.dtype),
            pltpu.VMEM(dir_l.shape, dir_l.dtype),
            pltpu.VMEM(diag_l.shape, diag_l.dtype),
            pltpu.VMEM(lower_l.shape, lower_l.dtype),
            pltpu.VMEM(upper_l.shape, upper_l.dtype),
            pltpu.VMEM(pivot_l.shape, pivot_l.dtype),
            pltpu.VMEM(downc_l.shape, downc_l.dtype),
            pltpu.SemaphoreType.DMA((7,)),
        ],
        compiler_params=pltpu.CompilerParams(collective_id=0, has_side_effects=True),
        cost_estimate=pl.CostEstimate(
            flops=flops, bytes_accessed=weight_bytes + 6 * resid_l.size * 2, transcendentals=0
        ),
    )(resid_l, dir_l, diag_l, lower_l, upper_l, pivot_l, downc_l)


def partner_kernel(
    col_ref, piece_ref, valc_ref, partial_ref, solved_ref, out_ref, solved_out,
    held, vbuf, pbuf, sbuf, sems, *, dc
):
    blocks = held.shape[0]
    solved_in = pltpu.make_async_copy(solved_ref, sbuf, sems.at[0])
    copies = []
    for b in range(blocks):
        col = col_ref[0, b // dc, b % dc]
        trio = (
            pltpu.make_async_copy(piece_ref.at[col * dc + b % dc], held.at[b], sems.at[1 + 3 * b]),
            pltpu.make_async_copy(valc_ref.at[b], vbuf.at[b], sems.at[2 + 3 * b]),
            pltpu.make_async_copy(partial_ref.at[b], pbuf.at[b], sems.at[3 + 3 * b]),
        )
        for copy in trio:
            copy.start()
        copies.append(trio)
    solved_in.start()
    for b in range(blocks):
        for copy in copies[b]:
            copy.wait()
        out_ref[b] = pbuf[b] + jnp.dot(held[b], vbuf[b], preferred_element_type=jnp.float32)
    solved_in.wait()
    solved_back = pltpu.make_async_copy(sbuf, solved_out, sems.at[1 + 3 * blocks])
    solved_back.start()
    solved_back.wait()


def add_partner(cols, piece, valc, partial, solved, dc):
    blocks, rows, width = partial.shape
    hbm = pl.BlockSpec(memory_space=pl.ANY)
    return pl.pallas_call(
        functools.partial(partner_kernel, dc=dc),
        out_shape=(
            jax.ShapeDtypeStruct(partial.shape, partial.dtype),
            jax.ShapeDtypeStruct(solved.shape, solved.dtype),
        ),
        in_specs=[pl.BlockSpec(memory_space=pltpu.SMEM), hbm, hbm, hbm, hbm],
        out_specs=(pl.BlockSpec(memory_space=pltpu.VMEM), hbm),
        scratch_shapes=[
            pltpu.VMEM((blocks, rows, width), piece.dtype),
            pltpu.VMEM(valc.shape, valc.dtype),
            pltpu.VMEM(partial.shape, partial.dtype),
            pltpu.VMEM(solved.shape, solved.dtype),
            pltpu.SemaphoreType.DMA((2 + 3 * blocks,)),
        ],
        cost_estimate=pl.CostEstimate(
            flops=2 * blocks * rows * width * width,
            bytes_accessed=blocks * (rows * width * 10 + width * width * 2) + 4 * solved.size,
            transcendentals=0,
        ),
    )(cols, piece, valc, partial, solved)


def local(
    resid,
    direction,
    diag_blocks,
    lower_blocks,
    upper_blocks,
    inv_pivots,
    down_coupling,
    valley_coupling,
    coupled_column,
):
    va, dc, nr, bs = resid.shape[1:]
    blocks = va * dc
    chunk_shape = (blocks * ROW_SPLIT, nr // ROW_SPLIT, bs)
    flat = (blocks, bs, bs)
    solved, partial = sweep(
        resid[0].reshape(chunk_shape),
        direction[0].reshape(blocks, nr, bs),
        diag_blocks[0].reshape(flat),
        lower_blocks[0].reshape(flat),
        upper_blocks[0].reshape(flat),
        inv_pivots[0].reshape(flat),
        down_coupling[0].reshape(flat),
        dc,
    )

    current = direction[0]
    piece = lax.all_gather(current, "valley", axis=0, tiled=True)
    image, solved = add_partner(
        coupled_column,
        piece.reshape((-1, nr, bs)),
        valley_coupling[0].reshape(flat),
        partial,
        solved,
        dc,
    )
    return (solved.reshape(resid.shape), image.reshape(resid.shape))


def solution(mesh):
    spec = P("elev", "valley", "down", None, None)
    in_specs = (spec,) * 8 + (P("elev", "valley", "down"),)
    out_specs = (spec, spec)
    return jax.shard_map(local, mesh=mesh, in_specs=in_specs, out_specs=out_specs, check_vma=False)
```

```python
import functools

import jax
import jax.numpy as jnp
from jax import lax
from jax.experimental import pallas as pl
from jax.experimental.pallas import tpu as pltpu
from jax.sharding import PartitionSpec as P

MESH = pl.DeviceIdType.MESH
ROW_SPLIT = 2


def apply_blocks(vectors, blocks):
    return jnp.einsum("bqrs,bqst->bqrt", vectors, blocks, preferred_element_type=jnp.float32)


def sweep_kernel(
    resid_hbm,
    dir_hbm,
    diag_hbm,
    lower_hbm,
    upper_hbm,
    pivot_hbm,
    downc_hbm,
    out_ref,
    img_ref,
    fronts,
    fwd_buf,
    bwd_buf,
    below_buf,
    above_buf,
    rim_buf,
    fsend,
    frecv,
    bsend,
    brecv,
    hsend,
    hrecv,
    rsend,
    rrecv,
    resid_ref,
    dir_ref,
    diag_ref,
    lower_ref,
    upper_ref,
    pivot_ref,
    downc_ref,
    load_sems,
    *,
    n,
    nd,
    dc,
    per_block,
):
    f32 = jnp.float32
    bf16 = jnp.bfloat16
    loads = [
        pltpu.make_async_copy(src, dst, load_sems.at[i])
        for i, (src, dst) in enumerate(
            [
                (resid_hbm, resid_ref),
                (pivot_hbm, pivot_ref),
                (lower_hbm, lower_ref),
                (dir_hbm, dir_ref),
                (upper_hbm, upper_ref),
                (diag_hbm, diag_ref),
                (downc_hbm, downc_ref),
            ]
        )
    ]
    for load in loads:
        load.start()
    h = lax.axis_index("elev")
    v = lax.axis_index("valley")
    d = lax.axis_index("down")
    chunks = resid_ref.shape[0]
    blocks = dir_ref.shape[0]
    rims = rim_buf.shape[0]
    has_below = h > 0
    has_above = h < n - 1
    has_up = d > 0
    has_dn = d < nd - 1

    barrier = pltpu.get_barrier_semaphore()
    peers = [
        (has_below, (h - 1, v, d)),
        (has_above, (h + 1, v, d)),
        (has_up, (h, v, d - 1)),
        (has_dn, (h, v, d + 1)),
    ]
    count = 0
    for cond, peer in peers:
        count = count + cond.astype(jnp.int32)

        @pl.when(cond)
        def _():
            pl.semaphore_signal(barrier, 1, device_id=peer, device_id_type=MESH)

    pl.semaphore_wait(barrier, count)

    def fwd_copy(g):
        return pltpu.make_async_remote_copy(
            src_ref=fronts.at[g],
            dst_ref=fwd_buf.at[g],
            send_sem=fsend.at[g],
            recv_sem=frecv.at[g],
            device_id=(h + 1, v, d),
            device_id_type=MESH,
        )

    def bwd_copy(g, src):
        return pltpu.make_async_remote_copy(
            src_ref=src.at[g],
            dst_ref=bwd_buf.at[g],
            send_sem=bsend.at[g],
            recv_sem=brecv.at[g],
            device_id=(h - 1, v, d),
            device_id_type=MESH,
        )

    def halo_down():
        return pltpu.make_async_remote_copy(
            src_ref=dir_ref,
            dst_ref=above_buf,
            send_sem=hsend.at[0],
            recv_sem=hrecv.at[0],
            device_id=(h - 1, v, d),
            device_id_type=MESH,
        )

    def halo_up():
        return pltpu.make_async_remote_copy(
            src_ref=dir_ref,
            dst_ref=below_buf,
            send_sem=hsend.at[1],
            recv_sem=hrecv.at[1],
            device_id=(h + 1, v, d),
            device_id_type=MESH,
        )

    def rim_copy(a):
        return pltpu.make_async_remote_copy(
            src_ref=dir_ref.at[a * dc + dc - 1],
            dst_ref=rim_buf.at[a],
            send_sem=rsend.at[a],
            recv_sem=rrecv.at[a],
            device_id=(h, v, d + 1),
            device_id_type=MESH,
        )

    @pl.when(jnp.logical_not(has_below))
    def _():
        below_buf[...] = jnp.zeros(below_buf.shape, bf16)

    @pl.when(jnp.logical_not(has_above))
    def _():
        above_buf[...] = jnp.zeros(above_buf.shape, bf16)

    @pl.when(jnp.logical_not(has_up))
    def _():
        rim_buf[...] = jnp.zeros(rim_buf.shape, bf16)

    def fwd_body(g, carry):
        blk = g // per_block

        @pl.when(has_below)
        def _():
            fwd_copy(g).wait_recv()
            inner = resid_ref[g].astype(f32) - jnp.dot(
                fwd_buf[g], lower_ref[blk], preferred_element_type=f32
            )
            fronts[g] = jnp.dot(
                inner.astype(bf16), pivot_ref[blk], preferred_element_type=f32
            ).astype(bf16)

        @pl.when(jnp.logical_not(has_below))
        def _():
            fronts[g] = jnp.dot(resid_ref[g], pivot_ref[blk], preferred_element_type=f32).astype(
                bf16
            )

        @pl.when(has_above)
        def _():
            fwd_copy(g).start()

        @pl.when(jnp.logical_not(has_above))
        def _():
            out_ref[g] = fronts[g]

        @pl.when(jnp.logical_and(jnp.logical_not(has_above), has_below))
        def _():
            bwd_copy(g, fronts).start()

        return carry

    loads[0].wait()
    loads[1].wait()
    send_early = h >= n // 2

    @pl.when(send_early)
    def _():
        loads[3].wait()

    def send_halos(when):
        @pl.when(jnp.logical_and(has_below, when))
        def _():
            halo_down().start()

        @pl.when(jnp.logical_and(has_dn, when))
        def _():
            for a in range(rims):
                rim_copy(a).start()

    send_halos(send_early)

    @pl.when(has_below)
    def _():
        loads[2].wait()

    lax.fori_loop(0, chunks, fwd_body, 0)

    @pl.when(jnp.logical_not(has_below))
    def _():
        loads[2].wait()

    @pl.when(jnp.logical_not(send_early))
    def _():
        loads[3].wait()

    for load in loads[4:]:
        load.wait()

    send_halos(jnp.logical_not(send_early))

    @pl.when(has_above)
    def _():
        halo_up().start()

    def image_body(b, carry):
        a = b // dc
        c = b % dc
        acc = jnp.dot(dir_ref[b], diag_ref[b], preferred_element_type=f32)
        acc = acc + jnp.dot(below_buf[b], lower_ref[b], preferred_element_type=f32)
        acc = acc + jnp.dot(above_buf[b], upper_ref[b], preferred_element_type=f32)
        upstream = jnp.where(c == 0, rim_buf[a], dir_ref[jnp.maximum(b - 1, 0)])
        img_ref[b] = acc + jnp.dot(upstream, downc_ref[b], preferred_element_type=f32)
        return carry

    def image():
        @pl.when(has_below)
        def _():
            halo_up().wait_recv()

        @pl.when(has_above)
        def _():
            halo_down().wait_recv()

        @pl.when(has_up)
        def _():
            for a in range(rims):
                rim_copy(a).wait_recv()

        lax.fori_loop(0, blocks, image_body, 0)

    early = h < n // 2

    @pl.when(early)
    def _():
        image()

    def bwd_body(g, carry):
        blk = g // per_block

        @pl.when(has_above)
        def _():
            bwd_copy(g, out_ref).wait_recv()
            carried = jnp.dot(bwd_buf[g], upper_ref[blk], preferred_element_type=f32).astype(bf16)
            out_ref[g] = (
                fronts[g].astype(f32) - jnp.dot(carried, pivot_ref[blk], preferred_element_type=f32)
            ).astype(bf16)

            @pl.when(has_below)
            def _():
                bwd_copy(g, out_ref).start()

        return carry

    lax.fori_loop(0, chunks, bwd_body, 0)

    @pl.when(jnp.logical_not(early))
    def _():
        image()

    def drain(g, carry):
        @pl.when(has_above)
        def _():
            fwd_copy(g).wait_send()

        @pl.when(has_below)
        def _():
            bwd_copy(g, out_ref).wait_send()

        return carry

    lax.fori_loop(0, chunks, drain, 0)

    @pl.when(has_below)
    def _():
        halo_down().wait_send()

    @pl.when(has_above)
    def _():
        halo_up().wait_send()

    @pl.when(has_dn)
    def _():
        for a in range(rims):
            rim_copy(a).wait_send()


def sweep(resid_l, dir_l, diag_l, lower_l, upper_l, pivot_l, downc_l, dc):
    n = lax.axis_size("elev")
    nd = lax.axis_size("down")
    chunks, rows, width = resid_l.shape
    blocks = lower_l.shape[0]
    per_block = chunks // blocks
    vmem = pl.BlockSpec(memory_space=pltpu.VMEM)
    flops = 2 * (2 * chunks * rows + 4 * dir_l.shape[0] * dir_l.shape[1]) * width * width
    weight_bytes = 6 * lower_l.size * lower_l.dtype.itemsize
    return pl.pallas_call(
        functools.partial(sweep_kernel, n=n, nd=nd, dc=dc, per_block=per_block),
        out_shape=(
            jax.ShapeDtypeStruct(resid_l.shape, resid_l.dtype),
            jax.ShapeDtypeStruct(dir_l.shape, jnp.float32),
        ),
        in_specs=[pl.BlockSpec(memory_space=pl.ANY)] * 7,
        out_specs=(vmem, vmem),
        scratch_shapes=[
            pltpu.VMEM(resid_l.shape, resid_l.dtype),
            pltpu.VMEM(resid_l.shape, resid_l.dtype),
            pltpu.VMEM(resid_l.shape, resid_l.dtype),
            pltpu.VMEM(dir_l.shape, dir_l.dtype),
            pltpu.VMEM(dir_l.shape, dir_l.dtype),
            pltpu.VMEM((blocks // dc,) + dir_l.shape[1:], dir_l.dtype),
            pltpu.SemaphoreType.DMA((chunks,)),
            pltpu.SemaphoreType.DMA((chunks,)),
            pltpu.SemaphoreType.DMA((chunks,)),
            pltpu.SemaphoreType.DMA((chunks,)),
            pltpu.SemaphoreType.DMA((2,)),
            pltpu.SemaphoreType.DMA((2,)),
            pltpu.SemaphoreType.DMA((blocks // dc,)),
            pltpu.SemaphoreType.DMA((blocks // dc,)),
            pltpu.VMEM(resid_l.shape, resid_l.dtype),
            pltpu.VMEM(dir_l.shape, dir_l.dtype),
            pltpu.VMEM(diag_l.shape, diag_l.dtype),
            pltpu.VMEM(lower_l.shape, lower_l.dtype),
            pltpu.VMEM(upper_l.shape, upper_l.dtype),
            pltpu.VMEM(pivot_l.shape, pivot_l.dtype),
            pltpu.VMEM(downc_l.shape, downc_l.dtype),
            pltpu.SemaphoreType.DMA((7,)),
        ],
        compiler_params=pltpu.CompilerParams(collective_id=0, has_side_effects=True),
        cost_estimate=pl.CostEstimate(
            flops=flops, bytes_accessed=weight_bytes + 6 * resid_l.size * 2, transcendentals=0
        ),
    )(resid_l, dir_l, diag_l, lower_l, upper_l, pivot_l, downc_l)


def partner_kernel(
    col_ref, piece_ref, valc_ref, partial_ref, solved_ref, out_ref, solved_out,
    held, vbuf, pbuf, sbuf, sems, *, dc
):
    blocks = held.shape[0]
    solved_in = pltpu.make_async_copy(solved_ref, sbuf, sems.at[0])
    solved_in.start()
    copies = []
    for b in range(blocks):
        col = col_ref[0, b // dc, b % dc]
        trio = (
            pltpu.make_async_copy(piece_ref.at[col * dc + b % dc], held.at[b], sems.at[1 + 3 * b]),
            pltpu.make_async_copy(valc_ref.at[b], vbuf.at[b], sems.at[2 + 3 * b]),
            pltpu.make_async_copy(partial_ref.at[b], pbuf.at[b], sems.at[3 + 3 * b]),
        )
        for copy in trio:
            copy.start()
        copies.append(trio)
    solved_in.wait()
    solved_back = pltpu.make_async_copy(sbuf, solved_out, sems.at[1 + 3 * blocks])
    solved_back.start()
    for b in range(blocks):
        for copy in copies[b]:
            copy.wait()
        out_ref[b] = pbuf[b] + jnp.dot(held[b], vbuf[b], preferred_element_type=jnp.float32)
    solved_back.wait()


def add_partner(cols, piece, valc, partial, solved, dc):
    blocks, rows, width = partial.shape
    hbm = pl.BlockSpec(memory_space=pl.ANY)
    return pl.pallas_call(
        functools.partial(partner_kernel, dc=dc),
        out_shape=(
            jax.ShapeDtypeStruct(partial.shape, partial.dtype),
            jax.ShapeDtypeStruct(solved.shape, solved.dtype),
        ),
        in_specs=[pl.BlockSpec(memory_space=pltpu.SMEM), hbm, hbm, hbm, hbm],
        out_specs=(pl.BlockSpec(memory_space=pltpu.VMEM), hbm),
        scratch_shapes=[
            pltpu.VMEM((blocks, rows, width), piece.dtype),
            pltpu.VMEM(valc.shape, valc.dtype),
            pltpu.VMEM(partial.shape, partial.dtype),
            pltpu.VMEM(solved.shape, solved.dtype),
            pltpu.SemaphoreType.DMA((2 + 3 * blocks,)),
        ],
        cost_estimate=pl.CostEstimate(
            flops=2 * blocks * rows * width * width,
            bytes_accessed=blocks * (rows * width * 10 + width * width * 2) + 4 * solved.size,
            transcendentals=0,
        ),
    )(cols, piece, valc, partial, solved)


def local(
    resid,
    direction,
    diag_blocks,
    lower_blocks,
    upper_blocks,
    inv_pivots,
    down_coupling,
    valley_coupling,
    coupled_column,
):
    va, dc, nr, bs = resid.shape[1:]
    blocks = va * dc
    chunk_shape = (blocks * ROW_SPLIT, nr // ROW_SPLIT, bs)
    flat = (blocks, bs, bs)
    solved, partial = sweep(
        resid[0].reshape(chunk_shape),
        direction[0].reshape(blocks, nr, bs),
        diag_blocks[0].reshape(flat),
        lower_blocks[0].reshape(flat),
        upper_blocks[0].reshape(flat),
        inv_pivots[0].reshape(flat),
        down_coupling[0].reshape(flat),
        dc,
    )

    current = direction[0]
    piece = lax.all_gather(current, "valley", axis=0, tiled=True)
    image, solved = add_partner(
        coupled_column,
        piece.reshape((-1, nr, bs)),
        valley_coupling[0].reshape(flat),
        partial,
        solved,
        dc,
    )
    return (solved.reshape(resid.shape), image.reshape(resid.shape))


def solution(mesh):
    spec = P("elev", "valley", "down", None, None)
    in_specs = (spec,) * 8 + (P("elev", "valley", "down"),)
    out_specs = (spec, spec)
    return jax.shard_map(local, mesh=mesh, in_specs=in_specs, out_specs=out_specs, check_vma=False)
```
